128 devices in a mesh: mode: 8 (over z, core), rad: 16 (over x, y).
Axes of the slice: x: 4, y: 4, z: 4, core: 2. Of those that a mesh axis runs over, the one named last changes fastest.
Arguments:
- field_coef: float32 [32, 2048, 384], P('mode', 'rad'), may hold values from -6 to 6
- prior_forcing: float32 [32, 2048, 384], P('mode', 'rad'), may hold values from -4 to 4
- base_flow: float32 [384, 1024], P('rad'), may hold values from 0.2 to 2
- keep_modes: int32 [32], P('mode'), may hold values from 256 to 341, as said below
- owner_band: int32 [262144, 1], P(('mode', 'rad')), may hold values from 0 to 15; in each aligned block of 2048 rows (0 to 2047, 2048 to 4095, ...) at most 256 rows name the same one
- cell_index: int32 [262144], P(('mode', 'rad')), may hold values from 0 to 3071
- axial_pos: float32 [262144], P(('mode', 'rad')), may hold values from 0 to 40
- particle_vel: float32 [262144], P(('mode', 'rad')), may hold values from -6 to 6
- response_rate: float32 [262144], P(('mode', 'rad')), may hold values from 0.5 to 4
- particle_mass: float32 [262144], P(('mode', 'rad')), may hold values from 0.5 to 5
Outputs:
- field_next: float32 [32, 2048, 384], P('mode', 'rad')
- forcing: float32 [32, 2048, 384], P('mode', 'rad')
The draws below stay inside these ranges and needn't reach their ends.
Inputs may be any that keep to these rules, and one draw needn't show every extreme that they name: Each axial mode k keeps azimuthal wavenumbers up to keep_modes[k]; the largest and the smallest allowed values both occur. `owner_band`: in the rows of one device no band is named by more than 256 particles, a bound that some block reaches. A particle's cell lies at radial offset cell_index // 128 in its owner band and angular offset cell_index % 128 in the angle block of its device's mode index.
All inputs are finite; a program needn't handle non-finite values.
Results may differ from the reference program's by a relative error of at most 0.0003.
Values sent between devices are 32-bit elements; how exact they have to be, the bound alone decides.
A program may use at most 64 MiB of HBM per device.

```python
import math
import jax
import jax.numpy as jnp
import numpy as np
from jax import lax

RADII = 384
AZIM = 1024
P_DEV = 2048
KZ = 32
COEF = 2048
BAND = 24
ARC = 128
CAP = 256
PARTICLES = 262144
N_RAD = 16


def draw_keep_modes(key, part):
    first, second, third = jax.random.split(jax.random.fold_in(key, 17), 3)
    values = jax.random.randint(first, (KZ,), AZIM // 4, AZIM // 3 + 1)
    highest = jax.random.randint(second, (), 0, KZ)
    lowest = (highest + 1 + jax.random.randint(third, (), 0, KZ - 1)) % KZ
    values = values.at[highest].set(AZIM // 3).at[lowest].set(AZIM // 4)
    return values.astype(jnp.int32)


def touch_ends(drawn, key, least, largest):
    index_at = [jax.random.randint(jax.random.fold_in(key, axis), (), 0, length) for axis, length in enumerate(drawn.shape)]
    main_axis = drawn.shape.index(max(drawn.shape))
    beside = index_at[:main_axis] + [(index_at[main_axis] + 1) % drawn.shape[main_axis]] + index_at[main_axis + 1:]
    return drawn.at[tuple(index_at)].set(least).at[tuple(beside)].set(largest)


def steps_of(stream_key, shape, cuts, least, high):
    def one(dim, shards_of):
        draws = jax.random.uniform(jax.random.fold_in(jax.random.fold_in(stream_key, 6), dim), (shards_of,), jnp.float32, least / len(cuts), high / len(cuts))
        return jnp.repeat(jnp.exp(draws), shape[dim] // shards_of).reshape((-1,) + (1,) * (len(shape) - dim - 1))

    level = one(*cuts[0])
    for cut in cuts[1:]:
        level = level * one(*cut)
    return level


def assign_block(stream_key, own, number, rows, amount, top, bound, slope):
    sequence = jax.random.permutation(stream_key, amount)
    packed, usual = shares(amount, rows * top, bound, slope, True), shares(amount, rows * top, bound, slope, False)
    places = jnp.arange(amount)

    def named(lengths, rotation):
        used = int((lengths > 0).sum())
        fixed = max(1, used // 4)
        moved = fixed + (places - fixed + rotation * (used - fixed)) % max(1, amount - fixed)
        return jnp.zeros((amount,), jnp.int32).at[sequence[jnp.where(places < fixed, places, moved)]].set(jnp.asarray(lengths, jnp.int32))

    lengths = jnp.where(number % 4 == 0, named(packed, number // 4), named(usual, number - number // 4 - 1))
    mixed = jax.random.permutation(jax.random.fold_in(own, 3), amount)
    source_of, taker = mixed[0:amount // 2 * 2:2], mixed[1:amount // 2 * 2:2]
    slack = jnp.minimum(lengths[source_of] - 1, bound - lengths[taker]) // 2
    slack = jnp.where((source_of == sequence[0]) | (taker == sequence[0]) | (lengths[taker] == 0), 0, jnp.maximum(slack, 0))
    moved = jax.random.randint(jax.random.fold_in(own, 4), (amount // 2,), 0, 1 << 20) % (slack + 1)
    lengths = lengths.at[source_of].add(-moved).at[taker].add(moved)
    labels = jnp.searchsorted(jnp.cumsum(lengths), jnp.arange(rows * top), side="right").astype(jnp.int32)
    listing = labels.reshape(top, rows).T
    listing = listing[jax.random.permutation(jax.random.fold_in(own, 1), rows)]
    rotation = jax.random.randint(jax.random.fold_in(own, 2), (rows, 1), 0, top)
    return jnp.take_along_axis(listing, (jnp.arange(top)[None, :] + rotation) % top, axis=1)


def shares(count, total, most, slope, full):
    weights = [(1 << 20) // math.isqrt(standing ** slope) + 1 for standing in range(1, count + 1)]
    largest = most if full else min(most, max(-(-total // count), total * weights[0] // sum(weights)))
    least = 1 if total - largest >= count - 1 else 0
    given, spare = [largest] + [least] * (count - 1), total - largest - least * (count - 1)
    while spare > 0:
        candidates = [i for i in range(1, count) if given[i] < largest] or [i for i in range(1, count) if given[i] < most]
        mass, remaining = sum([weights[i] for i in candidates]), spare
        for i in candidates:
            more = min(most - given[i], max(1, remaining * weights[i] // mass), spare)
            given[i] = given[i] + more
            spare = spare - more
    return np.array(given)


def bell_draw(rng, shape, spread, limit, shards=(), kind=jnp.bfloat16):
    drawn = spread * jax.random.normal(rng, shape, jnp.float32)
    if shards:
        drawn = drawn * steps_of(rng, shape, shards, -0.22, 0.18)
    return jnp.clip(drawn, -limit, limit).astype(kind)


def setup_inputs(seed: int = 0) -> dict:
    arg_keys = jax.random.split(jax.random.key(seed), 11)
    field_coef = bell_draw(arg_keys[0], (KZ, COEF, RADII), 1.0, 6.0, ((0, 8), (1, 16)), jnp.float32)
    prior_forcing = bell_draw(arg_keys[1], (KZ, COEF, RADII), 0.5, 4.0, ((0, 8), (1, 16)), jnp.float32)
    base_flow = jnp.clip(0.2 + 1.8 * jax.random.uniform(arg_keys[2], (RADII, AZIM), jnp.float32) ** steps_of(arg_keys[2], (RADII, AZIM), ((0, 16),), -0.2, 0.2), 0.2, 2.0)
    keep_modes = draw_keep_modes(jax.random.fold_in(arg_keys[10], 71), 0)
    owner_band_keys = jax.random.split(jax.random.fold_in(arg_keys[4], 1), PARTICLES // P_DEV)
    owner_band_turns = jax.random.permutation(jax.random.fold_in(arg_keys[4], 3), PARTICLES // P_DEV)
    owner_band = jax.vmap(lambda own, number: assign_block(jax.random.fold_in(arg_keys[4], 2), own, number, P_DEV, N_RAD, 1, CAP, 2))(owner_band_keys, owner_band_turns).reshape((PARTICLES, 1))
    cell_index = touch_ends(jax.random.randint(arg_keys[5], (PARTICLES,), 0, BAND * ARC), jax.random.fold_in(arg_keys[5], 1), 0, (BAND * ARC) - 1).astype(jnp.int32)
    axial_pos = jnp.clip(40.0 * jax.random.uniform(arg_keys[6], (PARTICLES,), jnp.float32) ** steps_of(arg_keys[6], (PARTICLES,), ((0, 128),), -0.2, 0.2), 0.0, 40.0)
    particle_vel = bell_draw(arg_keys[7], (PARTICLES,), 1.0, 6.0, ((0, 128),), jnp.float32)
    response_rate = jnp.clip(jnp.exp(math.log(4.0) - 2.0794415 * jax.random.uniform(arg_keys[8], (PARTICLES,), jnp.float32) ** steps_of(arg_keys[8], (PARTICLES,), ((0, 128),), -0.2, 0.2)), 0.5, 4.0)
    particle_mass = jnp.clip(jnp.exp(math.log(5.0) - 2.3025851 * jax.random.uniform(arg_keys[9], (PARTICLES,), jnp.float32) ** steps_of(arg_keys[9], (PARTICLES,), ((0, 128),), -0.2, 0.2)), 0.5, 5.0)
    return dict(field_coef=field_coef, prior_forcing=prior_forcing, base_flow=base_flow, keep_modes=keep_modes, owner_band=owner_band, cell_index=cell_index, axial_pos=axial_pos, particle_vel=particle_vel, response_rate=response_rate, particle_mass=particle_mass)


time_step = 0.5
viscosity = 0.0004
alpha_rk = 1.0 / 15.0
beta_rk = 1.0 / 15.0
gamma_rk = 5.0 / 12.0
zeta_rk = -17.0 / 60.0

def wavenumbers(indices, points):
    inner = indices % points
    return jnp.where(inner <= points // 2, inner, inner - points // 2)

def azimuth_table(points):
    indices = jnp.arange(points, dtype=jnp.int32)
    nyquist = points // 2
    wavenum = wavenumbers(indices, points)
    turn_count = indices[:, None] * wavenum[None, :] % points
    angles = turn_count.astype(jnp.float32) * (2.0 * math.pi / points)
    is_sine = indices[None, :] > nyquist
    scales = jnp.where((wavenum == 0) | (indices == nyquist), math.sqrt(1.0 / points), math.sqrt(2.0 / points))
    return jnp.where(is_sine, jnp.sin(angles), jnp.cos(angles)) * scales[None, :]

def axial_weights(position, kappas, total):
    phases = position[:, None] * kappas[None, :]
    scaling = 1.0 / math.sqrt(total)
    return jnp.stack([jnp.cos(phases), -jnp.sin(phases)], axis=2) * scaling

def advection(field, base, kappas):
    advect_speed = base[:, None, :] * kappas[None, :, None]
    return jnp.stack([advect_speed * field[:, :, 1, :], -advect_speed * field[:, :, 0, :]], axis=2)

def helmholtz_step(field, forcing, prior, kappas, wavenum):
    radial_count = field.shape[2]
    offsets = jnp.arange(radial_count, dtype=jnp.float32)
    at_wall = jnp.arange(radial_count) == radial_count - 1
    inverse = radial_count * radial_count / (offsets + 0.5)
    lower_band = offsets * inverse
    upper_band = jnp.where(at_wall, 0.0, (offsets + 1.0) * inverse)
    centre = -(offsets + (offsets + 1.0) * jnp.where(at_wall, 2.0, 1.0)) * inverse
    radius_sq = ((offsets + 0.5) / radial_count) ** 2
    wave_sq = wavenum.astype(jnp.float32) ** 2
    diagonal = centre[None, None, :] - wave_sq[None, :, None] / radius_sq[None, None, :] - (kappas ** 2)[:, None, None]
    below_row = jnp.pad(field[:, :, :-1], ((0, 0), (0, 0), (1, 0)))
    above_row = jnp.pad(field[:, :, 1:], ((0, 0), (0, 0), (0, 1)))
    laplace = lower_band * below_row + diagonal * field + upper_band * above_row
    right_side = field + time_step * (alpha_rk * viscosity * laplace + gamma_rk * forcing + zeta_rk * prior)
    implicit = beta_rk * time_step * viscosity
    full_shape = field.shape
    sub_diag = jnp.broadcast_to(-implicit * lower_band, full_shape)
    main_diag = 1.0 - implicit * diagonal
    super_diag = jnp.broadcast_to(-implicit * upper_band, full_shape)
    solved = lax.linalg.tridiagonal_solve(sub_diag, main_diag, super_diag, right_side[..., None])
    return solved[..., 0]

def reference(field_coef, prior_forcing, base_flow, keep_modes, owner_band, cell_index, axial_pos, particle_vel, response_rate, particle_mass):
    fourier = azimuth_table(AZIM)
    spectral = field_coef.reshape(KZ, 2, AZIM, RADII)
    physical = jnp.einsum('kcmr,tm->rkct', spectral, fourier, precision=lax.Precision.HIGHEST)
    kappa_all = 0.5 + 1.5 * jnp.arange(KZ, dtype=jnp.float32) / KZ
    device = jnp.arange(PARTICLES, dtype=jnp.int32) // P_DEV
    mode_block = device // N_RAD
    radial = owner_band[:, 0] * BAND + cell_index // ARC
    angular = mode_block * ARC + cell_index % ARC
    weights = axial_weights(axial_pos, kappa_all, KZ)
    sampled = physical[radial, :, :, angular]
    fluid_vel = lax.optimization_barrier(jnp.sum(sampled * weights, axis=(1, 2)))
    relative = (fluid_vel - particle_vel) * response_rate
    pushes = -particle_mass * relative
    deposit = jnp.zeros_like(physical).at[radial, :, :, angular].add(pushes[:, None, None] * weights)
    nonlinear = advection(physical, base_flow, kappa_all) + deposit
    raw_coef = jnp.einsum('rkct,tm->kcmr', nonlinear, fourier, precision=lax.Precision.HIGHEST)
    raw_coef = raw_coef.reshape(KZ, COEF, RADII)
    wavenum = wavenumbers(jnp.arange(COEF, dtype=jnp.int32), AZIM)
    retained = wavenum[None, :] <= keep_modes[:, None]
    forcing = jnp.where(retained[:, :, None], raw_coef, 0.0)
    field_next = helmholtz_step(field_coef, forcing, prior_forcing, kappa_all, wavenum)
    return (field_next, forcing)
```

```python
import math

import jax
import jax.numpy as jnp
import ml_dtypes
import numpy as np
from jax import lax
from jax.experimental import pallas as pl
from jax.experimental.pallas import tpu as pltpu
from jax.sharding import PartitionSpec as P

time_step = 0.5
viscosity = 0.0004
alpha_rk = 1.0 / 15.0
beta_rk = 1.0 / 15.0
gamma_rk = 5.0 / 12.0
zeta_rk = -17.0 / 60.0

RADII = 384
AZIM = 1024
HALF = 512
KZ = 32
P_DEV = 2048
BAND = 24
ARC = 128
CAP = 256
MODES = 8
RADS = 16
KL = 4
ROWS = BAND * KL
F32 = jnp.float32
BF16 = jnp.bfloat16
MESH = pl.DeviceIdType.MESH
implicit = beta_rk * time_step * viscosity
VMEM = pltpu.VMEM


def fourier_half():
    i = np.arange(AZIM)
    m = np.where(i <= HALF, i, i - HALF)
    t = np.arange(HALF)
    angle = 2.0 * math.pi * ((t[None, :] * m[:, None]) % AZIM) / AZIM
    scale = np.where((m == 0) | (i == HALF), math.sqrt(1.0 / AZIM), math.sqrt(2.0 / AZIM))
    table = (np.where((i > HALF)[:, None], np.sin(angle), np.cos(angle)) * scale[:, None]).astype(
        np.float32
    )
    high = table.astype(ml_dtypes.bfloat16)
    low = (table - high.astype(np.float32)).astype(ml_dtypes.bfloat16)
    return high, low


def split(x):
    high = x.astype(BF16)
    return high, (x - high.astype(F32)).astype(BF16)


def mm(a, b):
    return lax.dot_general(a, b, (((1,), (0,)), ((), ())), preferred_element_type=F32)


def mm_nt(a, b):
    return lax.dot_general(a, b, (((1,), (1,)), ((), ())), preferred_element_type=F32)


def iota(shape, dim):
    return lax.broadcasted_iota(jnp.int32, shape, dim)


def greet(mode_peers, rad_peers):
    barrier = pltpu.get_barrier_semaphore()
    mode, rad = lax.axis_index("mode"), lax.axis_index("rad")
    if rad_peers:
        for d in range(1, RADS):
            pl.semaphore_signal(
                barrier, inc=1, device_id=(mode, lax.rem(rad + d, RADS)), device_id_type=MESH
            )
    if mode_peers:
        for d in range(1, MODES):
            pl.semaphore_signal(
                barrier, inc=1, device_id=(lax.rem(mode + d, MODES), rad), device_id_type=MESH
            )
    return barrier, (RADS - 1) * rad_peers + (MODES - 1) * mode_peers


def push_copy(src, dst, send, recv, mode, rad):
    return pltpu.make_async_remote_copy(
        src_ref=src,
        dst_ref=dst,
        send_sem=send,
        recv_sem=recv,
        device_id=(mode, rad),
        device_id_type=MESH,
    )


def radial_tiles(shape, dims):
    j = iota(shape, dims[0])
    sub = iota(shape, dims[1])
    return jnp.where(sub < 4, j, RADII - 1 - j), sub


def factor(mode, rad, diag_ref, edge_ref, g_ref):
    shape = (RADII // 2, 8, 128)
    r, sub = radial_tiles(shape, (0, 1))
    off = r.astype(F32)
    inverse = (RADII * RADII) / (off + 0.5)
    last = r == RADII - 1
    lower = off * inverse
    upper = jnp.where(last, 0.0, (off + 1.0) * inverse)
    centre = -(off + (off + 1.0) * jnp.where(last, 2.0, 1.0)) * inverse
    k = mode * KL + sub % KL
    kappa = 0.5 + 1.5 * k.astype(F32) / KZ
    coef = lax.rem(rad, 8) * 128 + iota(shape, 2)
    m = jnp.where(coef <= HALF, coef, coef - HALF).astype(F32)
    unit = (off + 0.5) / RADII
    diagonal = centre - m * m / (unit * unit) - kappa * kappa
    diag_ref[...] = 1.0 - implicit * diagonal
    top = sub < 4
    before = jnp.where(top, off - 1.0, off + 1.0)
    before_inverse = (RADII * RADII) / (before + 0.5)
    inward = jnp.where(top, (before + 1.0) * before_inverse, before * before_inverse)
    outward = jnp.where(top, lower, upper)
    edge_ref[...] = jnp.where(
        (r == 0) | last, 0.0, (implicit * implicit) * inward * outward
    )

    def step(j, g):
        g = 1.0 / (diag_ref[j] - edge_ref[j] * g)
        g_ref[j] = g
        return g

    lax.fori_loop(0, RADII // 2, step, jnp.zeros((8, 128), F32))


def dispatch(own, cell, pos, vel, rate, mass, fields_ref):
    owner = own[...]
    bands = iota((RADS, P_DEV), 0)
    match = (bands == owner).astype(F32)
    match_bf = match.astype(BF16)
    chunk = 256
    tri = (iota((chunk, chunk), 0) < iota((chunk, chunk), 1)).astype(F32).astype(BF16)
    running = jnp.zeros((RADS, 1), F32)
    places = []
    for n in range(P_DEV // chunk):
        part = match[:, n * chunk : (n + 1) * chunk]
        ahead = mm(match_bf[:, n * chunk : (n + 1) * chunk], tri) + running
        places.append(jnp.sum(ahead * part, axis=0, keepdims=True))
        running = running + jnp.sum(part, axis=1, keepdims=True)
    place = jnp.concatenate(places, axis=1).astype(jnp.int32)
    slots = (iota((CAP, P_DEV), 0) == place).astype(F32).astype(BF16)
    cells = cell[...]
    pieces = [(cells // ARC).astype(F32), (cells % ARC).astype(F32)]
    for ref in (pos, vel, rate, mass):
        left = ref[...]
        for _ in range(3):
            piece = left.astype(BF16).astype(F32)
            pieces.append(piece)
            left = left - piece
    rows = jnp.concatenate([jnp.where(match > 0.5, p, 0.0) for p in pieces], axis=0).astype(BF16)
    sorted_rows = mm_nt(rows, slots)

    def take(n):
        return sorted_rows[n * RADS : (n + 1) * RADS]

    fields_ref[:, 0, :] = take(0) * ARC + take(1)
    for f in range(4):
        fields_ref[:, 1 + f, :] = take(2 + 3 * f) + take(3 + 3 * f) + take(4 + 3 * f)
    for f in range(5, 8):
        fields_ref[:, f, :] = jnp.zeros((RADS, CAP), F32)


def k1_body(
    field, own, cell, pos, vel, rate, mass,
    pieces, gathered, arrived, g_ref,
    outgoing, fields, diag, edge,
    fsend, frecv, psend, precv, gsend, grecv,
):
    mode, rad = lax.axis_index("mode"), lax.axis_index("rad")
    barrier, count = greet(True, True)
    dispatch(own, cell, pos, vel, rate, mass, fields)
    pl.semaphore_wait(barrier, count)

    def peer(d):
        return lax.rem(rad + d, RADS)

    def particle_copy(d):
        return push_copy(
            fields.at[peer(d)], arrived.at[rad], psend.at[d], precv.at[d], mode, peer(d)
        )

    def field_copy(d):
        return push_copy(
            outgoing.at[pl.ds(pl.multiple_of(peer(d) * ROWS, 8), ROWS)],
            pieces.at[pl.ds(pl.multiple_of(rad * ROWS, 8), ROWS)],
            fsend.at[d], frecv.at[d], mode, peer(d),
        )

    def gather_copy(d):
        other = lax.rem(mode + d, MODES)
        return push_copy(
            gathered.at[mode], gathered.at[mode], gsend.at[d], grecv.at[d], other, rad
        )

    for d in range(1, RADS):
        particle_copy(d).start()
    for k in range(KL):
        outgoing[pl.ds(k, RADII, stride=KL), :] = jnp.transpose(field[k])
    for d in range(1, RADS):
        field_copy(d).start()
    arrived[rad] = fields[rad]
    own_rows = pl.ds(pl.multiple_of(rad * ROWS, 8), ROWS)
    pieces[own_rows, :] = outgoing[own_rows, :]
    for d in range(1, RADS):
        particle_copy(d).wait_recv()
    gathered[mode, 0:RADS, :] = arrived[:, 0, :]
    gathered[mode, RADS : 2 * RADS, :] = arrived[:, 1, :]
    for d in range(1, MODES):
        gather_copy(d).start()
    factor(mode, rad, diag, edge, g_ref)
    for d in range(1, RADS):
        particle_copy(d).wait_send()
        field_copy(d).wait()
    for d in range(1, MODES):
        gather_copy(d).wait()


def cell_parts(cells):
    r = jnp.floor(cells * (1.0 / ARC))
    half = jnp.where(r >= BAND // 2, 1.0, 0.0)
    rh = r - half * (BAND // 2)
    pair = jnp.floor(rh * 0.5)
    column = cells + (half - r) * ARC
    return column.astype(jnp.int32), pair.astype(jnp.int32), (rh - 2.0 * pair).astype(jnp.int32)


def axial_rows(mode, positions, parity):
    sub = iota((8, 1), 0)
    k = mode * KL + sub % KL
    kappa = 0.5 + 1.5 * k.astype(F32) / KZ
    phases = kappa * positions
    chosen = (sub // KL) == parity
    scaling = 1.0 / math.sqrt(KZ)
    return (
        jnp.where(chosen, jnp.cos(phases) * scaling, 0.0),
        jnp.where(chosen, -jnp.sin(phases) * scaling, 0.0),
    )


PAIRS = BAND // 4


def k2_body(pieces, gathered, table_hi, table_lo, grid, partial):
    mode = lax.axis_index("mode")
    sign = jnp.where(iota((1, AZIM), 1) % 2 == 0, 1.0, -1.0)
    for c in range(2):
        x = jnp.concatenate(
            [pieces[(c * 8 + ib) * ROWS : (c * 8 + ib + 1) * ROWS, :] for ib in range(8)], axis=1
        )
        hi, lo = split(jnp.concatenate([x, x * sign], axis=0))
        for n in range(2):
            cols = slice(n * 256, (n + 1) * 256)
            th, tl = table_hi[:, cols], table_lo[:, cols]
            out = mm(hi, th) + mm(lo, th) + mm(hi, tl)
            for half in range(2):
                for a in range(2):
                    grid[half * 4 + n * 2 + a, c * ROWS : (c + 1) * ROWS, :] = out[
                        half * ROWS : (half + 1) * ROWS, a * 128 : (a + 1) * 128
                    ]

    def arc(m, carry):
        stack = []
        for c in range(2):
            lower = grid[m, c * ROWS : c * ROWS + 48, :]
            upper = grid[m, c * ROWS + 48 : (c + 1) * ROWS, :]
            stack.append(jnp.concatenate([lower, upper], axis=1))
        hi, lo = split(jnp.concatenate(stack, axis=0))
        lhs = jnp.concatenate([hi, lo], axis=0)
        for s in range(RADS):
            column, pair, parity = cell_parts(gathered[m, s : s + 1, :])
            onehot = (iota((256, CAP), 0) == column).astype(F32).astype(BF16)
            both = mm(lhs, onehot)
            values = both[:96] + both[96:]
            weights = axial_rows(mode, gathered[m, RADS + s : RADS + s + 1, :], parity)
            total = jnp.zeros((8, CAP), F32)
            for c in range(2):
                taken = jnp.zeros((8, CAP), F32)
                for q in range(PAIRS):
                    row = c * 48 + q * 8
                    taken = jnp.where(pair == q, values[row : row + 8], taken)
                total = total + taken * weights[c]
            partial[m, s : s + 1, :] = jnp.sum(total, axis=0, keepdims=True)
        return carry

    lax.fori_loop(0, MODES, arc, 0)


def k3_body(partial, arrived, pushes, parts, rsend, rrecv, gsend, grecv):
    mode, rad = lax.axis_index("mode"), lax.axis_index("rad")
    barrier, count = greet(True, False)
    pl.semaphore_wait(barrier, count)

    def reduce_copy(d):
        other = lax.rem(mode + d, MODES)
        return push_copy(
            partial.at[other], parts.at[mode], rsend.at[d], rrecv.at[d], other, rad
        )

    def gather_copy(d):
        other = lax.rem(mode + d, MODES)
        return push_copy(
            pushes.at[mode], pushes.at[mode], gsend.at[d], grecv.at[d], other, rad
        )

    for d in range(1, MODES):
        reduce_copy(d).start()
    parts[mode] = partial[mode]
    for d in range(1, MODES):
        reduce_copy(d).wait_recv()
    fluid = parts[0]
    for n in range(1, MODES):
        fluid = fluid + parts[n]
    relative = (fluid - arrived[:, 2, :]) * arrived[:, 3, :]
    pushes[mode] = -arrived[:, 4, :] * relative
    for d in range(1, MODES):
        gather_copy(d).start()
    for d in range(1, MODES):
        reduce_copy(d).wait_send()
        gather_copy(d).wait()


def k4_body(grid, gathered, pushes, base, table_hi, table_lo, spectral, terms, onehots, masses):
    mode = lax.axis_index("mode")

    def arc(m, carry):
        for s in range(RADS):
            lanes = slice(s * CAP, (s + 1) * CAP)
            column, pair, parity = cell_parts(gathered[m, s : s + 1, :])
            onehots[:, lanes] = (iota((256, CAP), 0) == column).astype(F32).astype(BF16)
            weights = axial_rows(mode, gathered[m, RADS + s : RADS + s + 1, :], parity)
            push = pushes[m, s : s + 1, :]
            rows = []
            lows = []
            for c in range(2):
                value = push * weights[c]
                high = value.astype(BF16).astype(F32)
                low = value - high
                for q in range(PAIRS):
                    rows.append(jnp.where(pair == q, high, 0.0))
                    lows.append(jnp.where(pair == q, low, 0.0))
            masses[:, lanes] = jnp.concatenate(rows + lows, axis=0).astype(BF16)
        both = mm_nt(masses[...], onehots[...])
        deposit = both[:96] + both[96:]
        for h in range(2):
            speed = base[m, h * 48 : (h + 1) * 48, :]
            cols = slice(h * 128, (h + 1) * 128)
            real = grid[m, h * 48 : (h + 1) * 48, :]
            imag = grid[m, ROWS + h * 48 : ROWS + (h + 1) * 48, :]
            terms[m, h * 48 : (h + 1) * 48, :] = speed * imag + deposit[:48, cols]
            terms[m, ROWS + h * 48 : ROWS + (h + 1) * 48, :] = deposit[48:, cols] - speed * real
        return carry

    lax.fori_loop(0, MODES, arc, 0)
    first = jnp.concatenate([terms[a] for a in range(4)], axis=1)
    second = jnp.concatenate([terms[a + 4] for a in range(4)], axis=1)
    hi, lo = split(jnp.concatenate([first + second, first - second], axis=0))
    even = iota((1, 128), 1) % 2 == 0
    for ib in (0, 1, 2, 4, 5, 6):
        th, tl = table_hi[ib * 128 : (ib + 1) * 128, :], table_lo[ib * 128 : (ib + 1) * 128, :]
        out = mm_nt(hi, th) + mm_nt(lo, th) + mm_nt(hi, tl)
        chosen = jnp.where(even, out[: 2 * ROWS], out[2 * ROWS :])
        spectral[ib * ROWS : (ib + 1) * ROWS, :] = chosen[:ROWS]
        spectral[(8 + ib) * ROWS : (9 + ib) * ROWS, :] = chosen[ROWS:]
    for ib in (3, 7, 11, 15):
        spectral[ib * ROWS : (ib + 1) * ROWS, :] = jnp.zeros((ROWS, 128), F32)


def k5_body(spectral, returned, send, recv):
    mode, rad = lax.axis_index("mode"), lax.axis_index("rad")
    barrier, count = greet(False, True)
    pl.semaphore_wait(barrier, count)
    takes = lax.rem(rad, 4) != 3

    def rows(n):
        return pl.ds(pl.multiple_of(n * ROWS, 8), ROWS)

    def copy(d):
        other = lax.rem(rad + d, RADS)
        return push_copy(
            spectral.at[rows(other)], returned.at[rows(rad)], send.at[d], recv.at[d], mode, other
        )

    for d in range(1, RADS):
        @pl.when(lax.rem(lax.rem(rad + d, RADS), 4) != 3)
        def _():
            copy(d).start()

    @pl.when(takes)
    def _():
        returned[rows(rad), :] = spectral[rows(rad), :]

    @pl.when(jnp.logical_not(takes))
    def _():
        returned[...] = jnp.zeros_like(returned)

    for d in range(1, RADS):
        @pl.when(lax.rem(lax.rem(rad + d, RADS), 4) != 3)
        def _():
            copy(d).wait_send()

        @pl.when(takes)
        def _():
            copy(d).wait_recv()


def band_rows(n):
    off = iota((1, RADII), 1).astype(F32)
    inverse = (RADII * RADII) / (off + 0.5)
    last = off == RADII - 1
    lower = off * inverse
    upper = jnp.where(last, 0.0, (off + 1.0) * inverse)
    centre = -(off + (off + 1.0) * jnp.where(last, 2.0, 1.0)) * inverse
    radius = (off + 0.5) / RADII
    return lower, upper, centre, radius * radius


def k6_body(returned, field, prior, keep, g_ref, nxt, forcing, rhs, work, coupling):
    mode, rad = lax.axis_index("mode"), lax.axis_index("rad")
    lower, upper, centre, radius_sq = band_rows(RADII)
    coef = lax.rem(rad, 8) * 128 + iota((128, 1), 0)
    m_col = jnp.where(coef <= HALF, coef, coef - HALF)
    wave_sq = m_col.astype(F32) * m_col.astype(F32)
    lane = lax.rem(rad, 8) * 128 + iota((1, 128), 1)
    m_row = jnp.where(lane <= HALF, lane, lane - HALF)
    for k in range(KL):
        kappa = 0.5 + 1.5 * (mode * KL + k).astype(F32) / KZ
        f = field[k]
        diagonal = centre - wave_sq / radius_sq - kappa * kappa
        laplace = lower * pltpu.roll(f, 1, 1) + diagonal * f + upper * pltpu.roll(f, RADII - 1, 1)
        known = f + time_step * (alpha_rk * viscosity * laplace + zeta_rk * prior[k])
        raw = returned[pl.ds(k, RADII, stride=KL), :]
        kept = jnp.where(m_row <= keep[k], raw, 0.0)
        forcing[k] = jnp.transpose(kept)
        rhs[pl.ds(k, RADII, stride=KL), :] = jnp.transpose(known) + (time_step * gamma_rk) * kept
    half = RADII // 2
    shape = (half, 8, 128)
    r, sub = radial_tiles(shape, (0, 1))
    off = r.astype(F32)
    scaled = implicit * (RADII * RADII) / (off + 0.5)
    inner = -scaled * jnp.where(sub < 4, off + 1.0, off)
    outer = -scaled * jnp.where(sub < 4, off, jnp.where(r == RADII - 1, 0.0, off + 1.0))
    g = g_ref[...]
    top_tile = iota((8, 128), 0) < 4

    def fold(q, carry):
        upper_rows = rhs[pl.ds(pl.multiple_of(q * 8, 8), 8), :]
        lower_rows = rhs[pl.ds(pl.multiple_of((half - 1 - q) * 8, 8), 8), :]
        work[2 * q] = jnp.where(top_tile, upper_rows, lower_rows)
        work[2 * q + 1] = pltpu.roll(jnp.where(top_tile, lower_rows, upper_rows), 4, 0)
        return carry

    lax.fori_loop(0, half // 2, fold, 0, unroll=4)
    work[...] = work[...] * g
    coupling[...] = outer * g

    def down(j, d):
        d = work[j] - coupling[j] * d
        work[j] = d
        return d

    d = lax.fori_loop(0, half, down, jnp.zeros((8, 128), F32), unroll=8)
    coupling[...] = inner * g
    v = coupling[half - 1]
    x = (d - v * pltpu.roll(d, 4, 0)) / (1.0 - v * pltpu.roll(v, 4, 0))
    work[half - 1] = x

    def back(n, x):
        j = half - 2 - n
        x = work[j] - coupling[j] * x
        work[j] = x
        return x

    lax.fori_loop(0, half - 1, back, x, unroll=8)

    def unfold(q, carry):
        even = work[2 * q]
        odd = pltpu.roll(work[2 * q + 1], 4, 0)
        rhs[pl.ds(pl.multiple_of(q * 8, 8), 8), :] = jnp.where(top_tile, even, odd)
        rhs[pl.ds(pl.multiple_of((half - 1 - q) * 8, 8), 8), :] = jnp.where(top_tile, odd, even)
        return carry

    lax.fori_loop(0, half // 2, unfold, 0, unroll=4)
    for k in range(KL):
        nxt[k] = jnp.transpose(rhs[pl.ds(k, RADII, stride=KL), :])


def vmem_call(body, outs, n_in, scratch, collective=None, smem=(), name=None):
    spec = [
        pl.BlockSpec(memory_space=pltpu.SMEM if n in smem else VMEM) for n in range(n_in)
    ]
    params = dict(vmem_limit_bytes=56 * 1024 * 1024)
    if collective is not None:
        params.update(collective_id=collective, has_side_effects=True)
    return pl.pallas_call(
        body,
        out_shape=[jax.ShapeDtypeStruct(s, F32) for s in outs],
        in_specs=spec,
        out_specs=[pl.BlockSpec(memory_space=VMEM)] * len(outs),
        scratch_shapes=scratch,
        compiler_params=pltpu.CompilerParams(**params),
        name=name,
    )


DMA = pltpu.SemaphoreType.DMA


def per_device(
    field_coef,
    prior_forcing,
    base_flow,
    keep_modes,
    owner_band,
    cell_index,
    axial_pos,
    particle_vel,
    response_rate,
    particle_mass,
):
    mode = lax.axis_index("mode")
    high, low = fourier_half()
    table_hi, table_lo = jnp.asarray(high), jnp.asarray(low)
    kappa = 0.5 + 1.5 * (mode * KL + jnp.arange(KL)).astype(F32) / KZ
    speed = base_flow[:, None, :] * kappa[None, :, None]
    speed = speed.reshape(ROWS, MODES, ARC).transpose(1, 0, 2)

    def row(x):
        return x.reshape(1, P_DEV)

    pieces, gathered, arrived, g = vmem_call(
        k1_body,
        [(RADS * ROWS, 128), (MODES, 2 * RADS, CAP), (RADS, 8, CAP), (RADII // 2, 8, 128)],
        7,
        [
            VMEM((RADS * ROWS, 128), F32),
            VMEM((RADS, 8, CAP), F32),
            VMEM((RADII // 2, 8, 128), F32),
            VMEM((RADII // 2, 8, 128), F32),
            DMA((RADS,)), DMA((RADS,)), DMA((RADS,)), DMA((RADS,)),
            DMA((MODES,)), DMA((MODES,)),
        ],
        collective=0,
        name="exchange",
    )(
        field_coef, row(owner_band), row(cell_index), row(axial_pos), row(particle_vel),
        row(response_rate), row(particle_mass),
    )
    grid, partial = vmem_call(
        k2_body,
        [(MODES, 2 * ROWS, 128), (MODES, RADS, CAP)],
        4,
        [],
        name="sample",
    )(pieces, gathered, table_hi, table_lo)
    (pushes,) = vmem_call(
        k3_body,
        [(MODES, RADS, CAP)],
        2,
        [VMEM((MODES, RADS, CAP), F32), DMA((MODES,)), DMA((MODES,)), DMA((MODES,)), DMA((MODES,))],
        collective=1,
        name="push",
    )(partial, arrived)
    (spectral,) = vmem_call(
        k4_body,
        [(RADS * ROWS, 128)],
        6,
        [
            VMEM((MODES, 2 * ROWS, 128), F32),
            VMEM((256, RADS * CAP), BF16),
            VMEM((192, RADS * CAP), BF16),
        ],
        name="deposit",
    )(grid, gathered, pushes, speed, table_hi, table_lo)
    (returned,) = vmem_call(
        k5_body,
        [(RADS * ROWS, 128)],
        1,
        [DMA((RADS,)), DMA((RADS,))],
        collective=2,
        name="give_back",
    )(spectral)
    field_next, forcing = vmem_call(
        k6_body,
        [(KL, 128, RADII), (KL, 128, RADII)],
        5,
        [
            VMEM((RADS * ROWS, 128), F32),
            VMEM((RADII // 2, 8, 128), F32),
            VMEM((RADII // 2, 8, 128), F32),
        ],
        smem=(3,),
        name="solve",
    )(returned, field_coef, prior_forcing, keep_modes, g)
    return (field_next, forcing)


def solution(mesh):
    in_specs = (
        P("mode", "rad", None),
        P("mode", "rad", None),
        P("rad", None),
        P("mode"),
        P(("mode", "rad"), None),
        P(("mode", "rad")),
        P(("mode", "rad")),
        P(("mode", "rad")),
        P(("mode", "rad")),
        P(("mode", "rad")),
    )
    out_specs = (P("mode", "rad", None), P("mode", "rad", None))
    return jax.shard_map(
        per_device, mesh=mesh, in_specs=in_specs, out_specs=out_specs, check_vma=False
    )
```

```python
import math

import jax
import jax.numpy as jnp
import ml_dtypes
import numpy as np
from jax import lax
from jax.experimental import pallas as pl
from jax.experimental.pallas import tpu as pltpu
from jax.sharding import PartitionSpec as P

time_step = 0.5
viscosity = 0.0004
alpha_rk = 1.0 / 15.0
beta_rk = 1.0 / 15.0
gamma_rk = 5.0 / 12.0
zeta_rk = -17.0 / 60.0

RADII = 384
AZIM = 1024
HALF = 512
KZ = 32
P_DEV = 2048
BAND = 24
ARC = 128
CAP = 256
MODES = 8
RADS = 16
KL = 4
ROWS = BAND * KL
F32 = jnp.float32
BF16 = jnp.bfloat16
MESH = pl.DeviceIdType.MESH
implicit = beta_rk * time_step * viscosity
VMEM = pltpu.VMEM


def fourier_half():
    i = np.arange(AZIM)
    m = np.where(i <= HALF, i, i - HALF)
    t = np.arange(HALF)
    angle = 2.0 * math.pi * ((t[None, :] * m[:, None]) % AZIM) / AZIM
    scale = np.where((m == 0) | (i == HALF), math.sqrt(1.0 / AZIM), math.sqrt(2.0 / AZIM))
    table = (np.where((i > HALF)[:, None], np.sin(angle), np.cos(angle)) * scale[:, None]).astype(
        np.float32
    )
    high = table.astype(ml_dtypes.bfloat16)
    low = (table - high.astype(np.float32)).astype(ml_dtypes.bfloat16)
    return high, low


def split(x):
    high = x.astype(BF16)
    return high, (x - high.astype(F32)).astype(BF16)


def mm(a, b):
    return lax.dot_general(a, b, (((1,), (0,)), ((), ())), preferred_element_type=F32)


def mm_nt(a, b):
    return lax.dot_general(a, b, (((1,), (1,)), ((), ())), preferred_element_type=F32)


def iota(shape, dim):
    return lax.broadcasted_iota(jnp.int32, shape, dim)


def greet(mode_peers, rad_peers):
    barrier = pltpu.get_barrier_semaphore()
    mode, rad = lax.axis_index("mode"), lax.axis_index("rad")
    if rad_peers:
        for d in range(1, RADS):
            pl.semaphore_signal(
                barrier, inc=1, device_id=(mode, lax.rem(rad + d, RADS)), device_id_type=MESH
            )
    if mode_peers:
        for d in range(1, MODES):
            pl.semaphore_signal(
                barrier, inc=1, device_id=(lax.rem(mode + d, MODES), rad), device_id_type=MESH
            )
    return barrier, (RADS - 1) * rad_peers + (MODES - 1) * mode_peers


def push_copy(src, dst, send, recv, mode, rad):
    return pltpu.make_async_remote_copy(
        src_ref=src,
        dst_ref=dst,
        send_sem=send,
        recv_sem=recv,
        device_id=(mode, rad),
        device_id_type=MESH,
    )


def radial_tiles(shape, dims):
    j = iota(shape, dims[0])
    sub = iota(shape, dims[1])
    return jnp.where(sub < 4, j, RADII - 1 - j), sub


def factor(mode, rad, diag_ref, edge_ref, g_ref):
    shape = (RADII // 2, 8, 128)
    r, sub = radial_tiles(shape, (0, 1))
    off = r.astype(F32)
    inverse = (RADII * RADII) / (off + 0.5)
    last = r == RADII - 1
    lower = off * inverse
    upper = jnp.where(last, 0.0, (off + 1.0) * inverse)
    centre = -(off + (off + 1.0) * jnp.where(last, 2.0, 1.0)) * inverse
    k = mode * KL + sub % KL
    kappa = 0.5 + 1.5 * k.astype(F32) / KZ
    coef = lax.rem(rad, 8) * 128 + iota(shape, 2)
    m = jnp.where(coef <= HALF, coef, coef - HALF).astype(F32)
    unit = (off + 0.5) / RADII
    diagonal = centre - m * m / (unit * unit) - kappa * kappa
    diag_ref[...] = 1.0 - implicit * diagonal
    top = sub < 4
    before = jnp.where(top, off - 1.0, off + 1.0)
    before_inverse = (RADII * RADII) / (before + 0.5)
    inward = jnp.where(top, (before + 1.0) * before_inverse, before * before_inverse)
    outward = jnp.where(top, lower, upper)
    edge_ref[...] = jnp.where(
        (r == 0) | last, 0.0, (implicit * implicit) * inward * outward
    )

    def step(j, g):
        g = 1.0 / (diag_ref[j] - edge_ref[j] * g)
        g_ref[j] = g
        return g

    lax.fori_loop(0, RADII // 2, step, jnp.zeros((8, 128), F32))


def dispatch(own, cell, pos, vel, rate, mass, fields_ref):
    owner = own[...]
    bands = iota((RADS, P_DEV), 0)
    match = (bands == owner).astype(F32)
    match_bf = match.astype(BF16)
    chunk = 256
    tri = (iota((chunk, chunk), 0) < iota((chunk, chunk), 1)).astype(F32).astype(BF16)
    running = jnp.zeros((RADS, 1), F32)
    places = []
    for n in range(P_DEV // chunk):
        part = match[:, n * chunk : (n + 1) * chunk]
        ahead = mm(match_bf[:, n * chunk : (n + 1) * chunk], tri) + running
        places.append(jnp.sum(ahead * part, axis=0, keepdims=True))
        running = running + jnp.sum(part, axis=1, keepdims=True)
    place = jnp.concatenate(places, axis=1).astype(jnp.int32)
    slots = (iota((CAP, P_DEV), 0) == place).astype(F32).astype(BF16)
    cells = cell[...]
    pieces = [(cells // ARC).astype(F32), (cells % ARC).astype(F32)]
    for ref in (pos, vel, rate, mass):
        left = ref[...]
        for _ in range(3):
            piece = left.astype(BF16).astype(F32)
            pieces.append(piece)
            left = left - piece
    rows = jnp.concatenate([jnp.where(match > 0.5, p, 0.0) for p in pieces], axis=0).astype(BF16)
    sorted_rows = mm_nt(rows, slots)

    def take(n):
        return sorted_rows[n * RADS : (n + 1) * RADS]

    fields_ref[:, 0, :] = take(0) * ARC + take(1)
    for f in range(4):
        fields_ref[:, 1 + f, :] = take(2 + 3 * f) + take(3 + 3 * f) + take(4 + 3 * f)
    for f in range(5, 8):
        fields_ref[:, f, :] = jnp.zeros((RADS, CAP), F32)


def cell_parts(cells):
    r = jnp.floor(cells * (1.0 / ARC))
    half = jnp.where(r >= BAND // 2, 1.0, 0.0)
    return cells + (half - r) * ARC, r - half * (BAND // 2)


QUARTER_HI = 1.57077026367187500
QUARTER_LO = math.pi / 2 - QUARTER_HI


def axial_tile(mode, positions):
    sub = iota((8, 1), 0)
    k = mode * KL + sub % KL
    kappa = 0.5 + 1.5 * k.astype(F32) / KZ
    phases = kappa * positions
    turns = jnp.floor(phases * (2.0 / math.pi) + 0.5)
    x = (phases - turns * QUARTER_HI) - turns * QUARTER_LO
    y = x * x
    sine = x + x * y * (-1.0 / 6 + y * (1.0 / 120 + y * (-1.0 / 5040 + y * (1.0 / 362880))))
    cosine = 1.0 + y * (-0.5 + y * (1.0 / 24 + y * (-1.0 / 720 + y * (1.0 / 40320))))
    quadrant = turns.astype(jnp.int32) + sub // KL
    scaling = 1.0 / math.sqrt(KZ)
    value = jnp.where((quadrant & 1) == 0, cosine, sine)
    return value * jnp.where(((quadrant + 1) & 2) == 0, scaling, -scaling)


HB = BAND // 2


def known_side(mode, rad, field, prior, known):
    lower, upper, centre, radius_sq = band_rows()
    coef = lax.rem(rad, 8) * 128 + iota((128, 1), 0)
    m_col = jnp.where(coef <= HALF, coef, coef - HALF).astype(F32)
    wave = m_col * m_col / radius_sq
    for k in range(KL):
        kappa = 0.5 + 1.5 * (mode * KL + k).astype(F32) / KZ
        f = field[k]
        diagonal = centre - wave - kappa * kappa
        laplace = lower * pltpu.roll(f, 1, 1) + diagonal * f + upper * pltpu.roll(f, RADII - 1, 1)
        side = f + time_step * (alpha_rk * viscosity * laplace + zeta_rk * prior[k])
        known[pl.ds(k, RADII, stride=KL), :] = jnp.transpose(side)


def forward(pieces, table_hi, table_lo, grid):
    sign = jnp.where(iota((1, AZIM), 1) % 2 == 0, 1.0, -1.0)
    xs = []
    for c in range(2):
        xs.append(jnp.concatenate(
            [pieces[(c * 8 + ib) * ROWS : (c * 8 + ib + 1) * ROWS, :] for ib in range(8)], axis=1
        ).reshape(HB, 8, AZIM))
    top = iota((1, 8, 1), 1) < KL
    even = jnp.where(top, xs[0], pltpu.roll(xs[1], 4, 1))
    odd = jnp.where(top, pltpu.roll(xs[0], 4, 1), xs[1])
    x = jnp.stack([even, odd], axis=1).reshape(2 * ROWS, AZIM)
    hi, lo = split(jnp.concatenate([x, x * sign], axis=0))
    for n in range(2):
        cols = slice(n * 256, (n + 1) * 256)
        th, tl = table_hi[:, cols], table_lo[:, cols]
        out = mm(hi, th) + mm(lo, th) + mm(hi, tl)
        for half in range(2):
            for a in range(2):
                grid[half * 4 + n * 2 + a] = out[
                    half * 2 * ROWS : (half + 1) * 2 * ROWS, a * 128 : (a + 1) * 128
                ]


def sample_arc(m, grid, gathered, onehots, weights, partial):
    hi, lo = split(jnp.concatenate([grid[m, :ROWS, :], grid[m, ROWS:, :]], axis=1))
    lhs = jnp.concatenate([hi, lo], axis=0)
    for s in range(RADS):
        _, rh = cell_parts(gathered[m, s : s + 1, :])
        both = mm(lhs, onehots[m, :, s * CAP : (s + 1) * CAP])
        values = both[:ROWS] + both[ROWS:]
        taken = jnp.zeros((8, CAP), F32)
        for q in range(HB):
            taken = jnp.where(rh == q, values[q * 8 : (q + 1) * 8], taken)
        partial[m, s : s + 1, :] = jnp.sum(taken * weights[m, s], axis=0, keepdims=True)


def deposit_arc(m, mode, grid, gathered, onehots, weights, pushes, flow, masses, terms):
    for s in range(RADS):
        _, rh = cell_parts(gathered[m, s : s + 1, :])
        value = pushes[m, s : s + 1, :] * weights[m, s]
        high = value.astype(BF16).astype(F32)
        low = value - high
        rows = [jnp.where(rh == q, high, 0.0) for q in range(HB)]
        rows += [jnp.where(rh == q, low, 0.0) for q in range(HB)]
        masses[:, s * CAP : (s + 1) * CAP] = jnp.concatenate(rows, axis=0).astype(BF16)
    both = mm_nt(masses[...], onehots[m])
    deposit = both[:ROWS] + both[ROWS:]
    sub = iota((8, 1), 0)
    kappa = 0.5 + 1.5 * (mode * KL + sub % KL).astype(F32) / KZ
    kappa = jnp.where(sub < KL, kappa, -kappa)
    for r in range(BAND):
        h, q = divmod(r, HB)
        rows = slice(r * 8, (r + 1) * 8)
        swapped = pltpu.roll(grid[m, rows, :], 4, 0)
        terms[m, rows, :] = (
            kappa * flow[m, r : r + 1, :] * swapped
            + deposit[q * 8 : (q + 1) * 8, h * 128 : (h + 1) * 128]
        )


def substep_body(
    field, prior, base, own, cell, pos, vel, rate, mass, table_hi, table_lo,
    returned, known, g_ref,
    outgoing, pieces, fields, arrived, gathered, diag, edge, flow, grid, terms, spectral,
    onehots, weights, masses, partial, parts, pushes,
    fsend, frecv, psend, precv, gsend, grecv, rsend, rrecv, asend, arecv, bsend, brecv,
):
    mode, rad = lax.axis_index("mode"), lax.axis_index("rad")
    barrier, count = greet(True, True)

    def rows(n):
        return pl.ds(pl.multiple_of(n * ROWS, 8), ROWS)

    def rad_peer(d):
        return lax.rem(rad + d, RADS)

    def mode_peer(d):
        return lax.rem(mode + d, MODES)

    def particle_copy(d):
        return push_copy(
            fields.at[rad_peer(d)], arrived.at[rad], psend.at[d], precv.at[d], mode, rad_peer(d)
        )

    def field_copy(d):
        return push_copy(
            outgoing.at[rows(rad_peer(d))], pieces.at[rows(rad)],
            fsend.at[d], frecv.at[d], mode, rad_peer(d),
        )

    def gather_copy(d):
        return push_copy(
            gathered.at[mode], gathered.at[mode], gsend.at[d], grecv.at[d], mode_peer(d), rad
        )

    def reduce_copy(d):
        return push_copy(
            partial.at[mode_peer(d)], parts.at[mode], rsend.at[d], rrecv.at[d], mode_peer(d), rad
        )

    def push_back(d):
        return push_copy(
            pushes.at[mode], pushes.at[mode], asend.at[d], arecv.at[d], mode_peer(d), rad
        )

    def back_copy(d):
        return push_copy(
            spectral.at[rows(rad_peer(d))], returned.at[rows(rad)],
            bsend.at[d], brecv.at[d], mode, rad_peer(d),
        )

    dispatch(own, cell, pos, vel, rate, mass, fields)
    pl.semaphore_wait(barrier, count)
    for d in range(1, RADS):
        particle_copy(d).start()
    for k in range(KL):
        outgoing[pl.ds(k, RADII, stride=KL), :] = jnp.transpose(field[k])
    for d in range(1, RADS):
        field_copy(d).start()
    arrived[rad] = fields[rad]
    pieces[rows(rad), :] = outgoing[rows(rad), :]
    for d in range(1, RADS):
        particle_copy(d).wait_recv()
    gathered[mode, 0:RADS, :] = arrived[:, 0, :]
    gathered[mode, RADS : 2 * RADS, :] = arrived[:, 1, :]
    for d in range(1, MODES):
        gather_copy(d).start()
    factor(mode, rad, diag, edge, g_ref)
    known_side(mode, rad, field, prior, known)
    for a in range(MODES):
        flow[a] = base[:, a * ARC : (a + 1) * ARC]
    for d in range(1, MODES):
        gather_copy(d).wait_recv()

    def prepare(m, carry):
        for s in range(RADS):
            column, _ = cell_parts(gathered[m, s : s + 1, :])
            index = iota((256, CAP), 0).astype(F32).astype(BF16)
            onehots[m, :, s * CAP : (s + 1) * CAP] = jnp.where(
                index == column.astype(BF16), jnp.ones((), BF16), jnp.zeros((), BF16)
            )
            weights[m, s] = axial_tile(mode, gathered[m, RADS + s : RADS + s + 1, :])
        return carry

    lax.fori_loop(0, MODES, prepare, 0)
    for d in range(1, RADS):
        field_copy(d).wait_recv()
    forward(pieces, table_hi, table_lo, grid)

    def sample(d, carry):
        sample_arc(mode_peer(d), grid, gathered, onehots, weights, partial)
        reduce_copy(d).start()
        return carry

    lax.fori_loop(1, MODES, sample, 0)
    sample_arc(mode, grid, gathered, onehots, weights, partial)
    parts[mode] = partial[mode]
    for d in range(1, MODES):
        reduce_copy(d).wait_recv()
    fluid = parts[0]
    for n in range(1, MODES):
        fluid = fluid + parts[n]
    relative = (fluid - arrived[:, 2, :]) * arrived[:, 3, :]
    pushes[mode] = -arrived[:, 4, :] * relative
    for d in range(1, MODES):
        push_back(d).start()

    def place(d, carry):
        @pl.when(d > 0)
        def _():
            push_back(MODES - d).wait_recv()

        deposit_arc(
            mode_peer(d), mode, grid, gathered, onehots, weights, pushes, flow, masses, terms
        )
        return carry

    lax.fori_loop(0, MODES, place, 0)
    first = jnp.concatenate([terms[a] for a in range(4)], axis=1)
    second = jnp.concatenate([terms[a + 4] for a in range(4)], axis=1)
    hi, lo = split(jnp.concatenate([first + second, first - second], axis=0))
    parity = iota((1, 128), 1) % 2 == 0
    top = iota((1, 8, 1), 1) < KL
    for ib in (0, 1, 2, 4, 5, 6):
        th, tl = table_hi[ib * 128 : (ib + 1) * 128, :], table_lo[ib * 128 : (ib + 1) * 128, :]
        out = mm_nt(hi, th) + mm_nt(lo, th) + mm_nt(hi, tl)
        chosen = jnp.where(parity, out[: 2 * ROWS], out[2 * ROWS :]).reshape(HB, 2, 8, 128)
        even, odd = chosen[:, 0], chosen[:, 1]
        real = jnp.where(top, even, pltpu.roll(odd, 4, 1))
        imag = jnp.where(top, pltpu.roll(even, 4, 1), odd)
        spectral[ib * ROWS : (ib + 1) * ROWS, :] = real.reshape(ROWS, 128)
        spectral[(8 + ib) * ROWS : (9 + ib) * ROWS, :] = imag.reshape(ROWS, 128)
    takes = lax.rem(rad, 4) != 3
    for d in range(1, RADS):
        @pl.when(lax.rem(rad_peer(d), 4) != 3)
        def _():
            back_copy(d).start()

    @pl.when(takes)
    def _():
        returned[rows(rad), :] = spectral[rows(rad), :]

    @pl.when(jnp.logical_not(takes))
    def _():
        returned[...] = jnp.zeros_like(returned)

    for d in range(1, RADS):
        particle_copy(d).wait_send()
        field_copy(d).wait_send()
    for d in range(1, MODES):
        gather_copy(d).wait_send()
        reduce_copy(d).wait_send()
        push_back(d).wait_send()
    for d in range(1, RADS):
        @pl.when(lax.rem(rad_peer(d), 4) != 3)
        def _():
            back_copy(d).wait_send()

        @pl.when(takes)
        def _():
            back_copy(d).wait_recv()


def band_rows():
    off = iota((1, RADII), 1).astype(F32)
    inverse = (RADII * RADII) / (off + 0.5)
    last = off == RADII - 1
    lower = off * inverse
    upper = jnp.where(last, 0.0, (off + 1.0) * inverse)
    centre = -(off + (off + 1.0) * jnp.where(last, 2.0, 1.0)) * inverse
    radius = (off + 0.5) / RADII
    return lower, upper, centre, radius * radius


def solve_body(returned, known, keep, g_ref, nxt, forcing, rhs, work):
    rad = lax.axis_index("rad")
    half = RADII // 2
    lane = lax.rem(rad, 8) * 128 + iota((8, 128), 1)
    m = jnp.where(lane <= HALF, lane, lane - HALF)
    sub = iota((8, 128), 0)
    most = jnp.where(
        sub % KL == 0, keep[0], jnp.where(sub % KL == 1, keep[1], jnp.where(sub % KL == 2, keep[2], keep[3]))
    )
    kept_here = m <= most
    top = sub < KL
    gain = time_step * gamma_rk

    def rows(q):
        return pl.ds(pl.multiple_of(q * 8, 8), 8)

    def fold(q, carry):
        sides = []
        for n in (q, half - 1 - q):
            kept = jnp.where(kept_here, returned[rows(n), :], 0.0)
            rhs[rows(n), :] = kept
            sides.append(known[rows(n), :] + gain * kept)
        work[2 * q] = jnp.where(top, sides[0], sides[1]) * g_ref[2 * q]
        odd = pltpu.roll(jnp.where(top, sides[1], sides[0]), 4, 0)
        work[2 * q + 1] = odd * g_ref[2 * q + 1]
        return carry

    lax.fori_loop(0, half // 2, fold, 0, unroll=8)
    for k in range(KL):
        forcing[k] = jnp.transpose(rhs[pl.ds(k, RADII, stride=KL), :])

    scale = -implicit * RADII * RADII

    def couplings(j):
        r = jnp.where(top, j, RADII - 1 - j)
        off = r.astype(F32)
        inverse = scale / (off + 0.5)
        after = jnp.where(r == RADII - 1, 0.0, off + 1.0)
        return jnp.where(top, off, after) * inverse, jnp.where(top, after, off) * inverse

    def down(j, d):
        outer, _ = couplings(j)
        d = work[j] - (outer * g_ref[j]) * d
        work[j] = d
        return d

    d = lax.fori_loop(0, half, down, jnp.zeros((8, 128), F32), unroll=8)
    _, inner = couplings(half - 1)
    v = inner * g_ref[half - 1]
    x = (d - v * pltpu.roll(d, 4, 0)) / (1.0 - v * pltpu.roll(v, 4, 0))
    work[half - 1] = x

    def back(n, x):
        j = half - 2 - n
        _, inner = couplings(j)
        x = work[j] - (inner * g_ref[j]) * x
        work[j] = x
        return x

    lax.fori_loop(0, half - 1, back, x, unroll=8)

    def unfold(q, carry):
        even = work[2 * q]
        odd = pltpu.roll(work[2 * q + 1], 4, 0)
        rhs[rows(q), :] = jnp.where(top, even, odd)
        rhs[rows(half - 1 - q), :] = jnp.where(top, odd, even)
        return carry

    lax.fori_loop(0, half // 2, unfold, 0, unroll=8)
    for k in range(KL):
        nxt[k] = jnp.transpose(rhs[pl.ds(k, RADII, stride=KL), :])


def vmem_call(body, outs, n_in, scratch, collective=None, smem=(), name=None):
    spec = [
        pl.BlockSpec(memory_space=pltpu.SMEM if n in smem else VMEM) for n in range(n_in)
    ]
    params = dict(vmem_limit_bytes=56 * 1024 * 1024)
    if collective is not None:
        params.update(collective_id=collective, has_side_effects=True)
    return pl.pallas_call(
        body,
        out_shape=[jax.ShapeDtypeStruct(s, F32) for s in outs],
        in_specs=spec,
        out_specs=[pl.BlockSpec(memory_space=VMEM)] * len(outs),
        scratch_shapes=scratch,
        compiler_params=pltpu.CompilerParams(**params),
        name=name,
    )


DMA = pltpu.SemaphoreType.DMA


def per_device(
    field_coef,
    prior_forcing,
    base_flow,
    keep_modes,
    owner_band,
    cell_index,
    axial_pos,
    particle_vel,
    response_rate,
    particle_mass,
):
    high, low = fourier_half()
    table_hi, table_lo = jnp.asarray(high), jnp.asarray(low)

    def row(x):
        return x.reshape(1, P_DEV)

    all_rows = (RADS * ROWS, 128)
    tiles = (RADII // 2, 8, 128)
    slots = (MODES, RADS, CAP)
    returned, known, g = vmem_call(
        substep_body,
        [all_rows, all_rows, tiles],
        11,
        [
            VMEM(all_rows, F32),
            VMEM(all_rows, F32),
            VMEM((RADS, 8, CAP), F32),
            VMEM((RADS, 8, CAP), F32),
            VMEM((MODES, 2 * RADS, CAP), F32),
            VMEM(tiles, F32),
            VMEM(tiles, F32),
            VMEM((MODES, BAND, ARC), F32),
            VMEM((MODES, 2 * ROWS, 128), F32),
            VMEM((MODES, 2 * ROWS, 128), F32),
            VMEM(all_rows, F32),
            VMEM((MODES, 256, RADS * CAP), BF16),
            VMEM((MODES, RADS, 8, CAP), F32),
            VMEM((2 * ROWS, RADS * CAP), BF16),
            VMEM(slots, F32),
            VMEM(slots, F32),
            VMEM(slots, F32),
            DMA((RADS,)), DMA((RADS,)), DMA((RADS,)), DMA((RADS,)),
            DMA((MODES,)), DMA((MODES,)), DMA((MODES,)), DMA((MODES,)),
            DMA((MODES,)), DMA((MODES,)), DMA((RADS,)), DMA((RADS,)),
        ],
        collective=0,
        name="substep",
    )(
        field_coef, prior_forcing, base_flow, row(owner_band), row(cell_index), row(axial_pos),
        row(particle_vel), row(response_rate), row(particle_mass), table_hi, table_lo,
    )
    field_next, forcing = vmem_call(
        solve_body,
        [(KL, 128, RADII), (KL, 128, RADII)],
        4,
        [VMEM(all_rows, F32), VMEM(tiles, F32)],
        smem=(2,),
        name="solve",
    )(returned, known, keep_modes, g)
    return (field_next, forcing)


def solution(mesh):
    in_specs = (
        P("mode", "rad", None),
        P("mode", "rad", None),
        P("rad", None),
        P("mode"),
        P(("mode", "rad"), None),
        P(("mode", "rad")),
        P(("mode", "rad")),
        P(("mode", "rad")),
        P(("mode", "rad")),
        P(("mode", "rad")),
    )
    out_specs = (P("mode", "rad", None), P("mode", "rad", None))
    return jax.shard_map(
        per_device, mesh=mesh, in_specs=in_specs, out_specs=out_specs, check_vma=False
    )
```

```python
import math

import jax
import jax.numpy as jnp
import ml_dtypes
import numpy as np
from jax import lax
from jax.experimental import pallas as pl
from jax.experimental.pallas import tpu as pltpu
from jax.sharding import PartitionSpec as P

time_step = 0.5
viscosity = 0.0004
alpha_rk = 1.0 / 15.0
beta_rk = 1.0 / 15.0
gamma_rk = 5.0 / 12.0
zeta_rk = -17.0 / 60.0

RADII = 384
AZIM = 1024
HALF = 512
KZ = 32
P_DEV = 2048
BAND = 24
ARC = 128
CAP = 256
MODES = 8
RADS = 16
KL = 4
ROWS = BAND * KL
F32 = jnp.float32
BF16 = jnp.bfloat16
MESH = pl.DeviceIdType.MESH
implicit = beta_rk * time_step * viscosity
VMEM = pltpu.VMEM


def fourier_half():
    i = np.arange(AZIM)
    m = np.where(i <= HALF, i, i - HALF)
    t = np.arange(HALF)
    angle = 2.0 * math.pi * ((t[None, :] * m[:, None]) % AZIM) / AZIM
    scale = np.where((m == 0) | (i == HALF), math.sqrt(1.0 / AZIM), math.sqrt(2.0 / AZIM))
    table = (np.where((i > HALF)[:, None], np.sin(angle), np.cos(angle)) * scale[:, None]).astype(
        np.float32
    )
    high = table.astype(ml_dtypes.bfloat16)
    low = (table - high.astype(np.float32)).astype(ml_dtypes.bfloat16)
    return high, low


def split(x):
    high = x.astype(BF16)
    return high, (x - high.astype(F32)).astype(BF16)


def mm(a, b):
    return lax.dot_general(a, b, (((1,), (0,)), ((), ())), preferred_element_type=F32)


def mm_nt(a, b):
    return lax.dot_general(a, b, (((1,), (1,)), ((), ())), preferred_element_type=F32)


def iota(shape, dim):
    return lax.broadcasted_iota(jnp.int32, shape, dim)


def greet(mode_peers, rad_peers):
    barrier = pltpu.get_barrier_semaphore()
    mode, rad = lax.axis_index("mode"), lax.axis_index("rad")
    if rad_peers:
        for d in range(1, RADS):
            pl.semaphore_signal(
                barrier, inc=1, device_id=(mode, lax.rem(rad + d, RADS)), device_id_type=MESH
            )
    if mode_peers:
        for d in range(1, MODES):
            pl.semaphore_signal(
                barrier, inc=1, device_id=(lax.rem(mode + d, MODES), rad), device_id_type=MESH
            )
    return barrier, (RADS - 1) * rad_peers + (MODES - 1) * mode_peers


def push_copy(src, dst, send, recv, mode, rad):
    return pltpu.make_async_remote_copy(
        src_ref=src,
        dst_ref=dst,
        send_sem=send,
        recv_sem=recv,
        device_id=(mode, rad),
        device_id_type=MESH,
    )


def radial_tiles(shape, dims):
    j = iota(shape, dims[0])
    sub = iota(shape, dims[1])
    return jnp.where(sub < 4, j, RADII - 1 - j), sub


def factor(mode, rad, diag_ref, edge_ref, g_ref):
    shape = (RADII // 2, 8, 128)
    r, sub = radial_tiles(shape, (0, 1))
    off = r.astype(F32)
    inverse = (RADII * RADII) / (off + 0.5)
    last = r == RADII - 1
    lower = off * inverse
    upper = jnp.where(last, 0.0, (off + 1.0) * inverse)
    centre = -(off + (off + 1.0) * jnp.where(last, 2.0, 1.0)) * inverse
    k = mode * KL + sub % KL
    kappa = 0.5 + 1.5 * k.astype(F32) / KZ
    coef = lax.rem(rad, 8) * 128 + iota(shape, 2)
    m = jnp.where(coef <= HALF, coef, coef - HALF).astype(F32)
    unit = (off + 0.5) / RADII
    diagonal = centre - m * m / (unit * unit) - kappa * kappa
    diag_ref[...] = 1.0 - implicit * diagonal
    top = sub < 4
    before = jnp.where(top, off - 1.0, off + 1.0)
    before_inverse = (RADII * RADII) / (before + 0.5)
    inward = jnp.where(top, (before + 1.0) * before_inverse, before * before_inverse)
    outward = jnp.where(top, lower, upper)
    edge_ref[...] = jnp.where(
        (r == 0) | last, 0.0, (implicit * implicit) * inward * outward
    )

    def step(j, g):
        g = 1.0 / (diag_ref[j] - edge_ref[j] * g)
        g_ref[j] = g
        return g

    lax.fori_loop(0, RADII // 2, step, jnp.zeros((8, 128), F32))


def dispatch(own, cell, pos, vel, rate, mass, fields_ref):
    owner = own[...]
    bands = iota((RADS, P_DEV), 0)
    match = (bands == owner).astype(F32)
    match_bf = match.astype(BF16)
    chunk = 256
    tri = (iota((chunk, chunk), 0) < iota((chunk, chunk), 1)).astype(F32).astype(BF16)
    running = jnp.zeros((RADS, 1), F32)
    places = []
    for n in range(P_DEV // chunk):
        part = match[:, n * chunk : (n + 1) * chunk]
        ahead = mm(match_bf[:, n * chunk : (n + 1) * chunk], tri) + running
        places.append(jnp.sum(ahead * part, axis=0, keepdims=True))
        running = running + jnp.sum(part, axis=1, keepdims=True)
    place = jnp.concatenate(places, axis=1).astype(jnp.int32)
    slots = (iota((CAP, P_DEV), 0) == place).astype(F32).astype(BF16)
    cells = cell[...]
    pieces = [(cells // ARC).astype(F32), (cells % ARC).astype(F32)]
    for ref in (pos, vel, rate, mass):
        left = ref[...]
        for _ in range(3):
            piece = left.astype(BF16).astype(F32)
            pieces.append(piece)
            left = left - piece
    rows = jnp.concatenate([jnp.where(match > 0.5, p, 0.0) for p in pieces], axis=0).astype(BF16)
    sorted_rows = mm_nt(rows, slots)

    def take(n):
        return sorted_rows[n * RADS : (n + 1) * RADS]

    fields_ref[:, 0, :] = take(0) * ARC + take(1)
    for f in range(4):
        fields_ref[:, 1 + f, :] = take(2 + 3 * f) + take(3 + 3 * f) + take(4 + 3 * f)
    for f in range(5, 8):
        fields_ref[:, f, :] = jnp.zeros((RADS, CAP), F32)


def cell_parts(cells):
    r = jnp.floor(cells * (1.0 / ARC))
    half = jnp.where(r >= BAND // 2, 1.0, 0.0)
    return cells + (half - r) * ARC, r - half * (BAND // 2)


QUARTER_HI = 1.57077026367187500
QUARTER_LO = math.pi / 2 - QUARTER_HI


def axial_tile(mode, positions):
    sub = iota((8, 1), 0)
    k = mode * KL + sub % KL
    kappa = 0.5 + 1.5 * k.astype(F32) / KZ
    phases = kappa * positions
    turns = jnp.floor(phases * (2.0 / math.pi) + 0.5)
    x = (phases - turns * QUARTER_HI) - turns * QUARTER_LO
    y = x * x
    sine = x + x * y * (-1.0 / 6 + y * (1.0 / 120 + y * (-1.0 / 5040 + y * (1.0 / 362880))))
    cosine = 1.0 + y * (-0.5 + y * (1.0 / 24 + y * (-1.0 / 720 + y * (1.0 / 40320))))
    quadrant = turns.astype(jnp.int32) + sub // KL
    scaling = 1.0 / math.sqrt(KZ)
    value = jnp.where((quadrant & 1) == 0, cosine, sine)
    return value * jnp.where(((quadrant + 1) & 2) == 0, scaling, -scaling)


HB = BAND // 2
EARLY = 0


def known_side(mode, rad, field, prior, known):
    lower, upper, centre, radius_sq = band_rows()
    coef = lax.rem(rad, 8) * 128 + iota((128, 1), 0)
    m_col = jnp.where(coef <= HALF, coef, coef - HALF).astype(F32)
    wave = m_col * m_col / radius_sq
    for k in range(KL):
        kappa = 0.5 + 1.5 * (mode * KL + k).astype(F32) / KZ
        f = field[k]
        diagonal = centre - wave - kappa * kappa
        laplace = lower * pltpu.roll(f, 1, 1) + diagonal * f + upper * pltpu.roll(f, RADII - 1, 1)
        side = f + time_step * (alpha_rk * viscosity * laplace + zeta_rk * prior[k])
        known[pl.ds(k, RADII, stride=KL), :] = jnp.transpose(side)


def forward(pieces, table_hi, table_lo, grid):
    sign = jnp.where(iota((1, AZIM), 1) % 2 == 0, 1.0, -1.0)
    xs = []
    for c in range(2):
        xs.append(jnp.concatenate(
            [pieces[(c * 8 + ib) * ROWS : (c * 8 + ib + 1) * ROWS, :] for ib in range(8)], axis=1
        ).reshape(HB, 8, AZIM))
    top = iota((1, 8, 1), 1) < KL
    even = jnp.where(top, xs[0], pltpu.roll(xs[1], 4, 1))
    odd = jnp.where(top, pltpu.roll(xs[0], 4, 1), xs[1])
    x = jnp.stack([even, odd], axis=1).reshape(2 * ROWS, AZIM)
    hi, lo = split(jnp.concatenate([x, x * sign], axis=0))
    for n in range(2):
        cols = slice(n * 256, (n + 1) * 256)
        th, tl = table_hi[:, cols], table_lo[:, cols]
        out = mm(hi, th) + mm(lo, th) + mm(hi, tl)
        for half in range(2):
            for a in range(2):
                grid[half * 4 + n * 2 + a] = out[
                    half * 2 * ROWS : (half + 1) * 2 * ROWS, a * 128 : (a + 1) * 128
                ]


def sample_arc(m, grid, gathered, onehots, weights, partial):
    hi, lo = split(jnp.concatenate([grid[m, :ROWS, :], grid[m, ROWS:, :]], axis=1))
    lhs = jnp.concatenate([hi, lo], axis=0)
    for s in range(RADS):
        _, rh = cell_parts(gathered[m, s : s + 1, :])
        both = mm(lhs, onehots[m, :, s * CAP : (s + 1) * CAP])
        values = both[:ROWS] + both[ROWS:]
        taken = jnp.zeros((8, CAP), F32)
        for q in range(HB):
            taken = jnp.where(rh == q, values[q * 8 : (q + 1) * 8], taken)
        partial[m, s : s + 1, :] = jnp.sum(taken * weights[m, s], axis=0, keepdims=True)


def deposit_arc(m, gathered, onehots, weights, pushes, masses, terms):
    for s in range(RADS):
        _, rh = cell_parts(gathered[m, s : s + 1, :])
        value = pushes[m, s : s + 1, :] * weights[m, s]
        high = value.astype(BF16).astype(F32)
        low = value - high
        rows = [jnp.where(rh == q, high, 0.0) for q in range(HB)]
        rows += [jnp.where(rh == q, low, 0.0) for q in range(HB)]
        masses[:, s * CAP : (s + 1) * CAP] = jnp.concatenate(rows, axis=0).astype(BF16)
    both = mm_nt(masses[...], onehots[m])
    deposit = both[:ROWS] + both[ROWS:]
    for h in range(2):
        rows = slice(h * ROWS, (h + 1) * ROWS)
        terms[m, rows, :] = terms[m, rows, :] + deposit[:, h * 128 : (h + 1) * 128]


def advect_arc(m, mode, grid, flow, terms):
    sub = iota((8, 1), 0)
    kappa = 0.5 + 1.5 * (mode * KL + sub % KL).astype(F32) / KZ
    kappa = jnp.where(sub < KL, kappa, -kappa)
    for r in range(BAND):
        rows = slice(r * 8, (r + 1) * 8)
        swapped = pltpu.roll(grid[m, rows, :], 4, 0)
        terms[m, rows, :] = kappa * flow[m, r : r + 1, :] * swapped


def substep_body(
    field_in, prior_in, base_in, own_in, cell_in, pos_in, vel_in, rate_in, mass_in, hi_in, lo_in,
    returned, known_out, g_out,
    field, prior, base, own, cell, pos, vel, rate, mass, table_hi, table_lo, known, g_ref,
    outgoing, pieces, fields, arrived, gathered, diag, edge, flow, grid, terms, spectral,
    onehots, weights, masses, splits, partial, parts, pushes, loads, stores,
    fsend, frecv, psend, precv, gsend, grecv, rsend, rrecv, asend, arecv, bsend, brecv,
):
    mode, rad = lax.axis_index("mode"), lax.axis_index("rad")
    barrier, count = greet(True, True)
    given = [
        (own_in, own), (cell_in, cell), (pos_in, pos), (vel_in, vel), (rate_in, rate),
        (mass_in, mass), (field_in, field), (hi_in, table_hi), (lo_in, table_lo),
        (prior_in, prior), (base_in, base),
    ]
    given = [pltpu.make_async_copy(x, y, loads.at[n]) for n, (x, y) in enumerate(given)]
    for copy in given:
        copy.start()

    def rows(n):
        return pl.ds(pl.multiple_of(n * ROWS, 8), ROWS)

    def rad_peer(d):
        return lax.rem(rad + d, RADS)

    def mode_peer(d):
        return lax.rem(mode + d, MODES)

    def particle_copy(d):
        return push_copy(
            fields.at[rad_peer(d)], arrived.at[rad], psend.at[d], precv.at[d], mode, rad_peer(d)
        )

    def field_copy(d):
        return push_copy(
            outgoing.at[rows(rad_peer(d))], pieces.at[rows(rad)],
            fsend.at[d], frecv.at[d], mode, rad_peer(d),
        )

    def gather_copy(d):
        return push_copy(
            gathered.at[mode], gathered.at[mode], gsend.at[d], grecv.at[d], mode_peer(d), rad
        )

    def reduce_copy(d):
        return push_copy(
            partial.at[mode_peer(d)], parts.at[mode], rsend.at[d], rrecv.at[d], mode_peer(d), rad
        )

    def push_back(d):
        return push_copy(
            pushes.at[mode], pushes.at[mode], asend.at[d], arecv.at[d], mode_peer(d), rad
        )

    def back_copy(d):
        return push_copy(
            spectral.at[rows(rad_peer(d))], returned.at[rows(rad)],
            bsend.at[d], brecv.at[d], mode, rad_peer(d),
        )

    for copy in given[:6]:
        copy.wait()
    dispatch(own, cell, pos, vel, rate, mass, fields)
    pl.semaphore_wait(barrier, count)
    for d in range(1, RADS):
        particle_copy(d).start()
    given[6].wait()
    for k in range(KL):
        outgoing[pl.ds(k, RADII, stride=KL), :] = jnp.transpose(field[k])
    for d in range(1, 1 + EARLY):
        field_copy(d).start()
    arrived[rad] = fields[rad]
    pieces[rows(rad), :] = outgoing[rows(rad), :]
    for d in range(1, RADS):
        particle_copy(d).wait_recv()
    gathered[mode, 0:RADS, :] = arrived[:, 0, :]
    gathered[mode, RADS : 2 * RADS, :] = arrived[:, 1, :]
    for d in (4, 3, 5, 2, 6, 1, 7):
        gather_copy(d).start()
    for d in range(1 + EARLY, RADS):
        field_copy(d).start()

    def prepare(d, carry):
        @pl.when(d > 0)
        def _():
            gather_copy(MODES - d).wait_recv()

        m = mode_peer(d)
        for s in range(RADS):
            column, _ = cell_parts(gathered[m, s : s + 1, :])
            index = iota((256, CAP), 0).astype(F32).astype(BF16)
            onehots[m, :, s * CAP : (s + 1) * CAP] = jnp.where(
                index == column.astype(BF16), jnp.ones((), BF16), jnp.zeros((), BF16)
            )
            weights[m, s] = axial_tile(mode, gathered[m, RADS + s : RADS + s + 1, :])
        return carry

    for copy in given[7:]:
        copy.wait()
    for a in range(MODES):
        flow[a] = base[:, a * ARC : (a + 1) * ARC]
    lax.fori_loop(0, MODES, prepare, 0)
    factor(mode, rad, diag, edge, g_ref)
    known_side(mode, rad, field, prior, known)
    kept = [
        pltpu.make_async_copy(known, known_out, stores.at[0]),
        pltpu.make_async_copy(g_ref, g_out, stores.at[1]),
    ]
    for copy in kept:
        copy.start()

    for d in range(1, RADS):
        field_copy(d).wait_recv()
    forward(pieces, table_hi, table_lo, grid)

    def sample(n, carry):
        d = lax.rem(n + 2, 7) + 1
        sample_arc(mode_peer(d), grid, gathered, onehots, weights, partial)
        reduce_copy(d).start()
        return carry

    lax.fori_loop(0, MODES - 1, sample, 0)
    sample_arc(mode, grid, gathered, onehots, weights, partial)
    parts[mode] = partial[mode]

    def advect(m, carry):
        advect_arc(m, mode, grid, flow, terms)
        return carry

    lax.fori_loop(0, MODES // 2, advect, 0)
    for d in range(1, MODES):
        reduce_copy(d).wait_recv()
    fluid = parts[0]
    for n in range(1, MODES):
        fluid = fluid + parts[n]
    relative = (fluid - arrived[:, 2, :]) * arrived[:, 3, :]
    pushes[mode] = -arrived[:, 4, :] * relative
    for d in (4, 3, 5, 2, 6, 1, 7):
        push_back(d).start()
    lax.fori_loop(MODES // 2, MODES, advect, 0)
    deposit_arc(mode, gathered, onehots, weights, pushes, masses, terms)

    def place(n, carry):
        d = lax.rem(n + 5, 7) + 1
        push_back(MODES - d).wait_recv()
        deposit_arc(mode_peer(d), gathered, onehots, weights, pushes, masses, terms)
        return carry

    lax.fori_loop(0, MODES - 1, place, 0)
    first = jnp.concatenate([terms[a] for a in range(4)], axis=1)
    second = jnp.concatenate([terms[a + 4] for a in range(4)], axis=1)
    hi, lo = split(jnp.concatenate([first + second, first - second], axis=0))
    splits[0] = hi
    splits[1] = lo
    parity = iota((1, 128), 1) % 2 == 0
    top = iota((1, 8, 1), 1) < KL

    def inverse(n, carry):
        j = lax.rem(rad + n, 6)
        ib = j + j // 3
        block = pl.ds(pl.multiple_of(ib * 128, 128), 128)
        th, tl = table_hi[block, :], table_lo[block, :]
        out = mm_nt(splits[0], th) + mm_nt(splits[1], th) + mm_nt(splits[0], tl)
        chosen = jnp.where(parity, out[: 2 * ROWS], out[2 * ROWS :]).reshape(HB, 2, 8, 128)
        even, odd = chosen[:, 0], chosen[:, 1]
        real = jnp.where(top, even, pltpu.roll(odd, 4, 1))
        imag = jnp.where(top, pltpu.roll(even, 4, 1), odd)
        spectral[rows(ib), :] = real.reshape(ROWS, 128)
        spectral[rows(8 + ib), :] = imag.reshape(ROWS, 128)
        for c in range(2):
            d = lax.rem(c * 8 + ib - rad + RADS, RADS)

            @pl.when(d > 0)
            def _():
                back_copy(d).start()

            @pl.when(d == 0)
            def _():
                own_back.start()

        return carry

    own_back = pltpu.make_async_copy(
        spectral.at[rows(rad)], returned.at[rows(rad)], stores.at[2]
    )
    lax.fori_loop(0, 6, inverse, 0)
    takes = lax.rem(rad, 4) != 3
    for copy in kept:
        copy.wait()
    for d in range(1, RADS):
        particle_copy(d).wait_send()
        field_copy(d).wait_send()
    for d in range(1, MODES):
        gather_copy(d).wait_send()
        reduce_copy(d).wait_send()
        push_back(d).wait_send()
    for d in range(1, RADS):
        @pl.when(lax.rem(rad_peer(d), 4) != 3)
        def _():
            back_copy(d).wait_send()

        @pl.when(takes)
        def _():
            back_copy(d).wait_recv()

    @pl.when(takes)
    def _():
        own_back.wait()


def band_rows():
    off = iota((1, RADII), 1).astype(F32)
    inverse = (RADII * RADII) / (off + 0.5)
    last = off == RADII - 1
    lower = off * inverse
    upper = jnp.where(last, 0.0, (off + 1.0) * inverse)
    centre = -(off + (off + 1.0) * jnp.where(last, 2.0, 1.0)) * inverse
    radius = (off + 0.5) / RADII
    return lower, upper, centre, radius * radius


def solve_body(returned, known, keep, g_ref, nxt, forcing, rhs, work):
    rad = lax.axis_index("rad")
    half = RADII // 2
    lane = lax.rem(rad, 8) * 128 + iota((8, 128), 1)
    m = jnp.where(lane <= HALF, lane, lane - HALF)
    sub = iota((8, 128), 0)
    most = jnp.where(
        sub % KL == 0, keep[0], jnp.where(sub % KL == 1, keep[1], jnp.where(sub % KL == 2, keep[2], keep[3]))
    )
    kept_here = m <= most
    top = sub < KL
    gain = time_step * gamma_rk

    def rows(q):
        return pl.ds(pl.multiple_of(q * 8, 8), 8)

    def fold(q, carry):
        sides = []
        for n in (q, half - 1 - q):
            kept = jnp.where(kept_here, returned[rows(n), :], 0.0)
            rhs[rows(n), :] = kept
            sides.append(known[rows(n), :] + gain * kept)
        work[2 * q] = jnp.where(top, sides[0], sides[1]) * g_ref[2 * q]
        odd = pltpu.roll(jnp.where(top, sides[1], sides[0]), 4, 0)
        work[2 * q + 1] = odd * g_ref[2 * q + 1]
        return carry

    lax.fori_loop(0, half // 2, fold, 0, unroll=8)
    for k in range(KL):
        forcing[k] = jnp.transpose(rhs[pl.ds(k, RADII, stride=KL), :])

    scale = -implicit * RADII * RADII

    def couplings(j):
        r = jnp.where(top, j, RADII - 1 - j)
        off = r.astype(F32)
        inverse = scale / (off + 0.5)
        after = jnp.where(r == RADII - 1, 0.0, off + 1.0)
        return jnp.where(top, off, after) * inverse, jnp.where(top, after, off) * inverse

    def down(j, d):
        outer, _ = couplings(j)
        d = work[j] - (outer * g_ref[j]) * d
        work[j] = d
        return d

    d = lax.fori_loop(0, half, down, jnp.zeros((8, 128), F32), unroll=8)
    _, inner = couplings(half - 1)
    v = inner * g_ref[half - 1]
    x = (d - v * pltpu.roll(d, 4, 0)) / (1.0 - v * pltpu.roll(v, 4, 0))
    work[half - 1] = x

    def back(n, x):
        j = half - 2 - n
        _, inner = couplings(j)
        x = work[j] - (inner * g_ref[j]) * x
        work[j] = x
        return x

    lax.fori_loop(0, half - 1, back, x, unroll=8)

    def unfold(q, carry):
        even = work[2 * q]
        odd = pltpu.roll(work[2 * q + 1], 4, 0)
        rhs[rows(q), :] = jnp.where(top, even, odd)
        rhs[rows(half - 1 - q), :] = jnp.where(top, odd, even)
        return carry

    lax.fori_loop(0, half // 2, unfold, 0, unroll=8)
    for k in range(KL):
        nxt[k] = jnp.transpose(rhs[pl.ds(k, RADII, stride=KL), :])


def vmem_call(body, outs, n_in, scratch, collective=None, smem=(), name=None, space=VMEM):
    spec = [
        pl.BlockSpec(memory_space=pltpu.SMEM if n in smem else space) for n in range(n_in)
    ]
    params = dict(vmem_limit_bytes=56 * 1024 * 1024)
    if collective is not None:
        params.update(collective_id=collective, has_side_effects=True)
    return pl.pallas_call(
        body,
        out_shape=[jax.ShapeDtypeStruct(s, F32) for s in outs],
        in_specs=spec,
        out_specs=[pl.BlockSpec(memory_space=space)] * len(outs),
        scratch_shapes=scratch,
        compiler_params=pltpu.CompilerParams(**params),
        name=name,
    )


DMA = pltpu.SemaphoreType.DMA


def per_device(
    field_coef,
    prior_forcing,
    base_flow,
    keep_modes,
    owner_band,
    cell_index,
    axial_pos,
    particle_vel,
    response_rate,
    particle_mass,
):
    high, low = fourier_half()
    table_hi, table_lo = jnp.asarray(high), jnp.asarray(low)

    def row(x):
        return x.reshape(1, P_DEV)

    all_rows = (RADS * ROWS, 128)
    tiles = (RADII // 2, 8, 128)
    slots = (MODES, RADS, CAP)
    returned, known, g = vmem_call(
        substep_body,
        [all_rows, all_rows, tiles],
        11,
        [
            VMEM(field_coef.shape, F32),
            VMEM(field_coef.shape, F32),
            VMEM(base_flow.shape, F32),
            VMEM((1, P_DEV), jnp.int32),
            VMEM((1, P_DEV), jnp.int32),
            VMEM((1, P_DEV), F32),
            VMEM((1, P_DEV), F32),
            VMEM((1, P_DEV), F32),
            VMEM((1, P_DEV), F32),
            VMEM(table_hi.shape, BF16),
            VMEM(table_hi.shape, BF16),
            VMEM(all_rows, F32),
            VMEM(tiles, F32),
            VMEM(all_rows, F32),
            VMEM(all_rows, F32),
            VMEM((RADS, 8, CAP), F32),
            VMEM((RADS, 8, CAP), F32),
            VMEM((MODES, 2 * RADS, CAP), F32),
            VMEM(tiles, F32),
            VMEM(tiles, F32),
            VMEM((MODES, BAND, ARC), F32),
            VMEM((MODES, 2 * ROWS, 128), F32),
            VMEM((MODES, 2 * ROWS, 128), F32),
            VMEM(all_rows, F32),
            VMEM((MODES, 256, RADS * CAP), BF16),
            VMEM((MODES, RADS, 8, CAP), F32),
            VMEM((2 * ROWS, RADS * CAP), BF16),
            VMEM((2, 4 * ROWS, HALF), BF16),
            VMEM(slots, F32),
            VMEM(slots, F32),
            VMEM(slots, F32),
            DMA((11,)), DMA((3,)),
            DMA((RADS,)), DMA((RADS,)), DMA((RADS,)), DMA((RADS,)),
            DMA((MODES,)), DMA((MODES,)), DMA((MODES,)), DMA((MODES,)),
            DMA((MODES,)), DMA((MODES,)), DMA((RADS,)), DMA((RADS,)),
        ],
        collective=0,
        name="substep",
        space=pl.ANY,
    )(
        field_coef, prior_forcing, base_flow, row(owner_band), row(cell_index), row(axial_pos),
        row(particle_vel), row(response_rate), row(particle_mass), table_hi, table_lo,
    )
    field_next, forcing = vmem_call(
        solve_body,
        [(KL, 128, RADII), (KL, 128, RADII)],
        4,
        [VMEM(all_rows, F32), VMEM(tiles, F32)],
        smem=(2,),
        name="solve",
    )(returned, known, keep_modes, g)
    return (field_next, forcing)


def solution(mesh):
    in_specs = (
        P("mode", "rad", None),
        P("mode", "rad", None),
        P("rad", None),
        P("mode"),
        P(("mode", "rad"), None),
        P(("mode", "rad")),
        P(("mode", "rad")),
        P(("mode", "rad")),
        P(("mode", "rad")),
        P(("mode", "rad")),
    )
    out_specs = (P("mode", "rad", None), P("mode", "rad", None))
    return jax.shard_map(
        per_device, mesh=mesh, in_specs=in_specs, out_specs=out_specs, check_vma=False
    )
```

```python
import math

import jax
import jax.numpy as jnp
import ml_dtypes
import numpy as np
from jax import lax
from jax.experimental import pallas as pl
from jax.experimental.pallas import tpu as pltpu
from jax.sharding import PartitionSpec as P

time_step = 0.5
viscosity = 0.0004
alpha_rk = 1.0 / 15.0
beta_rk = 1.0 / 15.0
gamma_rk = 5.0 / 12.0
zeta_rk = -17.0 / 60.0

RADII = 384
AZIM = 1024
HALF = 512
KZ = 32
P_DEV = 2048
BAND = 24
ARC = 128
CAP = 256
MODES = 8
RADS = 16
KL = 4
ROWS = BAND * KL
F32 = jnp.float32
BF16 = jnp.bfloat16
MESH = pl.DeviceIdType.MESH
implicit = beta_rk * time_step * viscosity
VMEM = pltpu.VMEM


def fourier_half():
    i = np.arange(AZIM)
    m = np.where(i <= HALF, i, i - HALF)
    t = np.arange(HALF)
    angle = 2.0 * math.pi * ((t[None, :] * m[:, None]) % AZIM) / AZIM
    scale = np.where((m == 0) | (i == HALF), math.sqrt(1.0 / AZIM), math.sqrt(2.0 / AZIM))
    table = (np.where((i > HALF)[:, None], np.sin(angle), np.cos(angle)) * scale[:, None]).astype(
        np.float32
    )
    high = table.astype(ml_dtypes.bfloat16)
    low = (table - high.astype(np.float32)).astype(ml_dtypes.bfloat16)
    return high, low


def split(x):
    high = x.astype(BF16)
    return high, (x - high.astype(F32)).astype(BF16)


def mm(a, b):
    return lax.dot_general(a, b, (((1,), (0,)), ((), ())), preferred_element_type=F32)


def mm_nt(a, b):
    return lax.dot_general(a, b, (((1,), (1,)), ((), ())), preferred_element_type=F32)


def iota(shape, dim):
    return lax.broadcasted_iota(jnp.int32, shape, dim)


def greet(mode_peers, rad_peers):
    barrier = pltpu.get_barrier_semaphore()
    mode, rad = lax.axis_index("mode"), lax.axis_index("rad")
    if rad_peers:
        for d in range(1, RADS):
            pl.semaphore_signal(
                barrier, inc=1, device_id=(mode, lax.rem(rad + d, RADS)), device_id_type=MESH
            )
    if mode_peers:
        for d in range(1, MODES):
            pl.semaphore_signal(
                barrier, inc=1, device_id=(lax.rem(mode + d, MODES), rad), device_id_type=MESH
            )
    return barrier, (RADS - 1) * rad_peers + (MODES - 1) * mode_peers


def push_copy(src, dst, send, recv, mode, rad):
    return pltpu.make_async_remote_copy(
        src_ref=src,
        dst_ref=dst,
        send_sem=send,
        recv_sem=recv,
        device_id=(mode, rad),
        device_id_type=MESH,
    )


def radial_tiles(shape, dims):
    j = iota(shape, dims[0])
    sub = iota(shape, dims[1])
    return jnp.where(sub < 4, j, RADII - 1 - j), sub


def factor(mode, rad, diag_ref, edge_ref, g_ref):
    shape = (RADII // 2, 8, 128)
    r, sub = radial_tiles(shape, (0, 1))
    off = r.astype(F32)
    inverse = (RADII * RADII) / (off + 0.5)
    last = r == RADII - 1
    centre = -(off + (off + 1.0) * jnp.where(last, 2.0, 1.0)) * inverse
    k = mode * KL + sub % KL
    kappa = 0.5 + 1.5 * k.astype(F32) / KZ
    coef = lax.rem(rad, 8) * 128 + iota(shape, 2)
    m = jnp.where(coef <= HALF, coef, coef - HALF).astype(F32)
    unit = (off + 0.5) / RADII
    diagonal = centre - m * m / (unit * unit) - kappa * kappa
    diag_ref[...] = (1.0 - implicit * diagonal) * (off + 0.5)
    outer = (implicit * RADII * RADII) * jnp.where(sub < 4, off, off + 1.0)
    edge_ref[...] = outer * outer

    def step(j, g):
        g = 1.0 / (diag_ref[j] - edge_ref[j] * g)
        g_ref[j] = g
        return g

    lax.fori_loop(0, RADII // 2, step, jnp.zeros((8, 128), F32))


def dispatch(own, cell, pos, vel, rate, mass, fields_ref):
    owner = own[...]
    bands = iota((RADS, P_DEV), 0)
    match = (bands == owner).astype(F32)
    match_bf = match.astype(BF16)
    chunk = 256
    tri = (iota((chunk, chunk), 0) < iota((chunk, chunk), 1)).astype(F32).astype(BF16)
    running = jnp.zeros((RADS, 1), F32)
    places = []
    for n in range(P_DEV // chunk):
        part = match[:, n * chunk : (n + 1) * chunk]
        ahead = mm(match_bf[:, n * chunk : (n + 1) * chunk], tri) + running
        places.append(jnp.sum(ahead * part, axis=0, keepdims=True))
        running = running + jnp.sum(part, axis=1, keepdims=True)
    place = jnp.concatenate(places, axis=1).astype(jnp.int32)
    slots = (iota((CAP, P_DEV), 0) == place).astype(F32).astype(BF16)
    cells = cell[...]
    pieces = [(cells // ARC).astype(F32), (cells % ARC).astype(F32)]
    for ref in (pos, vel, rate, mass):
        left = ref[...]
        for _ in range(3):
            piece = left.astype(BF16).astype(F32)
            pieces.append(piece)
            left = left - piece
    rows = jnp.concatenate([jnp.where(match > 0.5, p, 0.0) for p in pieces], axis=0).astype(BF16)
    sorted_rows = mm_nt(rows, slots)

    def take(n):
        return sorted_rows[n * RADS : (n + 1) * RADS]

    fields_ref[:, 0, :] = take(0) * ARC + take(1)
    for f in range(4):
        fields_ref[:, 1 + f, :] = take(2 + 3 * f) + take(3 + 3 * f) + take(4 + 3 * f)
    for f in range(5, 8):
        fields_ref[:, f, :] = jnp.zeros((RADS, CAP), F32)


def cell_parts(cells):
    r = jnp.floor(cells * (1.0 / ARC))
    half = jnp.where(r >= BAND // 2, 1.0, 0.0)
    return cells + (half - r) * ARC, r - half * (BAND // 2)


QUARTER_HI = 1.57077026367187500
QUARTER_LO = math.pi / 2 - QUARTER_HI


def axial_tile(mode, positions):
    sub = iota((8, 1), 0)
    k = mode * KL + sub % KL
    kappa = 0.5 + 1.5 * k.astype(F32) / KZ
    phases = kappa * positions
    turns = jnp.floor(phases * (2.0 / math.pi) + 0.5)
    x = (phases - turns * QUARTER_HI) - turns * QUARTER_LO
    y = x * x
    sine = x + x * y * (-1.0 / 6 + y * (1.0 / 120 + y * (-1.0 / 5040 + y * (1.0 / 362880))))
    cosine = 1.0 + y * (-0.5 + y * (1.0 / 24 + y * (-1.0 / 720 + y * (1.0 / 40320))))
    quadrant = turns.astype(jnp.int32) + sub // KL
    scaling = 1.0 / math.sqrt(KZ)
    value = jnp.where((quadrant & 1) == 0, cosine, sine)
    return value * jnp.where(((quadrant + 1) & 2) == 0, scaling, -scaling)


HB = BAND // 2
EARLY = 10
NEAR = (1, 3, 4, 12, 2, 5, 7, 8, 13, 15, 6, 14, 9, 11, 10)


def known_side(mode, rad, field, prior, known):
    lower, upper, centre, radius_sq = band_rows()
    coef = lax.rem(rad, 8) * 128 + iota((128, 1), 0)
    m_col = jnp.where(coef <= HALF, coef, coef - HALF).astype(F32)
    wave = m_col * m_col / radius_sq
    for k in range(KL):
        kappa = 0.5 + 1.5 * (mode * KL + k).astype(F32) / KZ
        f = field[k]
        diagonal = centre - wave - kappa * kappa
        laplace = lower * pltpu.roll(f, 1, 1) + diagonal * f + upper * pltpu.roll(f, RADII - 1, 1)
        side = f + time_step * (alpha_rk * viscosity * laplace + zeta_rk * prior[k])
        known[pl.ds(k, RADII, stride=KL), :] = jnp.transpose(side)


def forward(pieces, table_hi, table_lo, grid):
    sign = jnp.where(iota((1, AZIM), 1) % 2 == 0, 1.0, -1.0)
    xs = []
    for c in range(2):
        xs.append(jnp.concatenate(
            [pieces[(c * 8 + ib) * ROWS : (c * 8 + ib + 1) * ROWS, :] for ib in range(8)], axis=1
        ).reshape(HB, 8, AZIM))
    top = iota((1, 8, 1), 1) < KL
    even = jnp.where(top, xs[0], pltpu.roll(xs[1], 4, 1))
    odd = jnp.where(top, pltpu.roll(xs[0], 4, 1), xs[1])
    x = jnp.stack([even, odd], axis=1).reshape(2 * ROWS, AZIM)
    hi, lo = split(jnp.concatenate([x, x * sign], axis=0))
    for n in range(2):
        cols = slice(n * 256, (n + 1) * 256)
        th, tl = table_hi[:, cols], table_lo[:, cols]
        out = mm(hi, th) + mm(lo, th) + mm(hi, tl)
        for half in range(2):
            for a in range(2):
                grid[half * 4 + n * 2 + a] = out[
                    half * 2 * ROWS : (half + 1) * 2 * ROWS, a * 128 : (a + 1) * 128
                ]


def sample_arc(m, grid, gathered, onehots, weights, partial):
    hi, lo = split(jnp.concatenate([grid[m, :ROWS, :], grid[m, ROWS:, :]], axis=1))
    lhs = jnp.concatenate([hi, lo], axis=0)
    for s in range(RADS):
        _, rh = cell_parts(gathered[m, s : s + 1, :])
        both = mm(lhs, onehots[m, :, s * CAP : (s + 1) * CAP])
        values = both[:ROWS] + both[ROWS:]
        taken = jnp.zeros((8, CAP), F32)
        for q in range(HB):
            taken = jnp.where(rh == q, values[q * 8 : (q + 1) * 8], taken)
        partial[m, s : s + 1, :] = jnp.sum(taken * weights[m, s], axis=0, keepdims=True)


def deposit_arc(m, gathered, onehots, weights, pushes, masses, terms):
    for s in range(RADS):
        _, rh = cell_parts(gathered[m, s : s + 1, :])
        value = pushes[m, s : s + 1, :] * weights[m, s]
        high = value.astype(BF16).astype(F32)
        low = value - high
        rows = [jnp.where(rh == q, high, 0.0) for q in range(HB)]
        rows += [jnp.where(rh == q, low, 0.0) for q in range(HB)]
        masses[:, s * CAP : (s + 1) * CAP] = jnp.concatenate(rows, axis=0).astype(BF16)
    both = mm_nt(masses[...], onehots[m])
    deposit = both[:ROWS] + both[ROWS:]
    for h in range(2):
        rows = slice(h * ROWS, (h + 1) * ROWS)
        terms[m, rows, :] = terms[m, rows, :] + deposit[:, h * 128 : (h + 1) * 128]


def advect_arc(m, mode, grid, flow, terms):
    sub = iota((8, 1), 0)
    kappa = 0.5 + 1.5 * (mode * KL + sub % KL).astype(F32) / KZ
    kappa = jnp.where(sub < KL, kappa, -kappa)
    for r in range(BAND):
        rows = slice(r * 8, (r + 1) * 8)
        swapped = pltpu.roll(grid[m, rows, :], 4, 0)
        terms[m, rows, :] = kappa * flow[m, r : r + 1, :] * swapped


def substep_body(
    field_in, prior_in, base_in, own_in, cell_in, pos_in, vel_in, rate_in, mass_in, hi_in, lo_in,
    returned, known_out, g_out,
    field, prior, base, own, cell, pos, vel, rate, mass, table_hi, table_lo, known, g_ref,
    outgoing, pieces, fields, arrived, gathered, diag, edge, flow, grid, terms, spectral,
    onehots, weights, masses, splits, partial, twins, totals, parts, pushes, loads, stores,
    fsend, frecv, psend, precv, gsend, grecv, tsend, trecv, rsend, rrecv, asend, arecv, csend, crecv,
    bsend, brecv,
):
    mode, rad = lax.axis_index("mode"), lax.axis_index("rad")
    barrier, count = greet(True, True)
    given = [
        (own_in, own), (cell_in, cell), (pos_in, pos), (vel_in, vel), (rate_in, rate),
        (mass_in, mass), (field_in, field), (hi_in, table_hi), (lo_in, table_lo),
        (prior_in, prior), (base_in, base),
    ]
    given = [pltpu.make_async_copy(x, y, loads.at[n]) for n, (x, y) in enumerate(given)]
    for copy in given:
        copy.start()

    def rows(n):
        return pl.ds(pl.multiple_of(n * ROWS, 8), ROWS)

    x, y = rad // 4, lax.rem(rad, 4)
    z, core = mode // 2, lax.rem(mode, 2)
    twin = z * 2 + 1 - core

    def rad_peer(d):
        return lax.rem(x + d // 4, 4) * 4 + lax.rem(y + lax.rem(d, 4), 4)

    def mode_peer(d):
        return lax.rem(mode + d, MODES)

    def particle_copy(d):
        return push_copy(
            fields.at[rad_peer(d)], arrived.at[rad], psend.at[d], precv.at[d], mode, rad_peer(d)
        )

    def field_copy(d):
        return push_copy(
            outgoing.at[rows(rad_peer(d))], pieces.at[rows(rad)],
            fsend.at[d], frecv.at[d], mode, rad_peer(d),
        )

    def gather_copy(d):
        return push_copy(
            gathered.at[mode], gathered.at[mode], gsend.at[d], grecv.at[d], mode_peer(d), rad
        )

    def above(o):
        return lax.rem(z + o, 4) * 2 + core

    def twin_part(o):
        return push_copy(
            partial.at[lax.rem(z + o, 4) * 2 + 1 - core], twins.at[o],
            tsend.at[o], trecv.at[o], twin, rad,
        )

    def reduce_copy(o):
        return push_copy(
            totals.at[o], parts.at[o], rsend.at[o], rrecv.at[o], above(o), rad
        )

    def push_copy_above(o):
        return push_copy(
            pushes.at[mode], pushes.at[mode], asend.at[o], arecv.at[o], above(o), rad
        )

    def push_copy_twin(o):
        from_below = lax.rem(z - o + 4, 4) * 2 + core
        return push_copy(
            pushes.at[from_below], pushes.at[from_below], csend.at[o], crecv.at[o], twin, rad
        )

    def back_copy(d):
        return push_copy(
            spectral.at[rows(rad_peer(d))], returned.at[rows(rad)],
            bsend.at[d], brecv.at[d], mode, rad_peer(d),
        )

    for copy in given[:6]:
        copy.wait()
    dispatch(own, cell, pos, vel, rate, mass, fields)
    given[6].wait()
    for k in range(KL):
        outgoing[pl.ds(k, RADII, stride=KL), :] = jnp.transpose(field[k])
    pl.semaphore_wait(barrier, count)
    for d in NEAR[::-1]:
        particle_copy(d).start()
    for d in NEAR[:EARLY]:
        field_copy(d).start()
    arrived[rad] = fields[rad]
    pieces[rows(rad), :] = outgoing[rows(rad), :]
    for copy in given[7:]:
        copy.wait()
    known_side(mode, rad, field, prior, known)
    for d in NEAR:
        particle_copy(d).wait_recv()
    gathered[mode, 0:RADS, :] = arrived[:, 0, :]
    gathered[mode, RADS : 2 * RADS, :] = arrived[:, 1, :]
    for d in (4, 3, 5, 2, 6, 1, 7):
        gather_copy(d).start()
    for d in NEAR[EARLY:]:
        field_copy(d).start()
    factor(mode, rad, diag, edge, g_ref)
    kept = [
        pltpu.make_async_copy(known, known_out, stores.at[0]),
        pltpu.make_async_copy(g_ref, g_out, stores.at[1]),
    ]
    for copy in kept:
        copy.start()
    for a in range(MODES):
        flow[a] = base[:, a * ARC : (a + 1) * ARC]

    def prepare(d, carry):
        @pl.when(d > 0)
        def _():
            gather_copy(MODES - d).wait_recv()

        m = mode_peer(d)
        for s in range(RADS):
            column, _ = cell_parts(gathered[m, s : s + 1, :])
            index = iota((256, CAP), 0).astype(F32).astype(BF16)
            onehots[m, :, s * CAP : (s + 1) * CAP] = jnp.where(
                index == column.astype(BF16), jnp.ones((), BF16), jnp.zeros((), BF16)
            )
            weights[m, s] = axial_tile(mode, gathered[m, RADS + s : RADS + s + 1, :])
        return carry

    lax.fori_loop(0, MODES, prepare, 0)
    for d in range(1, RADS):
        field_copy(d).wait_recv()
    forward(pieces, table_hi, table_lo, grid)

    def outward(n):
        t = lax.rem(n + 2, 4)
        return t + (n // 2) * (1 - 2 * t)

    def sample_twin(n, carry):
        o = outward(n)
        m = lax.rem(z + o, 4) * 2 + 1 - core
        sample_arc(m, grid, gathered, onehots, weights, partial)
        twin_part(o).start()
        return carry

    def sample_own(n, carry):
        o = outward(n)
        m = above(o)
        sample_arc(m, grid, gathered, onehots, weights, partial)
        twin_part(o).wait_recv()
        totals[o] = partial[m] + twins[o]

        @pl.when(o > 0)
        def _():
            reduce_copy(o).start()

        return carry

    def advect(m, carry):
        advect_arc(m, mode, grid, flow, terms)
        return carry

    lax.fori_loop(0, 4, sample_twin, 0)
    lax.fori_loop(0, 4, sample_own, 0)
    lax.fori_loop(0, MODES, advect, 0)
    for o in (1, 3, 2):
        reduce_copy(o).wait_recv()
    fluid = (totals[0] + parts[1]) + (parts[2] + parts[3])
    relative = (fluid - arrived[:, 2, :]) * arrived[:, 3, :]
    pushes[mode] = -arrived[:, 4, :] * relative
    for o in (2, 3, 1):
        push_copy_above(o).start()
    push_copy_twin(0).start()

    def arrive(o):
        push_copy_above(o).wait_recv()
        push_copy_twin(o).start()

    def place(n, carry):
        j = jnp.where(n < 2, 0, lax.rem(n - 2, 3) + 1)
        o = j + (j // 2) * (5 - 2 * j)
        b = jnp.where((n == 1) | (n > 4), 1, 0)

        @pl.when(n == 2)
        def _():
            arrive(1)
            arrive(3)

        @pl.when(n == 3)
        def _():
            arrive(2)

        @pl.when(b == 1)
        def _():
            push_copy_twin(o).wait_recv()

        m = lax.rem(z - o + 4, 4) * 2 + lax.rem(core + b, 2)
        deposit_arc(m, gathered, onehots, weights, pushes, masses, terms)
        return carry

    lax.fori_loop(0, MODES, place, 0)
    first = jnp.concatenate([terms[a] for a in range(4)], axis=1)
    second = jnp.concatenate([terms[a + 4] for a in range(4)], axis=1)
    hi, lo = split(jnp.concatenate([first + second, first - second], axis=0))
    splits[0] = hi
    splits[1] = lo
    parity = iota((1, 128), 1) % 2 == 0
    top = iota((1, 8, 1), 1) < KL

    def inverse(n, carry):
        line = lax.rem(y + n // 2 + 2, 4)

        @pl.when(line != 3)
        def _():
            ib = lax.rem(x + n, 2) * 4 + line
            block = pl.ds(pl.multiple_of(ib * 128, 128), 128)
            th, tl = table_hi[block, :], table_lo[block, :]
            out = mm_nt(splits[0], th) + mm_nt(splits[1], th) + mm_nt(splits[0], tl)
            chosen = jnp.where(parity, out[: 2 * ROWS], out[2 * ROWS :]).reshape(HB, 2, 8, 128)
            even, odd = chosen[:, 0], chosen[:, 1]
            real = jnp.where(top, even, pltpu.roll(odd, 4, 1))
            imag = jnp.where(top, pltpu.roll(even, 4, 1), odd)
            spectral[rows(ib), :] = real.reshape(ROWS, 128)
            spectral[rows(8 + ib), :] = imag.reshape(ROWS, 128)
            for c in range(2):
                dx = lax.rem(2 * c + ib // 4 - x + 4, 4)
                d = dx * 4 + lax.rem(line - y + 4, 4)

                @pl.when(d > 0)
                def _():
                    back_copy(d).start()

                @pl.when(d == 0)
                def _():
                    own_back.start()

        return carry

    own_back = pltpu.make_async_copy(
        spectral.at[rows(rad)], returned.at[rows(rad)], stores.at[2]
    )
    lax.fori_loop(0, 8, inverse, 0)
    takes = lax.rem(rad, 4) != 3
    for copy in kept:
        copy.wait()
    for d in range(1, RADS):
        particle_copy(d).wait_send()
        field_copy(d).wait_send()
    for d in range(1, MODES):
        gather_copy(d).wait_send()
    for o in range(4):
        twin_part(o).wait_send()
        push_copy_twin(o).wait_send()
        if o:
            reduce_copy(o).wait_send()
            push_copy_above(o).wait_send()
    for d in range(1, RADS):
        @pl.when(lax.rem(rad_peer(d), 4) != 3)
        def _():
            back_copy(d).wait_send()

        @pl.when(takes)
        def _():
            back_copy(d).wait_recv()

    @pl.when(takes)
    def _():
        own_back.wait()


def band_rows():
    off = iota((1, RADII), 1).astype(F32)
    inverse = (RADII * RADII) / (off + 0.5)
    last = off == RADII - 1
    lower = off * inverse
    upper = jnp.where(last, 0.0, (off + 1.0) * inverse)
    centre = -(off + (off + 1.0) * jnp.where(last, 2.0, 1.0)) * inverse
    radius = (off + 0.5) / RADII
    return lower, upper, centre, radius * radius


def solve_body(returned, known, keep, g_ref, nxt_out, forcing_out, rhs, work, nxt, forcing, sems):
    rad = lax.axis_index("rad")
    half = RADII // 2
    lane = lax.rem(rad, 8) * 128 + iota((8, 128), 1)
    m = jnp.where(lane <= HALF, lane, lane - HALF)
    sub = iota((8, 128), 0)
    most = jnp.where(
        sub % KL == 0, keep[0], jnp.where(sub % KL == 1, keep[1], jnp.where(sub % KL == 2, keep[2], keep[3]))
    )
    kept_here = m <= most
    top = sub < KL
    gain = time_step * gamma_rk
    scale = -implicit * RADII * RADII
    slope = jnp.where(top, 1.0, -1.0)
    outer_start = jnp.where(top, 0.0, scale * RADII)
    inner_start = jnp.where(top, scale, scale * (RADII - 1))

    def rows(q):
        return pl.ds(pl.multiple_of(q * 8, 8), 8)

    def weighed(j):
        return (jnp.where(top, 0.5, RADII - 0.5) + slope * j.astype(F32)) * g_ref[j]

    def fold(q, carry):
        sides = []
        for n in (q, half - 1 - q):
            kept = jnp.where(kept_here, returned[rows(n), :], 0.0)
            rhs[rows(n), :] = kept
            sides.append(known[rows(n), :] + gain * kept)
        work[2 * q] = jnp.where(top, sides[0], sides[1]) * weighed(2 * q)
        odd = pltpu.roll(jnp.where(top, sides[1], sides[0]), 4, 0)
        work[2 * q + 1] = odd * weighed(2 * q + 1)
        return carry

    def save(n, k, src, dst):
        return pltpu.make_async_copy(src.at[k], dst.at[k], sems.at[n, k])

    lax.fori_loop(0, half // 2, fold, 0, unroll=8)
    for k in range(KL):
        forcing[k] = jnp.transpose(rhs[pl.ds(k, RADII, stride=KL), :])
        save(0, k, forcing, forcing_out).start()

    def down(j, d):
        d = work[j] - ((outer_start + (scale * slope) * j.astype(F32)) * g_ref[j]) * d
        work[j] = d
        return d

    d = lax.fori_loop(0, half, down, jnp.zeros((8, 128), F32), unroll=16)

    def inner(j):
        return (inner_start + (scale * slope) * j.astype(F32)) * g_ref[j]

    v = inner(jnp.int32(half - 1))
    x = (d - v * pltpu.roll(d, 4, 0)) / (1.0 - v * pltpu.roll(v, 4, 0))
    work[half - 1] = x

    def back(n, x):
        j = half - 2 - n
        x = work[j] - inner(j) * x
        work[j] = x
        return x

    lax.fori_loop(0, half - 1, back, x, unroll=16)

    def unfold(q, carry):
        even = work[2 * q]
        odd = pltpu.roll(work[2 * q + 1], 4, 0)
        rhs[rows(q), :] = jnp.where(top, even, odd)
        rhs[rows(half - 1 - q), :] = jnp.where(top, odd, even)
        return carry

    lax.fori_loop(0, half // 2, unfold, 0, unroll=8)
    for k in range(KL):
        nxt[k] = jnp.transpose(rhs[pl.ds(k, RADII, stride=KL), :])
        save(1, k, nxt, nxt_out).start()
    for k in range(KL):
        save(0, k, forcing, forcing_out).wait()
        save(1, k, nxt, nxt_out).wait()


def vmem_call(body, outs, n_in, scratch, collective=None, smem=(), name=None, space=VMEM,
    out_space=None):
    spec = [
        pl.BlockSpec(memory_space=pltpu.SMEM if n in smem else space) for n in range(n_in)
    ]
    params = dict(vmem_limit_bytes=56 * 1024 * 1024)
    if collective is not None:
        params.update(collective_id=collective, has_side_effects=True)
    return pl.pallas_call(
        body,
        out_shape=[jax.ShapeDtypeStruct(s, F32) for s in outs],
        in_specs=spec,
        out_specs=[pl.BlockSpec(memory_space=out_space or space)] * len(outs),
        scratch_shapes=scratch,
        compiler_params=pltpu.CompilerParams(**params),
        name=name,
    )


DMA = pltpu.SemaphoreType.DMA


def per_device(
    field_coef,
    prior_forcing,
    base_flow,
    keep_modes,
    owner_band,
    cell_index,
    axial_pos,
    particle_vel,
    response_rate,
    particle_mass,
):
    high, low = fourier_half()
    table_hi, table_lo = jnp.asarray(high), jnp.asarray(low)

    def row(x):
        return x.reshape(1, P_DEV)

    all_rows = (RADS * ROWS, 128)
    tiles = (RADII // 2, 8, 128)
    slots = (MODES, RADS, CAP)
    returned, known, g = vmem_call(
        substep_body,
        [all_rows, all_rows, tiles],
        11,
        [
            VMEM(field_coef.shape, F32),
            VMEM(field_coef.shape, F32),
            VMEM(base_flow.shape, F32),
            VMEM((1, P_DEV), jnp.int32),
            VMEM((1, P_DEV), jnp.int32),
            VMEM((1, P_DEV), F32),
            VMEM((1, P_DEV), F32),
            VMEM((1, P_DEV), F32),
            VMEM((1, P_DEV), F32),
            VMEM(table_hi.shape, BF16),
            VMEM(table_hi.shape, BF16),
            VMEM(all_rows, F32),
            VMEM(tiles, F32),
            VMEM(all_rows, F32),
            VMEM(all_rows, F32),
            VMEM((RADS, 8, CAP), F32),
            VMEM((RADS, 8, CAP), F32),
            VMEM((MODES, 2 * RADS, CAP), F32),
            VMEM(tiles, F32),
            VMEM(tiles, F32),
            VMEM((MODES, BAND, ARC), F32),
            VMEM((MODES, 2 * ROWS, 128), F32),
            VMEM((MODES, 2 * ROWS, 128), F32),
            VMEM(all_rows, F32),
            VMEM((MODES, 256, RADS * CAP), BF16),
            VMEM((MODES, RADS, 8, CAP), F32),
            VMEM((2 * ROWS, RADS * CAP), BF16),
            VMEM((2, 4 * ROWS, HALF), BF16),
            VMEM(slots, F32),
            VMEM((4, RADS, CAP), F32),
            VMEM((4, RADS, CAP), F32),
            VMEM((4, RADS, CAP), F32),
            VMEM(slots, F32),
            DMA((11,)), DMA((3,)),
            DMA((RADS,)), DMA((RADS,)), DMA((RADS,)), DMA((RADS,)),
            DMA((MODES,)), DMA((MODES,)),
            DMA((4,)), DMA((4,)), DMA((4,)), DMA((4,)), DMA((4,)), DMA((4,)), DMA((4,)), DMA((4,)),
            DMA((RADS,)), DMA((RADS,)),
        ],
        collective=0,
        name="substep",
        space=pl.ANY,
    )(
        field_coef, prior_forcing, base_flow, row(owner_band), row(cell_index), row(axial_pos),
        row(particle_vel), row(response_rate), row(particle_mass), table_hi, table_lo,
    )
    field_next, forcing = vmem_call(
        solve_body,
        [(KL, 128, RADII), (KL, 128, RADII)],
        4,
        [
            VMEM(all_rows, F32),
            VMEM(tiles, F32),
            VMEM(field_coef.shape, F32),
            VMEM(field_coef.shape, F32),
            DMA((2, KL)),
        ],
        smem=(2,),
        name="solve",
        out_space=pl.ANY,
    )(returned, known, keep_modes, g)
    return (field_next, forcing)


def solution(mesh):
    in_specs = (
        P("mode", "rad", None),
        P("mode", "rad", None),
        P("rad", None),
        P("mode"),
        P(("mode", "rad"), None),
        P(("mode", "rad")),
        P(("mode", "rad")),
        P(("mode", "rad")),
        P(("mode", "rad")),
        P(("mode", "rad")),
    )
    out_specs = (P("mode", "rad", None), P("mode", "rad", None))
    return jax.shard_map(
        per_device, mesh=mesh, in_specs=in_specs, out_specs=out_specs, check_vma=False
    )
```

```python
import math

import jax
import jax.numpy as jnp
import ml_dtypes
import numpy as np
from jax import lax
from jax.experimental import pallas as pl
from jax.experimental.pallas import tpu as pltpu
from jax.sharding import PartitionSpec as P

time_step = 0.5
viscosity = 0.0004
alpha_rk = 1.0 / 15.0
beta_rk = 1.0 / 15.0
gamma_rk = 5.0 / 12.0
zeta_rk = -17.0 / 60.0

RADII = 384
AZIM = 1024
HALF = 512
KZ = 32
P_DEV = 2048
BAND = 24
ARC = 128
CAP = 256
MODES = 8
RADS = 16
KL = 4
ROWS = BAND * KL
F32 = jnp.float32
BF16 = jnp.bfloat16
MESH = pl.DeviceIdType.MESH
implicit = beta_rk * time_step * viscosity
VMEM = pltpu.VMEM


def fourier_half():
    i = np.arange(AZIM)
    m = np.where(i <= HALF, i, i - HALF)
    t = np.arange(HALF)
    angle = 2.0 * math.pi * ((t[None, :] * m[:, None]) % AZIM) / AZIM
    scale = np.where((m == 0) | (i == HALF), math.sqrt(1.0 / AZIM), math.sqrt(2.0 / AZIM))
    table = (np.where((i > HALF)[:, None], np.sin(angle), np.cos(angle)) * scale[:, None]).astype(
        np.float32
    )
    high = table.astype(ml_dtypes.bfloat16)
    low = (table - high.astype(np.float32)).astype(ml_dtypes.bfloat16)
    return high, low


def split(x):
    high = x.astype(BF16)
    return high, (x - high.astype(F32)).astype(BF16)


def mm(a, b):
    return lax.dot_general(a, b, (((1,), (0,)), ((), ())), preferred_element_type=F32)


def mm_nt(a, b):
    return lax.dot_general(a, b, (((1,), (1,)), ((), ())), preferred_element_type=F32)


def iota(shape, dim):
    return lax.broadcasted_iota(jnp.int32, shape, dim)


def greet(mode_peers, rad_peers):
    barrier = pltpu.get_barrier_semaphore()
    mode, rad = lax.axis_index("mode"), lax.axis_index("rad")
    if rad_peers:
        for d in NEAR[::-1]:
            there = lax.rem(rad // 4 + d // 4, 4) * 4 + lax.rem(lax.rem(rad, 4) + d % 4, 4)
            pl.semaphore_signal(barrier, inc=1, device_id=(mode, there), device_id_type=MESH)
    if mode_peers:
        for d in (4, 5, 3, 2, 6, 7, 1):
            pl.semaphore_signal(
                barrier, inc=1, device_id=(lax.rem(mode + d, MODES), rad), device_id_type=MESH
            )
    return barrier, (RADS - 1) * rad_peers + (MODES - 1) * mode_peers


def push_copy(src, dst, send, recv, mode, rad):
    return pltpu.make_async_remote_copy(
        src_ref=src,
        dst_ref=dst,
        send_sem=send,
        recv_sem=recv,
        device_id=(mode, rad),
        device_id_type=MESH,
    )


def radial_tiles(shape, dims):
    j = iota(shape, dims[0])
    sub = iota(shape, dims[1])
    return jnp.where(sub < 4, j, RADII - 1 - j), sub


def factor(mode, rad, diag_ref, edge_ref, g_ref):
    shape = (RADII // 2, 8, 128)
    r, sub = radial_tiles(shape, (0, 1))
    off = r.astype(F32)
    inverse = (RADII * RADII) / (off + 0.5)
    last = r == RADII - 1
    centre = -(off + (off + 1.0) * jnp.where(last, 2.0, 1.0)) * inverse
    k = mode * KL + sub % KL
    kappa = 0.5 + 1.5 * k.astype(F32) / KZ
    coef = lax.rem(rad, 8) * 128 + iota(shape, 2)
    m = jnp.where(coef <= HALF, coef, coef - HALF).astype(F32)
    unit = (off + 0.5) / RADII
    diagonal = centre - m * m / (unit * unit) - kappa * kappa
    diag_ref[...] = (1.0 - implicit * diagonal) * (off + 0.5)
    outer = (implicit * RADII * RADII) * jnp.where(sub < 4, off, off + 1.0)
    edge_ref[...] = outer * outer

    def step(j, g):
        g = 1.0 / (diag_ref[j] - edge_ref[j] * g)
        g_ref[j] = g
        return g

    lax.fori_loop(0, RADII // 2, step, jnp.zeros((8, 128), F32))


def dispatch(own, cell, pos, vel, rate, mass, fields_ref):
    owner = own[...]
    bands = iota((RADS, P_DEV), 0)
    match = (bands == owner).astype(F32)
    match_bf = match.astype(BF16)
    chunk = 256
    tri = (iota((chunk, chunk), 0) < iota((chunk, chunk), 1)).astype(F32).astype(BF16)
    running = jnp.zeros((RADS, 1), F32)
    places = []
    for n in range(P_DEV // chunk):
        part = match[:, n * chunk : (n + 1) * chunk]
        ahead = mm(match_bf[:, n * chunk : (n + 1) * chunk], tri) + running
        places.append(jnp.sum(ahead * part, axis=0, keepdims=True))
        running = running + jnp.sum(part, axis=1, keepdims=True)
    place = jnp.concatenate(places, axis=1).astype(jnp.int32)
    slots = (iota((CAP, P_DEV), 0) == place).astype(F32).astype(BF16)
    cells = cell[...]
    pieces = [(cells // ARC).astype(F32), (cells % ARC).astype(F32)]
    for ref in (pos, vel, rate, mass):
        left = ref[...]
        for _ in range(3):
            piece = left.astype(BF16).astype(F32)
            pieces.append(piece)
            left = left - piece
    rows = jnp.concatenate([jnp.where(match > 0.5, p, 0.0) for p in pieces], axis=0).astype(BF16)
    sorted_rows = mm_nt(rows, slots)

    def take(n):
        return sorted_rows[n * RADS : (n + 1) * RADS]

    fields_ref[:, 0, :] = take(0) * ARC + take(1)
    for f in range(4):
        fields_ref[:, 1 + f, :] = take(2 + 3 * f) + take(3 + 3 * f) + take(4 + 3 * f)
    for f in range(5, 8):
        fields_ref[:, f, :] = jnp.zeros((RADS, CAP), F32)


def cell_parts(cells):
    r = jnp.floor(cells * (1.0 / ARC))
    half = jnp.where(r >= BAND // 2, 1.0, 0.0)
    return cells + (half - r) * ARC, r - half * (BAND // 2)


QUARTER_HI = 1.57077026367187500
QUARTER_LO = math.pi / 2 - QUARTER_HI


def axial_tile(mode, positions):
    sub = iota((8, 1), 0)
    k = mode * KL + sub % KL
    kappa = 0.5 + 1.5 * k.astype(F32) / KZ
    phases = kappa * positions
    turns = jnp.floor(phases * (2.0 / math.pi) + 0.5)
    x = (phases - turns * QUARTER_HI) - turns * QUARTER_LO
    y = x * x
    sine = x + x * y * (-1.0 / 6 + y * (1.0 / 120 + y * (-1.0 / 5040 + y * (1.0 / 362880))))
    cosine = 1.0 + y * (-0.5 + y * (1.0 / 24 + y * (-1.0 / 720 + y * (1.0 / 40320))))
    quadrant = turns.astype(jnp.int32) + sub // KL
    scaling = 1.0 / math.sqrt(KZ)
    value = jnp.where((quadrant & 1) == 0, cosine, sine)
    return value * jnp.where(((quadrant + 1) & 2) == 0, scaling, -scaling)


HB = BAND // 2
EARLY = 10
NEAR = (1, 3, 4, 12, 2, 5, 7, 8, 13, 15, 6, 14, 9, 11, 10)


def known_side(mode, rad, field, prior, known):
    lower, upper, centre, radius_sq = band_rows()
    coef = lax.rem(rad, 8) * 128 + iota((128, 1), 0)
    m_col = jnp.where(coef <= HALF, coef, coef - HALF).astype(F32)
    wave = m_col * m_col / radius_sq
    for k in range(KL):
        kappa = 0.5 + 1.5 * (mode * KL + k).astype(F32) / KZ
        f = field[k]
        diagonal = centre - wave - kappa * kappa
        laplace = lower * pltpu.roll(f, 1, 1) + diagonal * f + upper * pltpu.roll(f, RADII - 1, 1)
        side = f + time_step * (alpha_rk * viscosity * laplace + zeta_rk * prior[k])
        known[pl.ds(k, RADII, stride=KL), :] = jnp.transpose(side)


def forward(pieces, table_hi, table_lo, grid):
    sign = jnp.where(iota((1, AZIM), 1) % 2 == 0, 1.0, -1.0)
    xs = []
    for c in range(2):
        xs.append(jnp.concatenate(
            [pieces[(c * 8 + ib) * ROWS : (c * 8 + ib + 1) * ROWS, :] for ib in range(8)], axis=1
        ).reshape(HB, 8, AZIM))
    top = iota((1, 8, 1), 1) < KL
    even = jnp.where(top, xs[0], pltpu.roll(xs[1], 4, 1))
    odd = jnp.where(top, pltpu.roll(xs[0], 4, 1), xs[1])
    x = jnp.stack([even, odd], axis=1).reshape(2 * ROWS, AZIM)
    hi, lo = split(jnp.concatenate([x, x * sign], axis=0))
    for n in range(2):
        cols = slice(n * 256, (n + 1) * 256)
        th, tl = table_hi[:, cols], table_lo[:, cols]
        out = mm(hi, th) + mm(lo, th) + mm(hi, tl)
        for half in range(2):
            for a in range(2):
                grid[half * 4 + n * 2 + a] = out[
                    half * 2 * ROWS : (half + 1) * 2 * ROWS, a * 128 : (a + 1) * 128
                ]


def sample_arc(m, grid, gathered, onehots, weights, partial):
    hi, lo = split(jnp.concatenate([grid[m, :ROWS, :], grid[m, ROWS:, :]], axis=1))
    lhs = jnp.concatenate([hi, lo], axis=0)
    for s in range(RADS):
        _, rh = cell_parts(gathered[m, s : s + 1, :])
        both = mm(lhs, onehots[m, :, s * CAP : (s + 1) * CAP])
        values = both[:ROWS] + both[ROWS:]
        taken = jnp.zeros((8, CAP), F32)
        for q in range(HB):
            taken = jnp.where(rh == q, values[q * 8 : (q + 1) * 8], taken)
        partial[m, s : s + 1, :] = jnp.sum(taken * weights[m, s], axis=0, keepdims=True)


def deposit_arc(m, gathered, onehots, weights, pushes, masses, terms):
    for s in range(RADS):
        _, rh = cell_parts(gathered[m, s : s + 1, :])
        value = pushes[m, s : s + 1, :] * weights[m, s]
        tile = jnp.concatenate(split(value), axis=0)
        place = jnp.broadcast_to(rh.astype(BF16), (16, CAP))
        masses[:, s * CAP : (s + 1) * CAP] = jnp.concatenate(
            [jnp.where(place == q, tile, jnp.zeros((), BF16)) for q in range(HB)], axis=0
        )
    both = mm_nt(masses[...], onehots[m]).reshape(HB, 2, 8, 256)
    deposit = (both[:, 0] + both[:, 1]).reshape(ROWS, 256)
    for h in range(2):
        rows = slice(h * ROWS, (h + 1) * ROWS)
        terms[m, rows, :] = terms[m, rows, :] + deposit[:, h * 128 : (h + 1) * 128]


def advect_arc(m, mode, grid, flow, terms):
    sub = iota((8, 1), 0)
    kappa = 0.5 + 1.5 * (mode * KL + sub % KL).astype(F32) / KZ
    kappa = jnp.where(sub < KL, kappa, -kappa)
    for r in range(BAND):
        rows = slice(r * 8, (r + 1) * 8)
        swapped = pltpu.roll(grid[m, rows, :], 4, 0)
        terms[m, rows, :] = kappa * flow[m, r : r + 1, :] * swapped


def substep_body(
    field_in, prior_in, base_in, own_in, cell_in, pos_in, vel_in, rate_in, mass_in, hi_in, lo_in,
    returned, known_out, g_out,
    field, prior, base, own, cell, pos, vel, rate, mass, table_hi, table_lo, known, g_ref,
    outgoing, pieces, fields, arrived, gathered, diag, edge, flow, grid, terms, spectral,
    onehots, weights, masses, splits, partial, twins, totals, parts, pushes, loads, stores,
    fsend, frecv, psend, precv, gsend, grecv, tsend, trecv, rsend, rrecv, asend, arecv, csend, crecv,
    bsend, brecv,
):
    mode, rad = lax.axis_index("mode"), lax.axis_index("rad")
    barrier, count = greet(True, True)
    given = [
        (own_in, own), (cell_in, cell), (pos_in, pos), (vel_in, vel), (rate_in, rate),
        (mass_in, mass), (field_in, field), (hi_in, table_hi), (lo_in, table_lo),
        (prior_in, prior), (base_in, base),
    ]
    given = [pltpu.make_async_copy(x, y, loads.at[n]) for n, (x, y) in enumerate(given)]
    for copy in given:
        copy.start()

    def rows(n):
        return pl.ds(pl.multiple_of(n * ROWS, 8), ROWS)

    x, y = rad // 4, lax.rem(rad, 4)
    z, core = mode // 2, lax.rem(mode, 2)
    twin = z * 2 + 1 - core

    def rad_peer(d):
        return lax.rem(x + d // 4, 4) * 4 + lax.rem(y + lax.rem(d, 4), 4)

    def mode_peer(d):
        return lax.rem(mode + d, MODES)

    def particle_copy(d):
        return push_copy(
            fields.at[rad_peer(d)], arrived.at[rad], psend.at[d], precv.at[d], mode, rad_peer(d)
        )

    def field_copy(d):
        return push_copy(
            outgoing.at[rows(rad_peer(d))], pieces.at[rows(rad)],
            fsend.at[d], frecv.at[d], mode, rad_peer(d),
        )

    def gather_copy(d):
        return push_copy(
            gathered.at[mode], gathered.at[mode], gsend.at[d], grecv.at[d], mode_peer(d), rad
        )

    def above(o):
        return lax.rem(z + o, 4) * 2 + core

    def twin_part(o):
        return push_copy(
            partial.at[lax.rem(z + o, 4) * 2 + 1 - core], twins.at[o],
            tsend.at[o], trecv.at[o], twin, rad,
        )

    def reduce_copy(o):
        return push_copy(
            totals.at[o], parts.at[o], rsend.at[o], rrecv.at[o], above(o), rad
        )

    def push_copy_above(o):
        return push_copy(
            pushes.at[mode], pushes.at[mode], asend.at[o], arecv.at[o], above(o), rad
        )

    def push_copy_twin(o):
        from_below = lax.rem(z - o + 4, 4) * 2 + core
        return push_copy(
            pushes.at[from_below], pushes.at[from_below], csend.at[o], crecv.at[o], twin, rad
        )

    def back_copy(d):
        return push_copy(
            spectral.at[rows(rad_peer(d))], returned.at[rows(rad)],
            bsend.at[d], brecv.at[d], mode, rad_peer(d),
        )

    for copy in given[:6]:
        copy.wait()
    dispatch(own, cell, pos, vel, rate, mass, fields)
    given[6].wait()
    for k in range(KL):
        outgoing[pl.ds(k, RADII, stride=KL), :] = jnp.transpose(field[k])
    pl.semaphore_wait(barrier, count)
    for d in NEAR[::-1]:
        particle_copy(d).start()
    for d in NEAR[:EARLY]:
        field_copy(d).start()
    arrived[rad] = fields[rad]
    pieces[rows(rad), :] = outgoing[rows(rad), :]
    for copy in given[7:]:
        copy.wait()
    known_side(mode, rad, field, prior, known)
    for d in NEAR:
        particle_copy(d).wait_recv()
    gathered[mode, 0:RADS, :] = arrived[:, 0, :]
    gathered[mode, RADS : 2 * RADS, :] = arrived[:, 1, :]
    for d in (4, 3, 5, 2, 6, 1, 7):
        gather_copy(d).start()
    for d in NEAR[EARLY:]:
        field_copy(d).start()
    factor(mode, rad, diag, edge, g_ref)
    kept = [
        pltpu.make_async_copy(known, known_out, stores.at[0]),
        pltpu.make_async_copy(g_ref, g_out, stores.at[1]),
    ]
    for copy in kept:
        copy.start()
    for a in range(MODES):
        flow[a] = base[:, a * ARC : (a + 1) * ARC]

    def prepare(d, carry):
        @pl.when(d > 0)
        def _():
            gather_copy(MODES - d).wait_recv()

        m = mode_peer(d)
        for s in range(RADS):
            column, _ = cell_parts(gathered[m, s : s + 1, :])
            index = iota((256, CAP), 0).astype(F32).astype(BF16)
            onehots[m, :, s * CAP : (s + 1) * CAP] = jnp.where(
                index == column.astype(BF16), jnp.ones((), BF16), jnp.zeros((), BF16)
            )
            weights[m, s] = axial_tile(mode, gathered[m, RADS + s : RADS + s + 1, :])
        return carry

    lax.fori_loop(0, MODES, prepare, 0)
    for d in range(1, RADS):
        field_copy(d).wait_recv()
    forward(pieces, table_hi, table_lo, grid)

    def outward(n):
        t = lax.rem(n + 2, 4)
        return t + (n // 2) * (1 - 2 * t)

    def sample(n, carry):
        mine = jnp.where((n == 2) | (n == 4) | (n == 5) | (n == 7), 1, 0)
        late = jnp.where(n > 2, 1, 0) + jnp.where(n > 4, 1, 0) + jnp.where(n > 5, 1, 0)
        o = outward(mine * late + (1 - mine) * (n - late))
        m = lax.rem(z + o, 4) * 2 + lax.rem(core + 1 - mine, 2)
        sample_arc(m, grid, gathered, onehots, weights, partial)

        @pl.when(mine == 0)
        def _():
            twin_part(o).start()

        @pl.when(mine == 1)
        def _():
            twin_part(o).wait_recv()
            totals[o] = partial[m] + twins[o]

            @pl.when(o > 0)
            def _():
                reduce_copy(o).start()

        return carry

    def advect(m, carry):
        advect_arc(m, mode, grid, flow, terms)
        return carry

    lax.fori_loop(0, MODES, sample, 0)
    lax.fori_loop(0, MODES, advect, 0)
    for o in (1, 3, 2):
        reduce_copy(o).wait_recv()
    fluid = (totals[0] + parts[1]) + (parts[2] + parts[3])
    relative = (fluid - arrived[:, 2, :]) * arrived[:, 3, :]
    pushes[mode] = -arrived[:, 4, :] * relative
    for o in (2, 3, 1):
        push_copy_above(o).start()
    push_copy_twin(0).start()

    def arrive(o):
        push_copy_above(o).wait_recv()
        push_copy_twin(o).start()

    def place(n, carry):
        j = jnp.where(n < 2, 0, lax.rem(n - 2, 3) + 1)
        o = j + (j // 2) * (5 - 2 * j)
        b = jnp.where((n == 1) | (n > 4), 1, 0)

        @pl.when(n == 2)
        def _():
            arrive(1)
            arrive(3)

        @pl.when(n == 3)
        def _():
            arrive(2)

        @pl.when(b == 1)
        def _():
            push_copy_twin(o).wait_recv()

        m = lax.rem(z - o + 4, 4) * 2 + lax.rem(core + b, 2)
        deposit_arc(m, gathered, onehots, weights, pushes, masses, terms)
        return carry

    lax.fori_loop(0, MODES, place, 0)
    first = jnp.concatenate([terms[a] for a in range(4)], axis=1)
    second = jnp.concatenate([terms[a + 4] for a in range(4)], axis=1)
    hi, lo = split(jnp.concatenate([first + second, first - second], axis=0))
    splits[0] = hi
    splits[1] = lo
    parity = iota((1, 128), 1) % 2 == 0
    top = iota((1, 8, 1), 1) < KL

    def inverse(n, carry):
        line = lax.rem(y + n // 2 + 2, 4)

        @pl.when(line != 3)
        def _():
            ib = lax.rem(x + n, 2) * 4 + line
            block = pl.ds(pl.multiple_of(ib * 128, 128), 128)
            th, tl = table_hi[block, :], table_lo[block, :]
            out = mm_nt(splits[0], th) + mm_nt(splits[1], th) + mm_nt(splits[0], tl)
            chosen = jnp.where(parity, out[: 2 * ROWS], out[2 * ROWS :]).reshape(HB, 2, 8, 128)
            even, odd = chosen[:, 0], chosen[:, 1]
            real = jnp.where(top, even, pltpu.roll(odd, 4, 1))
            imag = jnp.where(top, pltpu.roll(even, 4, 1), odd)
            spectral[rows(ib), :] = real.reshape(ROWS, 128)
            spectral[rows(8 + ib), :] = imag.reshape(ROWS, 128)
            for c in range(2):
                dx = lax.rem(2 * c + ib // 4 - x + 4, 4)
                d = dx * 4 + lax.rem(line - y + 4, 4)

                @pl.when(d > 0)
                def _():
                    back_copy(d).start()

                @pl.when(d == 0)
                def _():
                    own_back.start()

        return carry

    own_back = pltpu.make_async_copy(
        spectral.at[rows(rad)], returned.at[rows(rad)], stores.at[2]
    )
    lax.fori_loop(0, 8, inverse, 0)
    takes = lax.rem(rad, 4) != 3
    for copy in kept:
        copy.wait()
    for d in range(1, RADS):
        particle_copy(d).wait_send()
        field_copy(d).wait_send()
    for d in range(1, MODES):
        gather_copy(d).wait_send()
    for o in range(4):
        twin_part(o).wait_send()
        push_copy_twin(o).wait_send()
        if o:
            reduce_copy(o).wait_send()
            push_copy_above(o).wait_send()
    for d in range(1, RADS):
        @pl.when(lax.rem(rad_peer(d), 4) != 3)
        def _():
            back_copy(d).wait_send()

        @pl.when(takes)
        def _():
            back_copy(d).wait_recv()

    @pl.when(takes)
    def _():
        own_back.wait()


def band_rows():
    off = iota((1, RADII), 1).astype(F32)
    inverse = (RADII * RADII) / (off + 0.5)
    last = off == RADII - 1
    lower = off * inverse
    upper = jnp.where(last, 0.0, (off + 1.0) * inverse)
    centre = -(off + (off + 1.0) * jnp.where(last, 2.0, 1.0)) * inverse
    radius = (off + 0.5) / RADII
    return lower, upper, centre, radius * radius


def solve_body(returned, known, keep, g_ref, nxt_out, forcing_out, rhs, work, nxt, forcing, sems):
    rad = lax.axis_index("rad")
    half = RADII // 2
    lane = lax.rem(rad, 8) * 128 + iota((8, 128), 1)
    m = jnp.where(lane <= HALF, lane, lane - HALF)
    sub = iota((8, 128), 0)
    most = jnp.where(
        sub % KL == 0, keep[0], jnp.where(sub % KL == 1, keep[1], jnp.where(sub % KL == 2, keep[2], keep[3]))
    )
    kept_here = m <= most
    top = sub < KL
    gain = time_step * gamma_rk
    scale = -implicit * RADII * RADII
    slope = jnp.where(top, 1.0, -1.0)
    outer_start = jnp.where(top, 0.0, scale * RADII)
    inner_start = jnp.where(top, scale, scale * (RADII - 1))

    def rows(q):
        return pl.ds(pl.multiple_of(q * 8, 8), 8)

    def weighed(j):
        return (jnp.where(top, 0.5, RADII - 0.5) + slope * j.astype(F32)) * g_ref[j]

    def fold(q, carry):
        sides = []
        for n in (q, half - 1 - q):
            kept = jnp.where(kept_here, returned[rows(n), :], 0.0)
            rhs[rows(n), :] = kept
            sides.append(known[rows(n), :] + gain * kept)
        work[2 * q] = jnp.where(top, sides[0], sides[1]) * weighed(2 * q)
        odd = pltpu.roll(jnp.where(top, sides[1], sides[0]), 4, 0)
        work[2 * q + 1] = odd * weighed(2 * q + 1)
        return carry

    def save(n, k, src, dst):
        return pltpu.make_async_copy(src.at[k], dst.at[k], sems.at[n, k])

    lax.fori_loop(0, half // 2, fold, 0, unroll=8)
    for k in range(KL):
        forcing[k] = jnp.transpose(rhs[pl.ds(k, RADII, stride=KL), :])
        save(0, k, forcing, forcing_out).start()

    def down(j, d):
        d = work[j] - ((outer_start + (scale * slope) * j.astype(F32)) * g_ref[j]) * d
        work[j] = d
        return d

    d = lax.fori_loop(0, half, down, jnp.zeros((8, 128), F32), unroll=16)

    def inner(j):
        return (inner_start + (scale * slope) * j.astype(F32)) * g_ref[j]

    v = inner(jnp.int32(half - 1))
    x = (d - v * pltpu.roll(d, 4, 0)) / (1.0 - v * pltpu.roll(v, 4, 0))
    work[half - 1] = x

    def back(n, x):
        j = half - 2 - n
        x = work[j] - inner(j) * x
        work[j] = x
        return x

    lax.fori_loop(0, half - 1, back, x, unroll=16)

    def unfold(q, carry):
        even = work[2 * q]
        odd = pltpu.roll(work[2 * q + 1], 4, 0)
        rhs[rows(q), :] = jnp.where(top, even, odd)
        rhs[rows(half - 1 - q), :] = jnp.where(top, odd, even)
        return carry

    lax.fori_loop(0, half // 2, unfold, 0, unroll=8)
    for k in range(KL):
        nxt[k] = jnp.transpose(rhs[pl.ds(k, RADII, stride=KL), :])
        save(1, k, nxt, nxt_out).start()
    for k in range(KL):
        save(0, k, forcing, forcing_out).wait()
        save(1, k, nxt, nxt_out).wait()


def vmem_call(body, outs, n_in, scratch, collective=None, smem=(), name=None, space=VMEM,
    out_space=None):
    spec = [
        pl.BlockSpec(memory_space=pltpu.SMEM if n in smem else space) for n in range(n_in)
    ]
    params = dict(vmem_limit_bytes=56 * 1024 * 1024)
    if collective is not None:
        params.update(collective_id=collective, has_side_effects=True)
    return pl.pallas_call(
        body,
        out_shape=[jax.ShapeDtypeStruct(s, F32) for s in outs],
        in_specs=spec,
        out_specs=[pl.BlockSpec(memory_space=out_space or space)] * len(outs),
        scratch_shapes=scratch,
        compiler_params=pltpu.CompilerParams(**params),
        name=name,
    )


DMA = pltpu.SemaphoreType.DMA


def per_device(
    field_coef,
    prior_forcing,
    base_flow,
    keep_modes,
    owner_band,
    cell_index,
    axial_pos,
    particle_vel,
    response_rate,
    particle_mass,
):
    high, low = fourier_half()
    table_hi, table_lo = jnp.asarray(high), jnp.asarray(low)

    def row(x):
        return x.reshape(1, P_DEV)

    all_rows = (RADS * ROWS, 128)
    tiles = (RADII // 2, 8, 128)
    slots = (MODES, RADS, CAP)
    returned, known, g = vmem_call(
        substep_body,
        [all_rows, all_rows, tiles],
        11,
        [
            VMEM(field_coef.shape, F32),
            VMEM(field_coef.shape, F32),
            VMEM(base_flow.shape, F32),
            VMEM((1, P_DEV), jnp.int32),
            VMEM((1, P_DEV), jnp.int32),
            VMEM((1, P_DEV), F32),
            VMEM((1, P_DEV), F32),
            VMEM((1, P_DEV), F32),
            VMEM((1, P_DEV), F32),
            VMEM(table_hi.shape, BF16),
            VMEM(table_hi.shape, BF16),
            VMEM(all_rows, F32),
            VMEM(tiles, F32),
            VMEM(all_rows, F32),
            VMEM(all_rows, F32),
            VMEM((RADS, 8, CAP), F32),
            VMEM((RADS, 8, CAP), F32),
            VMEM((MODES, 2 * RADS, CAP), F32),
            VMEM(tiles, F32),
            VMEM(tiles, F32),
            VMEM((MODES, BAND, ARC), F32),
            VMEM((MODES, 2 * ROWS, 128), F32),
            VMEM((MODES, 2 * ROWS, 128), F32),
            VMEM(all_rows, F32),
            VMEM((MODES, 256, RADS * CAP), BF16),
            VMEM((MODES, RADS, 8, CAP), F32),
            VMEM((2 * ROWS, RADS * CAP), BF16),
            VMEM((2, 4 * ROWS, HALF), BF16),
            VMEM(slots, F32),
            VMEM((4, RADS, CAP), F32),
            VMEM((4, RADS, CAP), F32),
            VMEM((4, RADS, CAP), F32),
            VMEM(slots, F32),
            DMA((11,)), DMA((3,)),
            DMA((RADS,)), DMA((RADS,)), DMA((RADS,)), DMA((RADS,)),
            DMA((MODES,)), DMA((MODES,)),
            DMA((4,)), DMA((4,)), DMA((4,)), DMA((4,)), DMA((4,)), DMA((4,)), DMA((4,)), DMA((4,)),
            DMA((RADS,)), DMA((RADS,)),
        ],
        collective=0,
        name="substep",
        space=pl.ANY,
    )(
        field_coef, prior_forcing, base_flow, row(owner_band), row(cell_index), row(axial_pos),
        row(particle_vel), row(response_rate), row(particle_mass), table_hi, table_lo,
    )
    field_next, forcing = vmem_call(
        solve_body,
        [(KL, 128, RADII), (KL, 128, RADII)],
        4,
        [
            VMEM(all_rows, F32),
            VMEM(tiles, F32),
            VMEM(field_coef.shape, F32),
            VMEM(field_coef.shape, F32),
            DMA((2, KL)),
        ],
        smem=(2,),
        name="solve",
        out_space=pl.ANY,
    )(returned, known, keep_modes, g)
    return (field_next, forcing)


def solution(mesh):
    in_specs = (
        P("mode", "rad", None),
        P("mode", "rad", None),
        P("rad", None),
        P("mode"),
        P(("mode", "rad"), None),
        P(("mode", "rad")),
        P(("mode", "rad")),
        P(("mode", "rad")),
        P(("mode", "rad")),
        P(("mode", "rad")),
    )
    out_specs = (P("mode", "rad", None), P("mode", "rad", None))
    return jax.shard_map(
        per_device, mesh=mesh, in_specs=in_specs, out_specs=out_specs, check_vma=False
    )
```

```python
import math

import jax
import jax.numpy as jnp
import ml_dtypes
import numpy as np
from jax import lax
from jax.experimental import pallas as pl
from jax.experimental.pallas import tpu as pltpu
from jax.sharding import PartitionSpec as P

time_step = 0.5
viscosity = 0.0004
alpha_rk = 1.0 / 15.0
beta_rk = 1.0 / 15.0
gamma_rk = 5.0 / 12.0
zeta_rk = -17.0 / 60.0

RADII = 384
AZIM = 1024
HALF = 512
KZ = 32
P_DEV = 2048
BAND = 24
ARC = 128
CAP = 256
MODES = 8
RADS = 16
KL = 4
ROWS = BAND * KL
F32 = jnp.float32
BF16 = jnp.bfloat16
MESH = pl.DeviceIdType.MESH
implicit = beta_rk * time_step * viscosity
VMEM = pltpu.VMEM


def fourier_half():
    i = np.arange(AZIM)
    m = np.where(i <= HALF, i, i - HALF)
    t = np.arange(HALF)
    angle = 2.0 * math.pi * ((t[None, :] * m[:, None]) % AZIM) / AZIM
    scale = np.where((m == 0) | (i == HALF), math.sqrt(1.0 / AZIM), math.sqrt(2.0 / AZIM))
    table = (np.where((i > HALF)[:, None], np.sin(angle), np.cos(angle)) * scale[:, None]).astype(
        np.float32
    )
    high = table.astype(ml_dtypes.bfloat16)
    low = (table - high.astype(np.float32)).astype(ml_dtypes.bfloat16)
    return high, low


def split(x):
    high = x.astype(BF16)
    return high, (x - high.astype(F32)).astype(BF16)


def mm(a, b):
    return lax.dot_general(a, b, (((1,), (0,)), ((), ())), preferred_element_type=F32)


def mm_nt(a, b):
    return lax.dot_general(a, b, (((1,), (1,)), ((), ())), preferred_element_type=F32)


def iota(shape, dim):
    return lax.broadcasted_iota(jnp.int32, shape, dim)


def greet(mode_peers, rad_peers):
    barrier = pltpu.get_barrier_semaphore()
    mode, rad = lax.axis_index("mode"), lax.axis_index("rad")
    if rad_peers:
        for d in NEAR[::-1]:
            there = lax.rem(rad // 4 + d // 4, 4) * 4 + lax.rem(lax.rem(rad, 4) + d % 4, 4)
            pl.semaphore_signal(barrier, inc=1, device_id=(mode, there), device_id_type=MESH)
    if mode_peers:
        for d in (4, 5, 3, 2, 6, 7, 1):
            pl.semaphore_signal(
                barrier, inc=1, device_id=(lax.rem(mode + d, MODES), rad), device_id_type=MESH
            )
    return barrier, (RADS - 1) * rad_peers + (MODES - 1) * mode_peers


def push_copy(src, dst, send, recv, mode, rad):
    return pltpu.make_async_remote_copy(
        src_ref=src,
        dst_ref=dst,
        send_sem=send,
        recv_sem=recv,
        device_id=(mode, rad),
        device_id_type=MESH,
    )


def radial_tiles(shape, dims):
    j = iota(shape, dims[0])
    sub = iota(shape, dims[1])
    return jnp.where(sub < 4, j, RADII - 1 - j), sub


def factor(mode, rad, diag_ref, edge_ref, g_ref):
    shape = (RADII // 2, 8, 128)
    r, sub = radial_tiles(shape, (0, 1))
    off = r.astype(F32)
    inverse = (RADII * RADII) / (off + 0.5)
    last = r == RADII - 1
    centre = -(off + (off + 1.0) * jnp.where(last, 2.0, 1.0)) * inverse
    k = mode * KL + sub % KL
    kappa = 0.5 + 1.5 * k.astype(F32) / KZ
    coef = lax.rem(rad, 8) * 128 + iota(shape, 2)
    m = jnp.where(coef <= HALF, coef, coef - HALF).astype(F32)
    unit = (off + 0.5) / RADII
    diagonal = centre - m * m / (unit * unit) - kappa * kappa
    diag_ref[...] = (1.0 - implicit * diagonal) * (off + 0.5)
    outer = (implicit * RADII * RADII) * jnp.where(sub < 4, off, off + 1.0)
    edge_ref[...] = outer * outer

    def step(j, g):
        g = 1.0 / (diag_ref[j] - edge_ref[j] * g)
        g_ref[j] = g
        return g

    lax.fori_loop(0, RADII // 2, step, jnp.zeros((8, 128), F32))


def dispatch(own, cell, pos, vel, rate, mass, fields_ref):
    owner = own[...]
    bands = iota((RADS, P_DEV), 0)
    match = (bands == owner).astype(F32)
    match_bf = match.astype(BF16)
    chunk = 256
    tri = (iota((chunk, chunk), 0) < iota((chunk, chunk), 1)).astype(F32).astype(BF16)
    running = jnp.zeros((RADS, 1), F32)
    places = []
    for n in range(P_DEV // chunk):
        part = match[:, n * chunk : (n + 1) * chunk]
        ahead = mm(match_bf[:, n * chunk : (n + 1) * chunk], tri) + running
        places.append(jnp.sum(ahead * part, axis=0, keepdims=True))
        running = running + jnp.sum(part, axis=1, keepdims=True)
    place = jnp.concatenate(places, axis=1).astype(jnp.int32)
    slots = (iota((CAP, P_DEV), 0) == place).astype(F32).astype(BF16)
    cells = cell[...]
    pieces = [(cells // ARC).astype(F32), (cells % ARC).astype(F32)]
    for ref in (pos, vel, rate, mass):
        left = ref[...]
        for _ in range(3):
            piece = left.astype(BF16).astype(F32)
            pieces.append(piece)
            left = left - piece
    rows = jnp.concatenate([jnp.where(match > 0.5, p, 0.0) for p in pieces], axis=0).astype(BF16)
    sorted_rows = mm_nt(rows, slots)

    def take(n):
        return sorted_rows[n * RADS : (n + 1) * RADS]

    fields_ref[:, 0, :] = take(0) * ARC + take(1)
    for f in range(4):
        fields_ref[:, 1 + f, :] = take(2 + 3 * f) + take(3 + 3 * f) + take(4 + 3 * f)
    for f in range(5, 8):
        fields_ref[:, f, :] = jnp.zeros((RADS, CAP), F32)


def cell_parts(cells):
    r = jnp.floor(cells * (1.0 / ARC))
    half = jnp.where(r >= BAND // 2, 1.0, 0.0)
    return cells + (half - r) * ARC, r - half * (BAND // 2)


QUARTER_HI = 1.57077026367187500
QUARTER_LO = math.pi / 2 - QUARTER_HI


def axial_tile(mode, positions):
    sub = iota((8, 1), 0)
    k = mode * KL + sub % KL
    kappa = 0.5 + 1.5 * k.astype(F32) / KZ
    phases = kappa * positions
    turns = jnp.floor(phases * (2.0 / math.pi) + 0.5)
    x = (phases - turns * QUARTER_HI) - turns * QUARTER_LO
    y = x * x
    sine = x + x * y * (-1.0 / 6 + y * (1.0 / 120 + y * (-1.0 / 5040 + y * (1.0 / 362880))))
    cosine = 1.0 + y * (-0.5 + y * (1.0 / 24 + y * (-1.0 / 720 + y * (1.0 / 40320))))
    quadrant = turns.astype(jnp.int32) + sub // KL
    scaling = 1.0 / math.sqrt(KZ)
    value = jnp.where((quadrant & 1) == 0, cosine, sine)
    return value * jnp.where(((quadrant + 1) & 2) == 0, scaling, -scaling)


HB = BAND // 2
EARLY = 10
NEAR = (1, 3, 4, 12, 2, 5, 7, 8, 13, 15, 6, 14, 9, 11, 10)


def known_side(mode, rad, field, prior, known):
    lower, upper, centre, radius_sq = band_rows()
    coef = lax.rem(rad, 8) * 128 + iota((128, 1), 0)
    m_col = jnp.where(coef <= HALF, coef, coef - HALF).astype(F32)
    wave = m_col * m_col / radius_sq
    for k in range(KL):
        kappa = 0.5 + 1.5 * (mode * KL + k).astype(F32) / KZ
        f = field[k]
        diagonal = centre - wave - kappa * kappa
        laplace = lower * pltpu.roll(f, 1, 1) + diagonal * f + upper * pltpu.roll(f, RADII - 1, 1)
        side = f + time_step * (alpha_rk * viscosity * laplace + zeta_rk * prior[k])
        known[pl.ds(k, RADII, stride=KL), :] = jnp.transpose(side)


def forward(pieces, table_hi, table_lo, grid):
    sign = jnp.where(iota((1, AZIM), 1) % 2 == 0, 1.0, -1.0)
    xs = []
    for c in range(2):
        xs.append(jnp.concatenate(
            [pieces[(c * 8 + ib) * ROWS : (c * 8 + ib + 1) * ROWS, :] for ib in range(8)], axis=1
        ).reshape(HB, 8, AZIM))
    top = iota((1, 8, 1), 1) < KL
    even = jnp.where(top, xs[0], pltpu.roll(xs[1], 4, 1))
    odd = jnp.where(top, pltpu.roll(xs[0], 4, 1), xs[1])
    x = jnp.stack([even, odd], axis=1).reshape(2 * ROWS, AZIM)
    hi, lo = split(jnp.concatenate([x, x * sign], axis=0))
    for n in range(2):
        cols = slice(n * 256, (n + 1) * 256)
        th, tl = table_hi[:, cols], table_lo[:, cols]
        out = mm(hi, th) + mm(lo, th) + mm(hi, tl)
        for half in range(2):
            for a in range(2):
                grid[half * 4 + n * 2 + a] = out[
                    half * 2 * ROWS : (half + 1) * 2 * ROWS, a * 128 : (a + 1) * 128
                ]


def sample_arc(m, grid, gathered, onehots, weights, partial):
    hi, lo = split(jnp.concatenate([grid[m, :ROWS, :], grid[m, ROWS:, :]], axis=1))
    lhs = jnp.concatenate([hi, lo], axis=0)
    for s in range(RADS):
        _, rh = cell_parts(gathered[m, s : s + 1, :])
        both = mm(lhs, onehots[m, :, s * CAP : (s + 1) * CAP])
        values = both[:ROWS] + both[ROWS:]
        taken = jnp.zeros((8, CAP), F32)
        for q in range(HB):
            taken = jnp.where(rh == q, values[q * 8 : (q + 1) * 8], taken)
        partial[m, s : s + 1, :] = jnp.sum(taken * weights[m, s], axis=0, keepdims=True)


def deposit_arc(m, gathered, onehots, weights, pushes, masses, terms):
    for s in range(RADS):
        _, rh = cell_parts(gathered[m, s : s + 1, :])
        value = pushes[m, s : s + 1, :] * weights[m, s]
        tile = jnp.concatenate(split(value), axis=0)
        place = jnp.broadcast_to(rh.astype(BF16), (16, CAP))
        masses[:, s * CAP : (s + 1) * CAP] = jnp.concatenate(
            [jnp.where(place == q, tile, jnp.zeros((), BF16)) for q in range(HB)], axis=0
        )
    both = mm_nt(masses[...], onehots[m]).reshape(HB, 2, 8, 256)
    deposit = (both[:, 0] + both[:, 1]).reshape(ROWS, 256)
    for h in range(2):
        rows = slice(h * ROWS, (h + 1) * ROWS)
        terms[m, rows, :] = terms[m, rows, :] + deposit[:, h * 128 : (h + 1) * 128]


def advect_arc(m, mode, grid, flow, terms):
    sub = iota((8, 1), 0)
    kappa = 0.5 + 1.5 * (mode * KL + sub % KL).astype(F32) / KZ
    kappa = jnp.where(sub < KL, kappa, -kappa)
    for r in range(BAND):
        rows = slice(r * 8, (r + 1) * 8)
        swapped = pltpu.roll(grid[m, rows, :], 4, 0)
        terms[m, rows, :] = kappa * flow[m, r : r + 1, :] * swapped


def substep_body(
    field_in, prior_in, base_in, own_in, cell_in, pos_in, vel_in, rate_in, mass_in, hi_in, lo_in,
    returned, known_out, g_out,
    field, prior, base, own, cell, pos, vel, rate, mass, table_hi, table_lo, known, g_ref,
    outgoing, pieces, fields, arrived, gathered, diag, edge, flow, grid, terms, spectral,
    onehots, weights, masses, splits, partial, twins, totals, parts, pushes, loads, stores,
    fsend, frecv, psend, precv, gsend, grecv, tsend, trecv, rsend, rrecv, asend, arecv, csend, crecv,
    bsend, brecv,
):
    mode, rad = lax.axis_index("mode"), lax.axis_index("rad")
    barrier, count = greet(True, True)
    given = [
        (own_in, own), (cell_in, cell), (pos_in, pos), (vel_in, vel), (rate_in, rate),
        (mass_in, mass), (field_in, field), (hi_in, table_hi), (lo_in, table_lo),
        (prior_in, prior), (base_in, base),
    ]
    given = [pltpu.make_async_copy(x, y, loads.at[n]) for n, (x, y) in enumerate(given)]
    for copy in given:
        copy.start()

    def rows(n):
        return pl.ds(pl.multiple_of(n * ROWS, 8), ROWS)

    x, y = rad // 4, lax.rem(rad, 4)
    z, core = mode // 2, lax.rem(mode, 2)
    twin = z * 2 + 1 - core

    def rad_peer(d):
        return lax.rem(x + d // 4, 4) * 4 + lax.rem(y + lax.rem(d, 4), 4)

    def mode_peer(d):
        return lax.rem(mode + d, MODES)

    def particle_copy(d):
        return push_copy(
            fields.at[rad_peer(d)], arrived.at[rad], psend.at[d], precv.at[d], mode, rad_peer(d)
        )

    def field_copy(d):
        return push_copy(
            outgoing.at[rows(rad_peer(d))], pieces.at[rows(rad)],
            fsend.at[d], frecv.at[d], mode, rad_peer(d),
        )

    def gather_copy(d):
        return push_copy(
            gathered.at[mode], gathered.at[mode], gsend.at[d], grecv.at[d], mode_peer(d), rad
        )

    def above(o):
        return lax.rem(z + o, 4) * 2 + core

    def twin_part(o):
        return push_copy(
            partial.at[lax.rem(z + o, 4) * 2 + 1 - core], twins.at[o],
            tsend.at[o], trecv.at[o], twin, rad,
        )

    def reduce_copy(o):
        return push_copy(
            totals.at[o], parts.at[o], rsend.at[o], rrecv.at[o], above(o), rad
        )

    def push_copy_above(o):
        return push_copy(
            pushes.at[mode], pushes.at[mode], asend.at[o], arecv.at[o], above(o), rad
        )

    def push_copy_twin(o):
        from_below = lax.rem(z - o + 4, 4) * 2 + core
        return push_copy(
            pushes.at[from_below], pushes.at[from_below], csend.at[o], crecv.at[o], twin, rad
        )

    def back_copy(d):
        return push_copy(
            spectral.at[rows(rad_peer(d))], returned.at[rows(rad)],
            bsend.at[d], brecv.at[d], mode, rad_peer(d),
        )

    for copy in given[:6]:
        copy.wait()
    dispatch(own, cell, pos, vel, rate, mass, fields)
    given[6].wait()
    for k in range(KL):
        outgoing[pl.ds(k, RADII, stride=KL), :] = jnp.transpose(field[k])
    pl.semaphore_wait(barrier, count)
    for d in NEAR[::-1]:
        particle_copy(d).start()
    for d in NEAR[:EARLY]:
        field_copy(d).start()
    arrived[rad] = fields[rad]
    pieces[rows(rad), :] = outgoing[rows(rad), :]
    for copy in given[7:]:
        copy.wait()
    known_side(mode, rad, field, prior, known)
    for d in NEAR:
        particle_copy(d).wait_recv()
    gathered[mode, 0:RADS, :] = arrived[:, 0, :]
    gathered[mode, RADS : 2 * RADS, :] = arrived[:, 1, :]
    for d in (4, 3, 5, 2, 6, 1, 7):
        gather_copy(d).start()
    for d in NEAR[EARLY:]:
        field_copy(d).start()
    factor(mode, rad, diag, edge, g_ref)
    kept = [
        pltpu.make_async_copy(known, known_out, stores.at[0]),
        pltpu.make_async_copy(g_ref, g_out, stores.at[1]),
    ]
    for copy in kept:
        copy.start()
    for a in range(MODES):
        flow[a] = base[:, a * ARC : (a + 1) * ARC]

    def prepare(d, carry):
        @pl.when(d > 0)
        def _():
            gather_copy(MODES - d).wait_recv()

        m = mode_peer(d)
        for s in range(RADS):
            column, _ = cell_parts(gathered[m, s : s + 1, :])
            index = iota((256, CAP), 0).astype(F32).astype(BF16)
            onehots[m, :, s * CAP : (s + 1) * CAP] = jnp.where(
                index == column.astype(BF16), jnp.ones((), BF16), jnp.zeros((), BF16)
            )
            weights[m, s] = axial_tile(mode, gathered[m, RADS + s : RADS + s + 1, :])
        return carry

    lax.fori_loop(0, MODES, prepare, 0)
    for d in range(1, RADS):
        field_copy(d).wait_recv()
    forward(pieces, table_hi, table_lo, grid)

    def outward(n):
        t = lax.rem(n + 2, 4)
        return t + (n // 2) * (1 - 2 * t)

    def sample(n, carry):
        mine = jnp.where((n == 2) | (n == 4) | (n == 5) | (n == 7), 1, 0)
        late = jnp.where(n > 2, 1, 0) + jnp.where(n > 4, 1, 0) + jnp.where(n > 5, 1, 0)
        o = outward(mine * late + (1 - mine) * (n - late))
        m = lax.rem(z + o, 4) * 2 + lax.rem(core + 1 - mine, 2)
        sample_arc(m, grid, gathered, onehots, weights, partial)

        @pl.when(mine == 0)
        def _():
            twin_part(o).start()

        @pl.when(mine == 1)
        def _():
            twin_part(o).wait_recv()
            totals[o] = partial[m] + twins[o]

            @pl.when(o > 0)
            def _():
                reduce_copy(o).start()

        return carry

    def advect(m, carry):
        advect_arc(m, mode, grid, flow, terms)
        return carry

    lax.fori_loop(0, MODES, sample, 0)
    lax.fori_loop(0, MODES, advect, 0)
    for o in (1, 3, 2):
        reduce_copy(o).wait_recv()
    fluid = (totals[0] + parts[1]) + (parts[2] + parts[3])
    relative = (fluid - arrived[:, 2, :]) * arrived[:, 3, :]
    pushes[mode] = -arrived[:, 4, :] * relative
    for o in (2, 3, 1):
        push_copy_above(o).start()
    push_copy_twin(0).start()

    def arrive(o):
        push_copy_above(o).wait_recv()
        push_copy_twin(o).start()

    def place(n, carry):
        j = jnp.where(n < 2, 0, lax.rem(n - 2, 3) + 1)
        o = j + (j // 2) * (5 - 2 * j)
        b = jnp.where((n == 1) | (n > 4), 1, 0)

        @pl.when(n == 2)
        def _():
            arrive(1)
            arrive(3)

        @pl.when(n == 3)
        def _():
            arrive(2)

        @pl.when(b == 1)
        def _():
            push_copy_twin(o).wait_recv()

        m = lax.rem(z - o + 4, 4) * 2 + lax.rem(core + b, 2)
        deposit_arc(m, gathered, onehots, weights, pushes, masses, terms)
        return carry

    lax.fori_loop(0, MODES, place, 0)
    first = jnp.concatenate([terms[a] for a in range(4)], axis=1)
    second = jnp.concatenate([terms[a + 4] for a in range(4)], axis=1)
    hi, lo = split(jnp.concatenate([first + second, first - second], axis=0))
    splits[0] = hi
    splits[1] = lo
    parity = iota((1, 128), 1) % 2 == 0
    top = iota((1, 8, 1), 1) < KL

    def inverse(n, carry):
        line = lax.rem(y + n // 2 + 0, 4)

        @pl.when(line != 3)
        def _():
            ib = lax.rem(x + n, 2) * 4 + line
            block = pl.ds(pl.multiple_of(ib * 128, 128), 128)
            th, tl = table_hi[block, :], table_lo[block, :]
            out = mm_nt(splits[0], th) + mm_nt(splits[1], th) + mm_nt(splits[0], tl)
            chosen = jnp.where(parity, out[: 2 * ROWS], out[2 * ROWS :]).reshape(HB, 2, 8, 128)
            even, odd = chosen[:, 0], chosen[:, 1]
            real = jnp.where(top, even, pltpu.roll(odd, 4, 1))
            imag = jnp.where(top, pltpu.roll(even, 4, 1), odd)
            spectral[rows(ib), :] = real.reshape(ROWS, 128)
            spectral[rows(8 + ib), :] = imag.reshape(ROWS, 128)
            for c in range(2):
                dx = lax.rem(2 * c + ib // 4 - x + 4, 4)
                d = dx * 4 + lax.rem(line - y + 4, 4)

                @pl.when(d > 0)
                def _():
                    back_copy(d).start()

                @pl.when(d == 0)
                def _():
                    own_back.start()

        return carry

    own_back = pltpu.make_async_copy(
        spectral.at[rows(rad)], returned.at[rows(rad)], stores.at[2]
    )
    lax.fori_loop(0, 8, inverse, 0)
    takes = lax.rem(rad, 4) != 3
    for copy in kept:
        copy.wait()
    for d in range(1, RADS):
        particle_copy(d).wait_send()
        field_copy(d).wait_send()
    for d in range(1, MODES):
        gather_copy(d).wait_send()
    for o in range(4):
        twin_part(o).wait_send()
        push_copy_twin(o).wait_send()
        if o:
            reduce_copy(o).wait_send()
            push_copy_above(o).wait_send()
    for d in range(1, RADS):
        @pl.when(lax.rem(rad_peer(d), 4) != 3)
        def _():
            back_copy(d).wait_send()

        @pl.when(takes)
        def _():
            back_copy(d).wait_recv()

    @pl.when(takes)
    def _():
        own_back.wait()


def band_rows():
    off = iota((1, RADII), 1).astype(F32)
    inverse = (RADII * RADII) / (off + 0.5)
    last = off == RADII - 1
    lower = off * inverse
    upper = jnp.where(last, 0.0, (off + 1.0) * inverse)
    centre = -(off + (off + 1.0) * jnp.where(last, 2.0, 1.0)) * inverse
    radius = (off + 0.5) / RADII
    return lower, upper, centre, radius * radius


def solve_body(returned, known, keep, g_ref, nxt_out, forcing_out, rhs, work, nxt, forcing, sems):
    rad = lax.axis_index("rad")
    half = RADII // 2
    lane = lax.rem(rad, 8) * 128 + iota((8, 128), 1)
    m = jnp.where(lane <= HALF, lane, lane - HALF)
    sub = iota((8, 128), 0)
    most = jnp.where(
        sub % KL == 0, keep[0], jnp.where(sub % KL == 1, keep[1], jnp.where(sub % KL == 2, keep[2], keep[3]))
    )
    kept_here = m <= most
    top = sub < KL
    gain = time_step * gamma_rk
    scale = -implicit * RADII * RADII
    slope = jnp.where(top, 1.0, -1.0)
    outer_start = jnp.where(top, 0.0, scale * RADII)
    inner_start = jnp.where(top, scale, scale * (RADII - 1))

    def rows(q):
        return pl.ds(pl.multiple_of(q * 8, 8), 8)

    def weighed(j):
        return (jnp.where(top, 0.5, RADII - 0.5) + slope * j.astype(F32)) * g_ref[j]

    def fold(q, carry):
        sides = []
        for n in (q, half - 1 - q):
            kept = jnp.where(kept_here, returned[rows(n), :], 0.0)
            rhs[rows(n), :] = kept
            sides.append(known[rows(n), :] + gain * kept)
        work[2 * q] = jnp.where(top, sides[0], sides[1]) * weighed(2 * q)
        odd = pltpu.roll(jnp.where(top, sides[1], sides[0]), 4, 0)
        work[2 * q + 1] = odd * weighed(2 * q + 1)
        return carry

    def save(n, k, src, dst):
        return pltpu.make_async_copy(src.at[k], dst.at[k], sems.at[n, k])

    lax.fori_loop(0, half // 2, fold, 0, unroll=8)
    for k in range(KL):
        forcing[k] = jnp.transpose(rhs[pl.ds(k, RADII, stride=KL), :])
        save(0, k, forcing, forcing_out).start()

    def down(j, d):
        d = work[j] - ((outer_start + (scale * slope) * j.astype(F32)) * g_ref[j]) * d
        work[j] = d
        return d

    d = lax.fori_loop(0, half, down, jnp.zeros((8, 128), F32), unroll=16)

    def inner(j):
        return (inner_start + (scale * slope) * j.astype(F32)) * g_ref[j]

    v = inner(jnp.int32(half - 1))
    x = (d - v * pltpu.roll(d, 4, 0)) / (1.0 - v * pltpu.roll(v, 4, 0))
    work[half - 1] = x

    def back(n, x):
        j = half - 2 - n
        x = work[j] - inner(j) * x
        work[j] = x
        return x

    lax.fori_loop(0, half - 1, back, x, unroll=16)

    def unfold(q, carry):
        even = work[2 * q]
        odd = pltpu.roll(work[2 * q + 1], 4, 0)
        rhs[rows(q), :] = jnp.where(top, even, odd)
        rhs[rows(half - 1 - q), :] = jnp.where(top, odd, even)
        return carry

    lax.fori_loop(0, half // 2, unfold, 0, unroll=8)
    for k in range(KL):
        nxt[k] = jnp.transpose(rhs[pl.ds(k, RADII, stride=KL), :])
        save(1, k, nxt, nxt_out).start()
    for k in range(KL):
        save(0, k, forcing, forcing_out).wait()
        save(1, k, nxt, nxt_out).wait()


def vmem_call(body, outs, n_in, scratch, collective=None, smem=(), name=None, space=VMEM,
    out_space=None):
    spec = [
        pl.BlockSpec(memory_space=pltpu.SMEM if n in smem else space) for n in range(n_in)
    ]
    params = dict(vmem_limit_bytes=56 * 1024 * 1024)
    if collective is not None:
        params.update(collective_id=collective, has_side_effects=True)
    return pl.pallas_call(
        body,
        out_shape=[jax.ShapeDtypeStruct(s, F32) for s in outs],
        in_specs=spec,
        out_specs=[pl.BlockSpec(memory_space=out_space or space)] * len(outs),
        scratch_shapes=scratch,
        compiler_params=pltpu.CompilerParams(**params),
        name=name,
    )


DMA = pltpu.SemaphoreType.DMA


def per_device(
    field_coef,
    prior_forcing,
    base_flow,
    keep_modes,
    owner_band,
    cell_index,
    axial_pos,
    particle_vel,
    response_rate,
    particle_mass,
):
    high, low = fourier_half()
    table_hi, table_lo = jnp.asarray(high), jnp.asarray(low)

    def row(x):
        return x.reshape(1, P_DEV)

    all_rows = (RADS * ROWS, 128)
    tiles = (RADII // 2, 8, 128)
    slots = (MODES, RADS, CAP)
    returned, known, g = vmem_call(
        substep_body,
        [all_rows, all_rows, tiles],
        11,
        [
            VMEM(field_coef.shape, F32),
            VMEM(field_coef.shape, F32),
            VMEM(base_flow.shape, F32),
            VMEM((1, P_DEV), jnp.int32),
            VMEM((1, P_DEV), jnp.int32),
            VMEM((1, P_DEV), F32),
            VMEM((1, P_DEV), F32),
            VMEM((1, P_DEV), F32),
            VMEM((1, P_DEV), F32),
            VMEM(table_hi.shape, BF16),
            VMEM(table_hi.shape, BF16),
            VMEM(all_rows, F32),
            VMEM(tiles, F32),
            VMEM(all_rows, F32),
            VMEM(all_rows, F32),
            VMEM((RADS, 8, CAP), F32),
            VMEM((RADS, 8, CAP), F32),
            VMEM((MODES, 2 * RADS, CAP), F32),
            VMEM(tiles, F32),
            VMEM(tiles, F32),
            VMEM((MODES, BAND, ARC), F32),
            VMEM((MODES, 2 * ROWS, 128), F32),
            VMEM((MODES, 2 * ROWS, 128), F32),
            VMEM(all_rows, F32),
            VMEM((MODES, 256, RADS * CAP), BF16),
            VMEM((MODES, RADS, 8, CAP), F32),
            VMEM((2 * ROWS, RADS * CAP), BF16),
            VMEM((2, 4 * ROWS, HALF), BF16),
            VMEM(slots, F32),
            VMEM((4, RADS, CAP), F32),
            VMEM((4, RADS, CAP), F32),
            VMEM((4, RADS, CAP), F32),
            VMEM(slots, F32),
            DMA((11,)), DMA((3,)),
            DMA((RADS,)), DMA((RADS,)), DMA((RADS,)), DMA((RADS,)),
            DMA((MODES,)), DMA((MODES,)),
            DMA((4,)), DMA((4,)), DMA((4,)), DMA((4,)), DMA((4,)), DMA((4,)), DMA((4,)), DMA((4,)),
            DMA((RADS,)), DMA((RADS,)),
        ],
        collective=0,
        name="substep",
        space=pl.ANY,
    )(
        field_coef, prior_forcing, base_flow, row(owner_band), row(cell_index), row(axial_pos),
        row(particle_vel), row(response_rate), row(particle_mass), table_hi, table_lo,
    )
    field_next, forcing = vmem_call(
        solve_body,
        [(KL, 128, RADII), (KL, 128, RADII)],
        4,
        [
            VMEM(all_rows, F32),
            VMEM(tiles, F32),
            VMEM(field_coef.shape, F32),
            VMEM(field_coef.shape, F32),
            DMA((2, KL)),
        ],
        smem=(2,),
        name="solve",
        out_space=pl.ANY,
    )(returned, known, keep_modes, g)
    return (field_next, forcing)


def solution(mesh):
    in_specs = (
        P("mode", "rad", None),
        P("mode", "rad", None),
        P("rad", None),
        P("mode"),
        P(("mode", "rad"), None),
        P(("mode", "rad")),
        P(("mode", "rad")),
        P(("mode", "rad")),
        P(("mode", "rad")),
        P(("mode", "rad")),
    )
    out_specs = (P("mode", "rad", None), P("mode", "rad", None))
    return jax.shard_map(
        per_device, mesh=mesh, in_specs=in_specs, out_specs=out_specs, check_vma=False
    )
```

```python
import math

import jax
import jax.numpy as jnp
import ml_dtypes
import numpy as np
from jax import lax
from jax.experimental import pallas as pl
from jax.experimental.pallas import tpu as pltpu
from jax.sharding import PartitionSpec as P

time_step = 0.5
viscosity = 0.0004
alpha_rk = 1.0 / 15.0
beta_rk = 1.0 / 15.0
gamma_rk = 5.0 / 12.0
zeta_rk = -17.0 / 60.0

RADII = 384
AZIM = 1024
HALF = 512
KZ = 32
P_DEV = 2048
BAND = 24
ARC = 128
CAP = 256
MODES = 8
RADS = 16
KL = 4
ROWS = BAND * KL
F32 = jnp.float32
BF16 = jnp.bfloat16
MESH = pl.DeviceIdType.MESH
implicit = beta_rk * time_step * viscosity
VMEM = pltpu.VMEM


def fourier_half():
    i = np.arange(AZIM)
    m = np.where(i <= HALF, i, i - HALF)
    t = np.arange(HALF)
    angle = 2.0 * math.pi * ((t[None, :] * m[:, None]) % AZIM) / AZIM
    scale = np.where((m == 0) | (i == HALF), math.sqrt(1.0 / AZIM), math.sqrt(2.0 / AZIM))
    table = (np.where((i > HALF)[:, None], np.sin(angle), np.cos(angle)) * scale[:, None]).astype(
        np.float32
    )
    high = table.astype(ml_dtypes.bfloat16)
    low = (table - high.astype(np.float32)).astype(ml_dtypes.bfloat16)
    return high, low


def split(x):
    high = x.astype(BF16)
    return high, (x - high.astype(F32)).astype(BF16)


def mm(a, b):
    return lax.dot_general(a, b, (((1,), (0,)), ((), ())), preferred_element_type=F32)


def mm_nt(a, b):
    return lax.dot_general(a, b, (((1,), (1,)), ((), ())), preferred_element_type=F32)


def iota(shape, dim):
    return lax.broadcasted_iota(jnp.int32, shape, dim)


def greet(mode_peers, rad_peers):
    barrier = pltpu.get_barrier_semaphore()
    mode, rad = lax.axis_index("mode"), lax.axis_index("rad")
    if rad_peers:
        for d in NEAR[::-1]:
            there = lax.rem(rad // 4 + d // 4, 4) * 4 + lax.rem(lax.rem(rad, 4) + d % 4, 4)
            pl.semaphore_signal(barrier, inc=1, device_id=(mode, there), device_id_type=MESH)
    if mode_peers:
        for d in (4, 5, 3, 2, 6, 7, 1):
            pl.semaphore_signal(
                barrier, inc=1, device_id=(lax.rem(mode + d, MODES), rad), device_id_type=MESH
            )
    return barrier, (RADS - 1) * rad_peers + (MODES - 1) * mode_peers


def push_copy(src, dst, send, recv, mode, rad):
    return pltpu.make_async_remote_copy(
        src_ref=src,
        dst_ref=dst,
        send_sem=send,
        recv_sem=recv,
        device_id=(mode, rad),
        device_id_type=MESH,
    )


def radial_tiles(shape, dims):
    j = iota(shape, dims[0])
    sub = iota(shape, dims[1])
    return jnp.where(sub < 4, j, RADII - 1 - j), sub


def factor(mode, rad, diag_ref, edge_ref, g_ref):
    shape = (RADII // 2, 8, 128)
    r, sub = radial_tiles(shape, (0, 1))
    off = r.astype(F32)
    inverse = (RADII * RADII) / (off + 0.5)
    last = r == RADII - 1
    centre = -(off + (off + 1.0) * jnp.where(last, 2.0, 1.0)) * inverse
    k = mode * KL + sub % KL
    kappa = 0.5 + 1.5 * k.astype(F32) / KZ
    coef = lax.rem(rad, 8) * 128 + iota(shape, 2)
    m = jnp.where(coef <= HALF, coef, coef - HALF).astype(F32)
    unit = (off + 0.5) / RADII
    diagonal = centre - m * m / (unit * unit) - kappa * kappa
    diag_ref[...] = (1.0 - implicit * diagonal) * (off + 0.5)
    outer = (implicit * RADII * RADII) * jnp.where(sub < 4, off, off + 1.0)
    edge_ref[...] = outer * outer

    def step(j, g):
        g = 1.0 / (diag_ref[j] - edge_ref[j] * g)
        g_ref[j] = g
        return g

    lax.fori_loop(0, RADII // 2, step, jnp.zeros((8, 128), F32))


def dispatch(own, cell, pos, vel, rate, mass, fields_ref):
    owner = own[...]
    bands = iota((RADS, P_DEV), 0)
    match = (bands == owner).astype(F32)
    match_bf = match.astype(BF16)
    chunk = 256
    tri = (iota((chunk, chunk), 0) < iota((chunk, chunk), 1)).astype(F32).astype(BF16)
    running = jnp.zeros((RADS, 1), F32)
    places = []
    for n in range(P_DEV // chunk):
        part = match[:, n * chunk : (n + 1) * chunk]
        ahead = mm(match_bf[:, n * chunk : (n + 1) * chunk], tri) + running
        places.append(jnp.sum(ahead * part, axis=0, keepdims=True))
        running = running + jnp.sum(part, axis=1, keepdims=True)
    place = jnp.concatenate(places, axis=1).astype(jnp.int32)
    slots = (iota((CAP, P_DEV), 0) == place).astype(F32).astype(BF16)
    cells = cell[...]
    pieces = [(cells // ARC).astype(F32), (cells % ARC).astype(F32)]
    for ref in (pos, vel, rate, mass):
        left = ref[...]
        for _ in range(3):
            piece = left.astype(BF16).astype(F32)
            pieces.append(piece)
            left = left - piece
    rows = jnp.concatenate([jnp.where(match > 0.5, p, 0.0) for p in pieces], axis=0).astype(BF16)
    sorted_rows = mm_nt(rows, slots)

    def take(n):
        return sorted_rows[n * RADS : (n + 1) * RADS]

    fields_ref[:, 0, :] = take(0) * ARC + take(1)
    for f in range(4):
        fields_ref[:, 1 + f, :] = take(2 + 3 * f) + take(3 + 3 * f) + take(4 + 3 * f)
    for f in range(5, 8):
        fields_ref[:, f, :] = jnp.zeros((RADS, CAP), F32)


def cell_parts(cells):
    r = jnp.floor(cells * (1.0 / ARC))
    half = jnp.where(r >= BAND // 2, 1.0, 0.0)
    return cells + (half - r) * ARC, r - half * (BAND // 2)


QUARTER_HI = 1.57077026367187500
QUARTER_LO = math.pi / 2 - QUARTER_HI


def axial_tile(mode, positions):
    sub = iota((8, 1), 0)
    k = mode * KL + sub % KL
    kappa = 0.5 + 1.5 * k.astype(F32) / KZ
    phases = kappa * positions
    turns = jnp.floor(phases * (2.0 / math.pi) + 0.5)
    x = (phases - turns * QUARTER_HI) - turns * QUARTER_LO
    y = x * x
    sine = x + x * y * (-1.0 / 6 + y * (1.0 / 120 + y * (-1.0 / 5040 + y * (1.0 / 362880))))
    cosine = 1.0 + y * (-0.5 + y * (1.0 / 24 + y * (-1.0 / 720 + y * (1.0 / 40320))))
    quadrant = turns.astype(jnp.int32) + sub // KL
    scaling = 1.0 / math.sqrt(KZ)
    value = jnp.where((quadrant & 1) == 0, cosine, sine)
    return value * jnp.where(((quadrant + 1) & 2) == 0, scaling, -scaling)


HB = BAND // 2
EARLY = 10
NEAR = (1, 3, 4, 12, 2, 5, 7, 8, 13, 15, 6, 14, 9, 11, 10)


def known_side(mode, rad, field, prior, known):
    lower, upper, centre, radius_sq = band_rows()
    coef = lax.rem(rad, 8) * 128 + iota((128, 1), 0)
    m_col = jnp.where(coef <= HALF, coef, coef - HALF).astype(F32)
    wave = m_col * m_col / radius_sq
    for k in range(KL):
        kappa = 0.5 + 1.5 * (mode * KL + k).astype(F32) / KZ
        f = field[k]
        diagonal = centre - wave - kappa * kappa
        laplace = lower * pltpu.roll(f, 1, 1) + diagonal * f + upper * pltpu.roll(f, RADII - 1, 1)
        side = f + time_step * (alpha_rk * viscosity * laplace + zeta_rk * prior[k])
        known[pl.ds(k, RADII, stride=KL), :] = jnp.transpose(side)


def forward(pieces, table_hi, table_lo, grid):
    sign = jnp.where(iota((1, AZIM), 1) % 2 == 0, 1.0, -1.0)
    xs = []
    for c in range(2):
        xs.append(jnp.concatenate(
            [pieces[(c * 8 + ib) * ROWS : (c * 8 + ib + 1) * ROWS, :] for ib in range(8)], axis=1
        ).reshape(HB, 8, AZIM))
    top = iota((1, 8, 1), 1) < KL
    even = jnp.where(top, xs[0], pltpu.roll(xs[1], 4, 1))
    odd = jnp.where(top, pltpu.roll(xs[0], 4, 1), xs[1])
    x = jnp.stack([even, odd], axis=1).reshape(2 * ROWS, AZIM)
    hi, lo = split(jnp.concatenate([x, x * sign], axis=0))
    for n in range(2):
        cols = slice(n * 256, (n + 1) * 256)
        th, tl = table_hi[:, cols], table_lo[:, cols]
        out = mm(hi, th) + mm(lo, th) + mm(hi, tl)
        for half in range(2):
            for a in range(2):
                grid[half * 4 + n * 2 + a] = out[
                    half * 2 * ROWS : (half + 1) * 2 * ROWS, a * 128 : (a + 1) * 128
                ]


def sample_arc(m, grid, gathered, onehots, weights, partial):
    hi, lo = split(jnp.concatenate([grid[m, :ROWS, :], grid[m, ROWS:, :]], axis=1))
    lhs = jnp.concatenate([hi, lo], axis=0)
    for s in range(RADS):
        _, rh = cell_parts(gathered[m, s : s + 1, :])
        both = mm(lhs, onehots[m, :, s * CAP : (s + 1) * CAP])
        values = both[:ROWS] + both[ROWS:]
        taken = jnp.zeros((8, CAP), F32)
        for q in range(HB):
            taken = jnp.where(rh == q, values[q * 8 : (q + 1) * 8], taken)
        partial[m, s : s + 1, :] = jnp.sum(taken * weights[m, s], axis=0, keepdims=True)


def deposit_arc(m, gathered, onehots, weights, pushes, masses, terms):
    for s in range(RADS):
        _, rh = cell_parts(gathered[m, s : s + 1, :])
        value = pushes[m, s : s + 1, :] * weights[m, s]
        tile = jnp.concatenate(split(value), axis=0)
        place = jnp.broadcast_to(rh.astype(BF16), (16, CAP))
        masses[:, s * CAP : (s + 1) * CAP] = jnp.concatenate(
            [jnp.where(place == q, tile, jnp.zeros((), BF16)) for q in range(HB)], axis=0
        )
    both = mm_nt(masses[...], onehots[m]).reshape(HB, 2, 8, 256)
    deposit = (both[:, 0] + both[:, 1]).reshape(ROWS, 256)
    for h in range(2):
        rows = slice(h * ROWS, (h + 1) * ROWS)
        terms[m, rows, :] = terms[m, rows, :] + deposit[:, h * 128 : (h + 1) * 128]


def advect_arc(m, mode, grid, flow, terms):
    sub = iota((8, 1), 0)
    kappa = 0.5 + 1.5 * (mode * KL + sub % KL).astype(F32) / KZ
    kappa = jnp.where(sub < KL, kappa, -kappa)
    for r in range(BAND):
        rows = slice(r * 8, (r + 1) * 8)
        swapped = pltpu.roll(grid[m, rows, :], 4, 0)
        terms[m, rows, :] = kappa * flow[m, r : r + 1, :] * swapped


def substep_body(
    field_in, prior_in, base_in, own_in, cell_in, pos_in, vel_in, rate_in, mass_in, hi_in, lo_in,
    returned, known_out, g_out,
    field, prior, base, own, cell, pos, vel, rate, mass, table_hi, table_lo, known, g_ref,
    outgoing, pieces, fields, arrived, gathered, diag, edge, flow, grid, terms, spectral,
    onehots, weights, masses, splits, partial, twins, totals, parts, pushes, loads, stores,
    fsend, frecv, psend, precv, gsend, grecv, tsend, trecv, rsend, rrecv, asend, arecv, csend, crecv,
    bsend, brecv,
):
    mode, rad = lax.axis_index("mode"), lax.axis_index("rad")
    barrier, count = greet(True, True)
    given = [
        (own_in, own), (cell_in, cell), (pos_in, pos), (vel_in, vel), (rate_in, rate),
        (mass_in, mass), (field_in, field), (hi_in, table_hi), (lo_in, table_lo),
        (prior_in, prior), (base_in, base),
    ]
    given = [pltpu.make_async_copy(x, y, loads.at[n]) for n, (x, y) in enumerate(given)]
    for copy in given:
        copy.start()

    def rows(n):
        return pl.ds(pl.multiple_of(n * ROWS, 8), ROWS)

    x, y = rad // 4, lax.rem(rad, 4)
    z, core = mode // 2, lax.rem(mode, 2)
    twin = z * 2 + 1 - core

    def rad_peer(d):
        return lax.rem(x + d // 4, 4) * 4 + lax.rem(y + lax.rem(d, 4), 4)

    def mode_peer(d):
        return lax.rem(mode + d, MODES)

    def particle_copy(d):
        return push_copy(
            fields.at[rad_peer(d)], arrived.at[rad], psend.at[d], precv.at[d], mode, rad_peer(d)
        )

    def field_copy(d):
        return push_copy(
            outgoing.at[rows(rad_peer(d))], pieces.at[rows(rad)],
            fsend.at[d], frecv.at[d], mode, rad_peer(d),
        )

    def gather_copy(d):
        return push_copy(
            gathered.at[mode], gathered.at[mode], gsend.at[d], grecv.at[d], mode_peer(d), rad
        )

    def above(o):
        return lax.rem(z + o, 4) * 2 + core

    def twin_part(o):
        return push_copy(
            partial.at[lax.rem(z + o, 4) * 2 + 1 - core], twins.at[o],
            tsend.at[o], trecv.at[o], twin, rad,
        )

    def reduce_copy(o):
        return push_copy(
            totals.at[o], parts.at[o], rsend.at[o], rrecv.at[o], above(o), rad
        )

    def push_copy_above(o):
        return push_copy(
            pushes.at[mode], pushes.at[mode], asend.at[o], arecv.at[o], above(o), rad
        )

    def push_copy_twin(o):
        from_below = lax.rem(z - o + 4, 4) * 2 + core
        return push_copy(
            pushes.at[from_below], pushes.at[from_below], csend.at[o], crecv.at[o], twin, rad
        )

    def back_copy(d):
        return push_copy(
            spectral.at[rows(rad_peer(d))], returned.at[rows(rad)],
            bsend.at[d], brecv.at[d], mode, rad_peer(d),
        )

    for copy in given[:6]:
        copy.wait()
    dispatch(own, cell, pos, vel, rate, mass, fields)
    given[6].wait()
    for k in range(KL):
        outgoing[pl.ds(k, RADII, stride=KL), :] = jnp.transpose(field[k])
    pl.semaphore_wait(barrier, count)
    for d in NEAR[::-1]:
        particle_copy(d).start()
    for d in NEAR[:EARLY]:
        field_copy(d).start()
    arrived[rad] = fields[rad]
    pieces[rows(rad), :] = outgoing[rows(rad), :]
    for copy in given[7:]:
        copy.wait()
    known_side(mode, rad, field, prior, known)
    for d in NEAR:
        particle_copy(d).wait_recv()
    gathered[mode, 0:RADS, :] = arrived[:, 0, :]
    gathered[mode, RADS : 2 * RADS, :] = arrived[:, 1, :]
    for d in (4, 3, 5, 2, 6, 1, 7):
        gather_copy(d).start()
    for d in NEAR[EARLY:]:
        field_copy(d).start()
    factor(mode, rad, diag, edge, g_ref)
    kept = [
        pltpu.make_async_copy(known, known_out, stores.at[0]),
        pltpu.make_async_copy(g_ref, g_out, stores.at[1]),
    ]
    for copy in kept:
        copy.start()
    for a in range(MODES):
        flow[a] = base[:, a * ARC : (a + 1) * ARC]

    def prepare(d, carry):
        @pl.when(d > 0)
        def _():
            gather_copy(MODES - d).wait_recv()

        m = mode_peer(d)
        for s in range(RADS):
            column, _ = cell_parts(gathered[m, s : s + 1, :])
            index = iota((256, CAP), 0).astype(F32).astype(BF16)
            onehots[m, :, s * CAP : (s + 1) * CAP] = jnp.where(
                index == column.astype(BF16), jnp.ones((), BF16), jnp.zeros((), BF16)
            )
            weights[m, s] = axial_tile(mode, gathered[m, RADS + s : RADS + s + 1, :])
        return carry

    lax.fori_loop(0, MODES, prepare, 0)
    for d in range(1, RADS):
        field_copy(d).wait_recv()
    forward(pieces, table_hi, table_lo, grid)

    def outward(n):
        t = lax.rem(n + 2, 4)
        return t + (n // 2) * (1 - 2 * t)

    def sample(n, carry):
        mine = jnp.where((n == 2) | (n == 4) | (n == 5) | (n == 7), 1, 0)
        late = jnp.where(n > 2, 1, 0) + jnp.where(n > 4, 1, 0) + jnp.where(n > 5, 1, 0)
        o = outward(mine * late + (1 - mine) * (n - late))
        m = lax.rem(z + o, 4) * 2 + lax.rem(core + 1 - mine, 2)
        sample_arc(m, grid, gathered, onehots, weights, partial)

        @pl.when(mine == 0)
        def _():
            twin_part(o).start()

        @pl.when(mine == 1)
        def _():
            twin_part(o).wait_recv()
            totals[o] = partial[m] + twins[o]

            @pl.when(o > 0)
            def _():
                reduce_copy(o).start()

        return carry

    def advect(m, carry):
        advect_arc(m, mode, grid, flow, terms)
        return carry

    lax.fori_loop(0, MODES, sample, 0)
    lax.fori_loop(0, MODES // 2, advect, 0)
    for o in (1, 3, 2):
        reduce_copy(o).wait_recv()
    fluid = (totals[0] + parts[1]) + (parts[2] + parts[3])
    relative = (fluid - arrived[:, 2, :]) * arrived[:, 3, :]
    pushes[mode] = -arrived[:, 4, :] * relative
    for o in (2, 3, 1):
        push_copy_above(o).start()
    push_copy_twin(0).start()
    lax.fori_loop(MODES // 2, MODES, advect, 0)

    def arrive(o):
        push_copy_above(o).wait_recv()
        push_copy_twin(o).start()

    def place(n, carry):
        j = jnp.where(n < 2, 0, lax.rem(n - 2, 3) + 1)
        o = j + (j // 2) * (5 - 2 * j)
        b = jnp.where((n == 1) | (n > 4), 1, 0)

        @pl.when(n == 2)
        def _():
            arrive(1)
            arrive(3)

        @pl.when(n == 3)
        def _():
            arrive(2)

        @pl.when(b == 1)
        def _():
            push_copy_twin(o).wait_recv()

        m = lax.rem(z - o + 4, 4) * 2 + lax.rem(core + b, 2)
        deposit_arc(m, gathered, onehots, weights, pushes, masses, terms)
        return carry

    lax.fori_loop(0, MODES, place, 0)
    first = jnp.concatenate([terms[a] for a in range(4)], axis=1)
    second = jnp.concatenate([terms[a + 4] for a in range(4)], axis=1)
    hi, lo = split(jnp.concatenate([first + second, first - second], axis=0))
    splits[0] = hi
    splits[1] = lo
    parity = iota((1, 128), 1) % 2 == 0
    top = iota((1, 8, 1), 1) < KL

    def inverse(n, carry):
        line = lax.rem(y + n // 2 + 0, 4)

        @pl.when(line != 3)
        def _():
            ib = lax.rem(x + n, 2) * 4 + line
            block = pl.ds(pl.multiple_of(ib * 128, 128), 128)
            th, tl = table_hi[block, :], table_lo[block, :]
            out = mm_nt(splits[0], th) + mm_nt(splits[1], th) + mm_nt(splits[0], tl)
            chosen = jnp.where(parity, out[: 2 * ROWS], out[2 * ROWS :]).reshape(HB, 2, 8, 128)
            even, odd = chosen[:, 0], chosen[:, 1]
            real = jnp.where(top, even, pltpu.roll(odd, 4, 1))
            imag = jnp.where(top, pltpu.roll(even, 4, 1), odd)
            spectral[rows(ib), :] = real.reshape(ROWS, 128)
            spectral[rows(8 + ib), :] = imag.reshape(ROWS, 128)
            for c in range(2):
                dx = lax.rem(2 * c + ib // 4 - x + 4, 4)
                d = dx * 4 + lax.rem(line - y + 4, 4)

                @pl.when(d > 0)
                def _():
                    back_copy(d).start()

                @pl.when(d == 0)
                def _():
                    own_back.start()

        return carry

    own_back = pltpu.make_async_copy(
        spectral.at[rows(rad)], returned.at[rows(rad)], stores.at[2]
    )
    lax.fori_loop(0, 8, inverse, 0)
    takes = lax.rem(rad, 4) != 3
    for copy in kept:
        copy.wait()
    for d in range(1, RADS):
        particle_copy(d).wait_send()
        field_copy(d).wait_send()
    for d in range(1, MODES):
        gather_copy(d).wait_send()
    for o in range(4):
        twin_part(o).wait_send()
        push_copy_twin(o).wait_send()
        if o:
            reduce_copy(o).wait_send()
            push_copy_above(o).wait_send()
    for d in range(1, RADS):
        @pl.when(lax.rem(rad_peer(d), 4) != 3)
        def _():
            back_copy(d).wait_send()

        @pl.when(takes)
        def _():
            back_copy(d).wait_recv()

    @pl.when(takes)
    def _():
        own_back.wait()


def band_rows():
    off = iota((1, RADII), 1).astype(F32)
    inverse = (RADII * RADII) / (off + 0.5)
    last = off == RADII - 1
    lower = off * inverse
    upper = jnp.where(last, 0.0, (off + 1.0) * inverse)
    centre = -(off + (off + 1.0) * jnp.where(last, 2.0, 1.0)) * inverse
    radius = (off + 0.5) / RADII
    return lower, upper, centre, radius * radius


def solve_body(returned, known, keep, g_ref, nxt_out, forcing_out, rhs, work, nxt, forcing, sems):
    rad = lax.axis_index("rad")
    half = RADII // 2
    lane = lax.rem(rad, 8) * 128 + iota((8, 128), 1)
    m = jnp.where(lane <= HALF, lane, lane - HALF)
    sub = iota((8, 128), 0)
    most = jnp.where(
        sub % KL == 0, keep[0], jnp.where(sub % KL == 1, keep[1], jnp.where(sub % KL == 2, keep[2], keep[3]))
    )
    kept_here = m <= most
    top = sub < KL
    gain = time_step * gamma_rk
    scale = -implicit * RADII * RADII
    slope = jnp.where(top, 1.0, -1.0)
    outer_start = jnp.where(top, 0.0, scale * RADII)
    inner_start = jnp.where(top, scale, scale * (RADII - 1))

    def rows(q):
        return pl.ds(pl.multiple_of(q * 8, 8), 8)

    def weighed(j):
        return (jnp.where(top, 0.5, RADII - 0.5) + slope * j.astype(F32)) * g_ref[j]

    def fold(q, carry):
        sides = []
        for n in (q, half - 1 - q):
            kept = jnp.where(kept_here, returned[rows(n), :], 0.0)
            rhs[rows(n), :] = kept
            sides.append(known[rows(n), :] + gain * kept)
        work[2 * q] = jnp.where(top, sides[0], sides[1]) * weighed(2 * q)
        odd = pltpu.roll(jnp.where(top, sides[1], sides[0]), 4, 0)
        work[2 * q + 1] = odd * weighed(2 * q + 1)
        return carry

    def save(n, k, src, dst):
        return pltpu.make_async_copy(src.at[k], dst.at[k], sems.at[n, k])

    lax.fori_loop(0, half // 2, fold, 0, unroll=8)
    for k in range(KL):
        forcing[k] = jnp.transpose(rhs[pl.ds(k, RADII, stride=KL), :])
        save(0, k, forcing, forcing_out).start()

    def down(j, d):
        d = work[j] - ((outer_start + (scale * slope) * j.astype(F32)) * g_ref[j]) * d
        work[j] = d
        return d

    d = lax.fori_loop(0, half, down, jnp.zeros((8, 128), F32), unroll=16)

    def inner(j):
        return (inner_start + (scale * slope) * j.astype(F32)) * g_ref[j]

    v = inner(jnp.int32(half - 1))
    x = (d - v * pltpu.roll(d, 4, 0)) / (1.0 - v * pltpu.roll(v, 4, 0))
    work[half - 1] = x

    def back(n, x):
        j = half - 2 - n
        x = work[j] - inner(j) * x
        work[j] = x
        return x

    lax.fori_loop(0, half - 1, back, x, unroll=16)

    def unfold(q, carry):
        even = work[2 * q]
        odd = pltpu.roll(work[2 * q + 1], 4, 0)
        rhs[rows(q), :] = jnp.where(top, even, odd)
        rhs[rows(half - 1 - q), :] = jnp.where(top, odd, even)
        return carry

    lax.fori_loop(0, half // 2, unfold, 0, unroll=8)
    for k in range(KL):
        nxt[k] = jnp.transpose(rhs[pl.ds(k, RADII, stride=KL), :])
        save(1, k, nxt, nxt_out).start()
    for k in range(KL):
        save(0, k, forcing, forcing_out).wait()
        save(1, k, nxt, nxt_out).wait()


def vmem_call(body, outs, n_in, scratch, collective=None, smem=(), name=None, space=VMEM,
    out_space=None):
    spec = [
        pl.BlockSpec(memory_space=pltpu.SMEM if n in smem else space) for n in range(n_in)
    ]
    params = dict(vmem_limit_bytes=56 * 1024 * 1024)
    if collective is not None:
        params.update(collective_id=collective, has_side_effects=True)
    return pl.pallas_call(
        body,
        out_shape=[jax.ShapeDtypeStruct(s, F32) for s in outs],
        in_specs=spec,
        out_specs=[pl.BlockSpec(memory_space=out_space or space)] * len(outs),
        scratch_shapes=scratch,
        compiler_params=pltpu.CompilerParams(**params),
        name=name,
    )


DMA = pltpu.SemaphoreType.DMA


def per_device(
    field_coef,
    prior_forcing,
    base_flow,
    keep_modes,
    owner_band,
    cell_index,
    axial_pos,
    particle_vel,
    response_rate,
    particle_mass,
):
    high, low = fourier_half()
    table_hi, table_lo = jnp.asarray(high), jnp.asarray(low)

    def row(x):
        return x.reshape(1, P_DEV)

    all_rows = (RADS * ROWS, 128)
    tiles = (RADII // 2, 8, 128)
    slots = (MODES, RADS, CAP)
    returned, known, g = vmem_call(
        substep_body,
        [all_rows, all_rows, tiles],
        11,
        [
            VMEM(field_coef.shape, F32),
            VMEM(field_coef.shape, F32),
            VMEM(base_flow.shape, F32),
            VMEM((1, P_DEV), jnp.int32),
            VMEM((1, P_DEV), jnp.int32),
            VMEM((1, P_DEV), F32),
            VMEM((1, P_DEV), F32),
            VMEM((1, P_DEV), F32),
            VMEM((1, P_DEV), F32),
            VMEM(table_hi.shape, BF16),
            VMEM(table_hi.shape, BF16),
            VMEM(all_rows, F32),
            VMEM(tiles, F32),
            VMEM(all_rows, F32),
            VMEM(all_rows, F32),
            VMEM((RADS, 8, CAP), F32),
            VMEM((RADS, 8, CAP), F32),
            VMEM((MODES, 2 * RADS, CAP), F32),
            VMEM(tiles, F32),
            VMEM(tiles, F32),
            VMEM((MODES, BAND, ARC), F32),
            VMEM((MODES, 2 * ROWS, 128), F32),
            VMEM((MODES, 2 * ROWS, 128), F32),
            VMEM(all_rows, F32),
            VMEM((MODES, 256, RADS * CAP), BF16),
            VMEM((MODES, RADS, 8, CAP), F32),
            VMEM((2 * ROWS, RADS * CAP), BF16),
            VMEM((2, 4 * ROWS, HALF), BF16),
            VMEM(slots, F32),
            VMEM((4, RADS, CAP), F32),
            VMEM((4, RADS, CAP), F32),
            VMEM((4, RADS, CAP), F32),
            VMEM(slots, F32),
            DMA((11,)), DMA((3,)),
            DMA((RADS,)), DMA((RADS,)), DMA((RADS,)), DMA((RADS,)),
            DMA((MODES,)), DMA((MODES,)),
            DMA((4,)), DMA((4,)), DMA((4,)), DMA((4,)), DMA((4,)), DMA((4,)), DMA((4,)), DMA((4,)),
            DMA((RADS,)), DMA((RADS,)),
        ],
        collective=0,
        name="substep",
        space=pl.ANY,
    )(
        field_coef, prior_forcing, base_flow, row(owner_band), row(cell_index), row(axial_pos),
        row(particle_vel), row(response_rate), row(particle_mass), table_hi, table_lo,
    )
    field_next, forcing = vmem_call(
        solve_body,
        [(KL, 128, RADII), (KL, 128, RADII)],
        4,
        [
            VMEM(all_rows, F32),
            VMEM(tiles, F32),
            VMEM(field_coef.shape, F32),
            VMEM(field_coef.shape, F32),
            DMA((2, KL)),
        ],
        smem=(2,),
        name="solve",
        out_space=pl.ANY,
    )(returned, known, keep_modes, g)
    return (field_next, forcing)


def solution(mesh):
    in_specs = (
        P("mode", "rad", None),
        P("mode", "rad", None),
        P("rad", None),
        P("mode"),
        P(("mode", "rad"), None),
        P(("mode", "rad")),
        P(("mode", "rad")),
        P(("mode", "rad")),
        P(("mode", "rad")),
        P(("mode", "rad")),
    )
    out_specs = (P("mode", "rad", None), P("mode", "rad", None))
    return jax.shard_map(
        per_device, mesh=mesh, in_specs=in_specs, out_specs=out_specs, check_vma=False
    )
```
